128 devices in a mesh: ap: 16 (over z_lo, y, core), sc: 8 (over z_hi, x).
Axes of the slice: x: 4, y: 4, z: 4 (z_hi: 2, z_lo: 2; z = z_hi * 2 + z_lo), core: 2. Of those that a mesh axis runs over, the one named last changes fastest.
Arguments:
- observed_signal: float32 [2, 14, 128, 4, 2048], P(None, None, 'sc', None, 'ap'), may hold values from -6 to 6
- delays: float32 [4, 256, 2048], P(None, 'sc', 'ap'), may hold values from 0 to 64
- sines: float32 [4, 256, 2048], P(None, 'sc', 'ap'), may hold values from -1 to 1
- path_gain_real: float32 [4, 256, 2048], P(None, 'sc', 'ap'), may hold values from -0.078125 to 0.078125
- path_gain_imaginary: float32 [4, 256, 2048], P(None, 'sc', 'ap'), may hold values from -0.078125 to 0.078125
- counts: int32 [256, 2048], P(None, 'ap'), may hold values from 0 to 4
- regularizer: float32 [256], replicated, may hold values from 0.3 to 3
Outputs:
- estimates: float32 [2, 14, 128, 256], P(None, None, 'sc')
The draws below stay inside these ranges and needn't reach their ends.
All inputs are finite; a program needn't handle non-finite values.
Results may differ from the reference program's by a relative error of at most 0.00038.
Values sent between devices are 32-bit elements; how exact they have to be, the bound alone decides.
No kernel may reach another device: no remote copies, remote signals or barrier semaphores. Data moves between devices by JAX's collectives and lax.ppermute only.
A program may use at most 128 MiB of HBM per device.

```python
import math
import jax
import jax.numpy as jnp
from jax import lax

USER_COUNT = 256
ELEMENTS_PER_UNIT = 4
PATH_SLOTS = 4
SAMPLES_PER_TONE = 14
FFT_LEN = 512
RADIO_UNITS = 2048
TONE_TOTAL = 128


def place_ends(array, own_key, smallest, largest):
    longest = array.shape.index(max(array.shape))
    spots = []
    for shift in (0, 1):
        where = [jax.random.randint(jax.random.fold_in(own_key, axis), (), 0, length) for axis, length in enumerate(array.shape)]
        where[longest] = (where[longest] + shift) % array.shape[longest]
        spots.append(tuple(where))
    return array.at[spots[0]].set(smallest).at[spots[1]].set(largest)


def block_levels(key, extent, pieces, low, largest):
    level = 1.0
    for axis_at, parts in pieces:
        draws = jax.random.uniform(jax.random.fold_in(jax.random.fold_in(key, 6), axis_at), (parts,), jnp.float32, low / len(pieces), largest / len(pieces))
        level = level * jnp.repeat(jnp.exp(draws), extent[axis_at] // parts).reshape((-1,) + (1,) * (len(extent) - 1 - axis_at))
    return level


def scatter_about(key, extent, width, bound, cuts=(), held_as=jnp.bfloat16):
    entries = width * jax.random.normal(key, extent, jnp.float32)
    if cuts:
        entries = entries * block_levels(key, extent, cuts, -0.22, 0.18)
    return jnp.clip(entries, -bound, bound).astype(held_as)


def setup_inputs(seed: int = 0) -> dict:
    streams_of = jax.random.split(jax.random.key(seed), 8)
    return {
        "observed_signal": scatter_about(streams_of[0], (2, SAMPLES_PER_TONE, TONE_TOTAL, ELEMENTS_PER_UNIT, RADIO_UNITS), 1.0, 6.0, ((2, 8), (4, 16)), jnp.float32),
        "delays": jnp.clip(64.0 * jax.random.uniform(streams_of[1], (PATH_SLOTS, USER_COUNT, RADIO_UNITS), jnp.float32) ** block_levels(streams_of[1], (PATH_SLOTS, USER_COUNT, RADIO_UNITS), ((1, 8), (2, 16)), -0.2, 0.2), 0.0, 64.0),
        "sines": jnp.clip(jax.random.uniform(streams_of[2], (PATH_SLOTS, USER_COUNT, RADIO_UNITS), jnp.float32, -1.0, 1.0) * block_levels(streams_of[2], (PATH_SLOTS, USER_COUNT, RADIO_UNITS), ((1, 8), (2, 16)), -0.4, 0.0), -1.0, 1.0),
        "path_gain_real": scatter_about(streams_of[3], (PATH_SLOTS, USER_COUNT, RADIO_UNITS), (1.0 / (ELEMENTS_PER_UNIT * RADIO_UNITS * PATH_SLOTS) ** 0.5), 0.078125, ((1, 8), (2, 16)), jnp.float32),
        "path_gain_imaginary": scatter_about(streams_of[4], (PATH_SLOTS, USER_COUNT, RADIO_UNITS), (1.0 / (ELEMENTS_PER_UNIT * RADIO_UNITS * PATH_SLOTS) ** 0.5), 0.078125, ((1, 8), (2, 16)), jnp.float32),
        "counts": place_ends(jax.random.randint(streams_of[5], (USER_COUNT, RADIO_UNITS), 0, PATH_SLOTS + 1), jax.random.fold_in(streams_of[5], 1), 0, PATH_SLOTS).astype(jnp.int32),
        "regularizer": jnp.clip(jnp.exp(jax.random.uniform(streams_of[6], (USER_COUNT,), jnp.float32, math.log(0.3), math.log(3.0))), 0.3, 3.0),
    }


def build_channel(tone_frequency, delays, sines, weight_re, weight_im):
    user_index = delays.shape[1]
    access_stations = delays.shape[2]
    antenna_index = jnp.arange(ELEMENTS_PER_UNIT, dtype=jnp.float32)

    def add_path(path, totals):
        real_sum, imag_sum = totals
        phase_angle = math.pi * antenna_index[None, :, None] * sines[path][:, None, :] - 2.0 * math.pi / FFT_LEN * tone_frequency * delays[path][:, None, :]
        cosine = jnp.cos(phase_angle)
        sine_part = jnp.sin(phase_angle)
        part_re = weight_re[path][:, None, :]
        part_im = weight_im[path][:, None, :]
        return (real_sum + part_re * cosine - part_im * sine_part, imag_sum + part_re * sine_part + part_im * cosine)
    zero_block = jnp.zeros((user_index, ELEMENTS_PER_UNIT, access_stations), jnp.float32)
    real_sum, imag_sum = lax.fori_loop(0, delays.shape[0], add_path, (zero_block, zero_block))
    return (real_sum.reshape(user_index, -1), imag_sum.reshape(user_index, -1))

def solve_one(gram_matrices, filtered_output, regularizer):
    user_index = gram_matrices.shape[1]
    shifted = gram_matrices[0] + jnp.diag(regularizer)
    system = jnp.concatenate([jnp.concatenate([shifted, -gram_matrices[1]], 1), jnp.concatenate([gram_matrices[1], shifted], 1)], 0)
    rhs = jnp.concatenate([filtered_output[0].T, filtered_output[1].T], 0)
    solved = jnp.linalg.solve(system, rhs)
    return jnp.stack([solved[:user_index].T, solved[user_index:].T])

def reference(observed_signal, delays, sines, path_gain_real, path_gain_imaginary, counts, regularizer):
    slots = jnp.arange(PATH_SLOTS, dtype=jnp.int32)[:, None, None]
    alive = (slots < counts[None]).astype(jnp.float32)
    weight_re = path_gain_real * alive
    weight_im = path_gain_imaginary * alive

    def tone_responses(tone_position):
        tone_frequency = tone_position.astype(jnp.float32)
        real_part, imag_part = build_channel(tone_frequency, delays, sines, weight_re, weight_im)
        stacked = jnp.concatenate([real_part, imag_part], 0)
        packed = stacked.astype(jnp.bfloat16)
        blocks = lax.dot_general(packed.astype(jnp.float32), packed.astype(jnp.float32), (((1,), (1,)), ((), ())), preferred_element_type=jnp.float32)
        gram_re = blocks[:USER_COUNT, :USER_COUNT] + blocks[USER_COUNT:, USER_COUNT:]
        gram_im = blocks[:USER_COUNT, USER_COUNT:] - blocks[USER_COUNT:, :USER_COUNT]
        measured_values = observed_signal[:, :, tone_position].reshape(2 * SAMPLES_PER_TONE, -1)
        matched = lax.dot_general(stacked.astype(jnp.float32), measured_values.astype(jnp.float32), (((1,), (1,)), ((), ())), precision=lax.Precision.HIGHEST, preferred_element_type=jnp.float32)
        filt_re = matched[:USER_COUNT, :SAMPLES_PER_TONE] + matched[USER_COUNT:, SAMPLES_PER_TONE:]
        filt_im = matched[:USER_COUNT, SAMPLES_PER_TONE:] - matched[USER_COUNT:, :SAMPLES_PER_TONE]
        filtered_output = jnp.stack([filt_re.T, filt_im.T])
        return solve_one(jnp.stack([gram_re, gram_im]), filtered_output, regularizer)
    merged_estimate = lax.map(tone_responses, jnp.arange(TONE_TOTAL, dtype=jnp.int32))
    return jnp.transpose(merged_estimate, (1, 2, 0, 3))
```

```python
import functools
import math

import jax
import jax.numpy as jnp
import numpy as np
from jax import lax
from jax.experimental import pallas as pl
from jax.experimental.pallas import tpu as pltpu
from jax.sharding import PartitionSpec as P

CORES = 2
OWNERS = 8
Y_CHIPS = 4
Z_CHIPS = 2
X_CHIPS = 4
ANTENNAS = 4
PATHS = 4
FFT_LEN = 512
FIT_POINTS = 4001
ROWS = 16
HALF = 16
SOLVE_STEPS = 60
TOLERANCE = 2e-7


def turn_fit():
    u = 0.25 * np.cos(np.pi * (np.arange(FIT_POINTS) + 0.5) / FIT_POINTS)
    cheb = np.polynomial.chebyshev.Chebyshev
    poly = np.polynomial.Polynomial
    x = u * u
    fits = []
    for values, degree in ((np.sin(2 * np.pi * u) / u, 4), (np.cos(2 * np.pi * u), 5)):
        fits.append([float(c) for c in cheb.fit(x, values, degree, domain=[0, 0.0625]).convert(kind=poly).coef])
    return fits


SIN_FIT, COS_FIT = turn_fit()


def horner(x, coefs):
    total = jnp.full_like(x, coefs[-1])
    for c in coefs[-2::-1]:
        total = total * x + c
    return total


def small_turn(u):
    x = u * u
    return horner(x, COS_FIT), u * horner(x, SIN_FIT)


def doubled(c, s):
    return 1.0 - 2.0 * (s * s), 2.0 * (s * c)


def times(a, b):
    return a[0] * b[0] - a[1] * b[1], a[0] * b[1] + a[1] * b[0]


NT = (((1,), (1,)), ((), ()))


def product(a, b):
    return lax.dot_general(a, b, NT, preferred_element_type=jnp.float32)


def gram_kernel(place_ref, tone_ref, *refs):
    tab_refs, refs = refs[:OWNERS], refs[OWNERS:]
    count_ref, y_kept_ref, y_sent_ref, kept_ref, sent_ref, lead, step_turn, turn, hi, lo, received = refs
    pair = pl.program_id(0)
    users = count_ref.shape[0]
    per_block = tab_refs[0].shape[1]
    blocks = users // ROWS
    width = tab_refs[0].shape[2]
    half = ANTENNAS * width

    @pl.when(pair == 0)
    def _():
        centre = tone_ref[0]
        side = tone_ref[1]

        def prepare(slot, block, carry):
            tab_ref = tab_refs[slot]
            across, along = divmod(slot, X_CHIPS)
            owner = jnp.abs(place_ref[3] - across) * X_CHIPS + (place_ref[4] - along + X_CHIPS) % X_CHIPS
            inside = pl.ds(pl.multiple_of(block * ROWS, ROWS), ROWS)
            here = pl.ds(pl.multiple_of(owner * per_block + block * ROWS, ROWS), ROWS)
            count = count_ref[here, :]
            for p in range(PATHS):
                delay = tab_ref[p, inside, :]
                sine = tab_ref[PATHS + p, inside, :]
                alive = p < count
                re = jnp.where(alive, tab_ref[2 * PATHS + p, inside, :], 0.0)
                im = jnp.where(alive, tab_ref[3 * PATHS + p, inside, :], 0.0)
                half_step = small_turn(delay * (side * (0.5 / FFT_LEN)))
                turn[p, 0, here, :], turn[p, 1, here, :] = half_step
                step_turn[p, 0, here, :], step_turn[p, 1, here, :] = doubled(*half_step)
                turns = delay * centre
                turns = turns - jnp.round(turns)
                c, s = doubled(*small_turn(0.5 * turns))
                z = times((re, im), (c, -s))
                steer = doubled(*small_turn(0.25 * sine))
                for n in range(ANTENNAS):
                    lead[n, p, 0, here, :], lead[n, p, 1, here, :] = z
                    if n + 1 < ANTENNAS:
                        z = times(z, steer)
            return carry

        for slot in range(OWNERS):
            lax.fori_loop(0, per_block // ROWS, functools.partial(prepare, slot), 0)

    def build(block, carry):
        here = pl.ds(pl.multiple_of(block * ROWS, ROWS), ROWS)
        cs = [(turn[p, 0, here, :], turn[p, 1, here, :]) for p in range(PATHS)]
        for p in range(PATHS):
            turn[p, 0, here, :], turn[p, 1, here, :] = times(
                cs[p], (step_turn[p, 0, here, :], step_turn[p, 1, here, :])
            )
        for n in range(ANTENNAS):
            sums = None
            for p in range(PATHS):
                c, s = cs[p]
                re, im = lead[n, p, 0, here, :], lead[n, p, 1, here, :]
                four = (re * c, im * s, im * c, re * s)
                sums = four if sums is None else tuple(a + b for a, b in zip(sums, four))
            a, b, c, d = sums
            for tone, (re, im) in enumerate(((a - b, c + d), (a + b, c - d))):
                for start, value in ((n * width, re), (half + n * width, im)):
                    packed = value.astype(jnp.bfloat16)
                    hi[tone, here, start : start + width] = packed
                    lo[tone, here, start : start + width] = (value - packed.astype(jnp.float32)).astype(jnp.bfloat16)
        return carry

    lax.fori_loop(0, blocks, build, 0)
    for tone, (y_ref, out_ref) in enumerate(((y_sent_ref, sent_ref), (y_kept_ref, kept_ref))):
        y = y_ref[0]
        y_hi = y.astype(jnp.bfloat16)
        y_lo = (y - y_hi.astype(jnp.float32)).astype(jnp.bfloat16)
        received[...] = jnp.concatenate([y_hi, y_lo], 0)
        a = hi[tone]
        re, im = a[:, :half], a[:, half:]
        out_ref[0, :users, :] = product(a, a) + (product(re, im) - product(im, re))
        both = product(received[...], a)
        out_ref[0, users:, :] = both[: 2 * HALF] + both[2 * HALF :] + product(y_hi, lo[tone])


def tone_systems(place, centre, tables, counts, received):
    users, width = counts.shape
    tones = received.shape[0]
    wide = received.shape[2]
    pairs = tones // 2
    f32, bf16 = jnp.float32, jnp.bfloat16
    block = (1, users + 2 * HALF, users)

    def distance(j, place):
        along = (j % Y_CHIPS - place[2] + Y_CHIPS) % Y_CHIPS
        return (jnp.abs(j // Y_CHIPS - place[1]) * Y_CHIPS + along, 0, 0)

    grid_spec = pltpu.PrefetchScalarGridSpec(
        num_scalar_prefetch=1,
        grid=(pairs,),
        in_specs=[
            pl.BlockSpec(memory_space=pltpu.SMEM),
            *[pl.BlockSpec(t.shape, lambda j, place: (0, 0, 0), pipeline_mode=pl.Buffered(1)) for t in tables],
            pl.BlockSpec(counts.shape, lambda j, place: (0, 0), pipeline_mode=pl.Buffered(1)),
            pl.BlockSpec((1, 2 * HALF, wide), lambda j, place: (pairs - 1 - j + place[0] * (2 * j + 1), 0, 0)),
            pl.BlockSpec((1, 2 * HALF, wide), lambda j, place: (pairs + j - place[0] * (2 * j + 1), 0, 0)),
        ],
        out_specs=[pl.BlockSpec(block, distance)] * 2,
        scratch_shapes=[
            pltpu.VMEM((ANTENNAS, PATHS, 2, users, width), f32),
            pltpu.VMEM((PATHS, 2, users, width), f32),
            pltpu.VMEM((PATHS, 2, users, width), f32),
            pltpu.VMEM((2, users, wide), bf16),
            pltpu.VMEM((2, users, wide), bf16),
            pltpu.VMEM((4 * HALF, wide), bf16),
        ],
    )
    half = jax.ShapeDtypeStruct((pairs, users + 2 * HALF, users), f32)
    return pl.pallas_call(gram_kernel, grid_spec=grid_spec, out_shape=[half, half], name="tone_systems")(
        place, centre, *tables, counts, received, received
    )


def three_parts(x):
    hi = x.astype(jnp.bfloat16)
    rest = x - hi.astype(jnp.float32)
    mid = rest.astype(jnp.bfloat16)
    return hi, mid, (rest - mid.astype(jnp.float32)).astype(jnp.bfloat16)


def solve_kernel(*refs):
    *part_refs, regularizer_ref, out_ref, system_ref, parts, x_ref, r_ref, p_ref, work = refs
    system_ref[...] = sum(ref[0] for ref in part_refs)
    users = regularizer_ref.shape[1]
    f32 = jnp.float32
    g = system_ref[:users, :]
    flipped = g.T
    row = lax.broadcasted_iota(jnp.int32, (users, users), 0)
    column = lax.broadcasted_iota(jnp.int32, (users, users), 1)
    eye = row == column
    re = 0.5 * (g + flipped)
    im = 0.5 * (g - flipped)
    re = jnp.where(eye, re + regularizer_ref[...], re)
    diagonal = jnp.where(eye, re, 0.0)
    across = lax.rsqrt(jnp.sum(diagonal, 0, keepdims=True))
    down = lax.rsqrt(jnp.sum(diagonal, 1, keepdims=True))
    for k, matrix in enumerate((re, im)):
        for at, part in enumerate(three_parts(matrix * across * down)):
            parts[k, at] = part
    right = system_ref[users:, :] * across

    def together(v):
        total = jnp.sum(v[:HALF] + v[HALF:], 1, keepdims=True)
        return jnp.concatenate([total, total], 0)

    def dot(a, b):
        return jnp.dot(a, b, preferred_element_type=f32)

    rows = 2 * HALF

    def applied(p):
        hi, mid, low = three_parts(p)
        left3 = jnp.concatenate([hi, mid, low], 0)
        left2 = jnp.concatenate([hi, mid], 0)
        result = []
        for k in range(2):
            a = dot(left3, parts[k, 0])
            b = dot(left2, parts[k, 1])
            c = dot(hi, parts[k, 2])
            small = a[2 * rows :] + b[rows:] + c
            result.append(a[:rows] + ((a[rows : 2 * rows] + b[:rows]) + small))
        s, i = result
        return jnp.concatenate([s[:HALF] + i[HALF:], s[HALF:] - i[:HALF]], 0)

    norm = together(right * right)
    goal = norm * (TOLERANCE * TOLERANCE)
    x_ref[...] = jnp.zeros_like(right)
    r_ref[...] = right
    p_ref[...] = right

    def advance(state):
        done, _, rr = state
        for _ in range(2):
            p = p_ref[...]
            q = applied(p)
            pq = together(p * q)
            alpha = jnp.where(pq > 0.0, rr / pq, 0.0)
            x_ref[...] += alpha * p
            r = r_ref[...] - alpha * q
            r_ref[...] = r
            latest = together(r * r)
            p_ref[...] = r + jnp.where(rr > 0.0, latest / rr, 0.0) * p
            rr = latest
        return done + 2, jnp.max(jnp.where(rr <= goal, 0, 1)), rr

    def unfinished(state):
        done, left, _ = state
        return (left > 0) & (done < SOLVE_STEPS)

    _, left, _ = lax.while_loop(unfinished, advance, (0, jnp.max(jnp.where(norm <= goal, 0, 1)), norm))
    out_ref[...] = x_ref[...] * across

    @pl.when(left > 0)
    def _():
        work[0, :users, :] = re
        work[1, :users, :] = -im
        work[0, users:, :] = system_ref[users : users + HALF, :]
        work[1, users:, :] = system_ref[users + HALF :, :]
        lane = lax.broadcasted_iota(jnp.int32, (1, users), 1)

        def eliminate(j, carry):
            a, b = work[0], work[1]
            here = lane == j
            row_re = work[0, pl.ds(j, 1), :]
            row_im = work[1, pl.ds(j, 1), :]
            pivot = 1.0 / jnp.sum(jnp.where(here, row_re, 0.0), 1, keepdims=True)
            col_re = jnp.sum(jnp.where(here, a, 0.0), 1, keepdims=True) * pivot
            col_im = jnp.sum(jnp.where(here, b, 0.0), 1, keepdims=True) * pivot
            work[0] = jnp.where(here, col_re, a - (col_re * row_re - col_im * row_im))
            work[1] = jnp.where(here, col_im, b - (col_re * row_im + col_im * row_re))
            return carry

        lax.fori_loop(0, users, eliminate, 0)
        out_ref[:HALF, :] = work[0, users:, :]
        out_ref[HALF:, :] = work[1, users:, :]


def solved(systems, regularizer):
    _, rows, users = systems[0].shape
    f32 = jnp.float32
    vmem = pl.BlockSpec(memory_space=pltpu.VMEM)
    pair = pltpu.VMEM((2 * HALF, users), f32)
    return pl.pallas_call(
        solve_kernel,
        in_specs=[vmem] * (len(systems) + 1),
        out_specs=vmem,
        out_shape=jax.ShapeDtypeStruct((2 * HALF, users), f32),
        scratch_shapes=[
            pltpu.VMEM((rows, users), f32),
            pltpu.VMEM((2, 3, users, users), jnp.bfloat16),
            pair,
            pair,
            pair,
            pltpu.VMEM((2, users + HALF, users), f32),
        ],
        name="solved",
    )(*systems, regularizer.reshape(1, users))


def received_rows(observed_signal):
    _, samples, tones, antennas, width = observed_signal.shape
    y = jnp.moveaxis(observed_signal, 2, 0).reshape(tones, 2, samples, antennas * width)
    re, im = y[:, 0], y[:, 1]
    gap = ((0, 0), (0, HALF - samples), (0, 0))
    top = jnp.pad(jnp.concatenate([re, im], 2), gap)
    bottom = jnp.pad(jnp.concatenate([im, -re], 2), gap)
    return jnp.concatenate([top, bottom], 1)


def ap_at(z, y, core):
    return (z * Y_CHIPS + y % Y_CHIPS) * CORES + core


def over_ap(value, dz, dy, dcore):
    spots = [(z, y, c) for z in range(Z_CHIPS) for y in range(Y_CHIPS) for c in range(CORES)]
    pairs = [(ap_at(z, y, c), ap_at(z ^ dz, y + dy, c ^ dcore)) for z, y, c in spots]
    return lax.ppermute(value, "ap", pairs)


def over_sc(value, dz, dx):
    spots = [(z, x) for z in range(2) for x in range(X_CHIPS)]
    pairs = [(z * X_CHIPS + x, (z ^ dz) * X_CHIPS + (x + dx) % X_CHIPS) for z, x in spots]
    return lax.ppermute(value, "sc", pairs)


def gathered_tables(own):
    across = over_sc(own, 1, 0)
    near = [over_sc(own, 0, dx) for dx in (1, 2, 3)]
    far = [over_sc(across, 0, dx) for dx in (1, 2, 3)]
    return [own, *near, across, *far]


def on_device(observed_signal, delays, sines, path_gain_real, path_gain_imaginary, counts, regularizer):
    tones = observed_signal.shape[2]
    samples = observed_signal.shape[1]
    users = counts.shape[0]
    sc = lax.axis_index("sc")
    ap = lax.axis_index("ap")
    core = ap % CORES
    chip = ap // CORES
    place = jnp.stack([core, chip // Y_CHIPS, chip % Y_CHIPS, sc // X_CHIPS, sc % X_CHIPS]).astype(jnp.int32)
    first = (sc * tones).astype(jnp.float32)
    side = jnp.where(core == 0, -1.0, 1.0)
    centre = jnp.stack([(first + 0.5 * (tones - 1)) * (1.0 / FFT_LEN), side])
    own = jnp.concatenate([delays, sines, path_gain_real, path_gain_imaginary], 0)
    tables = gathered_tables(own)
    kept, sent = tone_systems(place, centre, tables, counts, received_rows(observed_signal))
    mine = kept + over_ap(sent, 0, 0, 1)
    steps = [(dz, dy) for dz in (1, 0) for dy in (2, 1, 3, 0) if dz or dy]
    parts = [over_ap(mine[dz * Y_CHIPS + dy][None], dz, dy, 0) for dz, dy in steps]
    own_tone = solved([mine[:1], *parts], regularizer)
    length = lax.axis_size("ap")
    every = lax.all_to_all(jnp.broadcast_to(own_tone[None], (length, *own_tone.shape)), "ap", 0, 0, tiled=True)
    every = every.reshape(length // CORES, CORES, 2, HALF, users)[:, :, :, :samples]
    every = jnp.concatenate([every[::-1, 0], every[:, 1]], 0)
    return jnp.transpose(every, (1, 2, 0, 3))


def solution(mesh):
    placed = (
        P(None, None, "sc", None, "ap"),
        P(None, "sc", "ap"),
        P(None, "sc", "ap"),
        P(None, "sc", "ap"),
        P(None, "sc", "ap"),
        P(None, "ap"),
        P(),
    )
    return jax.shard_map(
        on_device, mesh=mesh, in_specs=placed, out_specs=P(None, None, "sc", None), check_vma=False
    )
```

```python
import functools
import math

import jax
import jax.numpy as jnp
import numpy as np
from jax import lax
from jax.experimental import pallas as pl
from jax.experimental.pallas import tpu as pltpu
from jax.sharding import PartitionSpec as P

CORES = 2
OWNERS = 8
SLOTS = [(0, 0, 0, 8), (2, 0, 2, 8), (4, 0, 5, 0), (3, 0, 3, 8), (1, 0, 1, 8), (6, 0, 6, 8), (8, 0, 9, 0), (7, 0, 7, 8)]
PIECES = 10
Y_CHIPS = 4
Z_CHIPS = 2
X_CHIPS = 4
ANTENNAS = 4
PATHS = 4
FFT_LEN = 512
FIT_POINTS = 4001
ROWS = 16
HALF = 16
SOLVE_STEPS = 60
TOLERANCE = 2e-7


def turn_fit():
    u = 0.25 * np.cos(np.pi * (np.arange(FIT_POINTS) + 0.5) / FIT_POINTS)
    cheb = np.polynomial.chebyshev.Chebyshev
    poly = np.polynomial.Polynomial
    x = u * u
    fits = []
    for values, degree in ((np.sin(2 * np.pi * u) / u, 4), (np.cos(2 * np.pi * u), 5)):
        fits.append([float(c) for c in cheb.fit(x, values, degree, domain=[0, 0.0625]).convert(kind=poly).coef])
    return fits


SIN_FIT, COS_FIT = turn_fit()


def horner(x, coefs):
    total = jnp.full_like(x, coefs[-1])
    for c in coefs[-2::-1]:
        total = total * x + c
    return total


def small_turn(u):
    x = u * u
    return horner(x, COS_FIT), u * horner(x, SIN_FIT)


def doubled(c, s):
    return 1.0 - 2.0 * (s * s), 2.0 * (s * c)


def times(a, b):
    return a[0] * b[0] - a[1] * b[1], a[0] * b[1] + a[1] * b[0]


NT = (((1,), (1,)), ((), ()))


def product(a, b):
    return lax.dot_general(a, b, NT, preferred_element_type=jnp.float32)


def gram_kernel(place_ref, tone_ref, *refs):
    tab_refs, refs = refs[:PIECES], refs[PIECES:]
    count_ref, y_ref, kept_ref, sent_ref, lead, step_turn, turn, hi_a, lo_a, hi_b, lo_b, rec_a, rec_b = refs
    users = count_ref.shape[0]
    per_block = users // OWNERS
    blocks = users // ROWS
    width = count_ref.shape[1]
    half = ANTENNAS * width
    pairs = kept_ref.shape[0]
    core, chip_z, chip_y, sc_z, sc_x = [place_ref[k] for k in range(5)]
    centre = tone_ref[0]
    side = tone_ref[1]

    def prepare(slot, block, carry):
        angles, a_at, gains, g_at = SLOTS[slot]
        angles, gains = tab_refs[angles], tab_refs[gains]
        across, along = divmod(slot, X_CHIPS)
        owner = jnp.abs(sc_z - across) * X_CHIPS + (sc_x - along + X_CHIPS) % X_CHIPS
        inside = pl.ds(pl.multiple_of(block * ROWS, ROWS), ROWS)
        here = pl.ds(pl.multiple_of(owner * per_block + block * ROWS, ROWS), ROWS)
        count = count_ref[here, :]
        for p in range(PATHS):
            delay = angles[a_at + p, inside, :]
            sine = angles[a_at + PATHS + p, inside, :]
            alive = p < count
            re = jnp.where(alive, gains[g_at + p, inside, :], 0.0)
            im = jnp.where(alive, gains[g_at + PATHS + p, inside, :], 0.0)
            half_step = small_turn(delay * (side * (0.5 / FFT_LEN)))
            turn[p, 0, here, :], turn[p, 1, here, :] = half_step
            step_turn[p, 0, here, :], step_turn[p, 1, here, :] = doubled(*half_step)
            turns = delay * centre
            turns = turns - jnp.round(turns)
            c, s = doubled(*small_turn(0.5 * turns))
            z = times((re, im), (c, -s))
            steer = doubled(*small_turn(0.25 * sine))
            for n in range(ANTENNAS):
                lead[n, p, 0, here, :], lead[n, p, 1, here, :] = z
                if n + 1 < ANTENNAS:
                    z = times(z, steer)
        return carry

    for slot in range(OWNERS):
        lax.fori_loop(0, per_block // ROWS, functools.partial(prepare, slot), 0)

    def build(hi, lo, block):
        here = pl.ds(block * ROWS, ROWS)
        cs = [(turn[p, 0, here, :], turn[p, 1, here, :]) for p in range(PATHS)]
        for p in range(PATHS):
            turn[p, 0, here, :], turn[p, 1, here, :] = times(
                cs[p], (step_turn[p, 0, here, :], step_turn[p, 1, here, :])
            )
        for n in range(ANTENNAS):
            sums = None
            for p in range(PATHS):
                c, s = cs[p]
                re, im = lead[n, p, 0, here, :], lead[n, p, 1, here, :]
                four = (re * c, im * s, im * c, re * s)
                sums = four if sums is None else tuple(a + b for a, b in zip(sums, four))
            a, b, c, d = sums
            for tone, (re, im) in enumerate(((a - b, c + d), (a + b, c - d))):
                for start, value in ((n * width, re), (half + n * width, im)):
                    packed = value.astype(jnp.bfloat16)
                    hi[tone, here, start : start + width] = packed
                    lo[tone, here, start : start + width] = (value - packed.astype(jnp.float32)).astype(jnp.bfloat16)

    def multiply(hi, lo, received, pair):
        along = (pair % Y_CHIPS - chip_y + Y_CHIPS) % Y_CHIPS
        slot = jnp.abs(pair // Y_CHIPS - chip_z) * Y_CHIPS + along
        plus, minus = pairs + pair, pairs - 1 - pair
        first = jnp.where(core == 0, plus, minus)
        for tone, (at, out_ref) in enumerate(((first, sent_ref), (plus + minus - first, kept_ref))):
            y = y_ref[at]
            y_hi = y.astype(jnp.bfloat16)
            y_lo = (y - y_hi.astype(jnp.float32)).astype(jnp.bfloat16)
            received[tone, : 2 * HALF] = y_hi
            received[tone, 2 * HALF :] = y_lo
            a = hi[tone]
            re, im = a[:, :half], a[:, half:]
            out_ref[slot, :users, :] = product(a, a) + (product(re, im) - product(im, re))
            both = product(received[tone], a)
            out_ref[slot, users:, :] = both[: 2 * HALF] + both[2 * HALF :] + product(y_hi, lo[tone])

    even, odd = (hi_a, lo_a), (hi_b, lo_b)

    def step(now, received, later, pair):
        multiply(*now, received, pair)
        for block in range(blocks):
            build(*later, block)

    for block in range(blocks):
        build(*even, block)

    def two(i, carry):
        step(even, rec_a, odd, 2 * i)
        step(odd, rec_b, even, 2 * i + 1)
        return carry

    lax.fori_loop(0, pairs // 2 - 1, two, 0)
    step(even, rec_a, odd, pairs - 2)
    multiply(*odd, rec_b, pairs - 1)


def in_vmem(x):
    return pltpu.with_memory_space_constraint(x, pltpu.VMEM)


def tone_systems(place, centre, tables, counts, received):
    users, width = counts.shape
    tones = received.shape[0]
    wide = received.shape[2]
    pairs = tones // 2
    f32, bf16 = jnp.float32, jnp.bfloat16
    vmem = pl.BlockSpec(memory_space=pltpu.VMEM)
    smem = pl.BlockSpec(memory_space=pltpu.SMEM)
    channel = pltpu.VMEM((2, users, wide), bf16)
    rows = pltpu.VMEM((2, 4 * HALF, wide), bf16)
    return pl.pallas_call(
        gram_kernel,
        in_specs=[smem, smem] + [vmem] * (len(tables) + 2),
        out_specs=[vmem, vmem],
        out_shape=[pltpu.VMEM((pairs, users + 2 * HALF, users), f32)] * 2,
        scratch_shapes=[
            pltpu.VMEM((ANTENNAS, PATHS, 2, users, width), f32),
            pltpu.VMEM((PATHS, 2, users, width), f32),
            pltpu.VMEM((PATHS, 2, users, width), f32),
            channel,
            channel,
            channel,
            channel,
            rows,
            rows,
        ],
        compiler_params=pltpu.CompilerParams(vmem_limit_bytes=20 << 20),
        name="tone_systems",
    )(place, centre, *[in_vmem(t) for t in tables], in_vmem(counts), in_vmem(received))


def three_parts(x):
    hi = x.astype(jnp.bfloat16)
    rest = x - hi.astype(jnp.float32)
    mid = rest.astype(jnp.bfloat16)
    return hi, mid, (rest - mid.astype(jnp.float32)).astype(jnp.bfloat16)


def solve_kernel(*refs):
    *part_refs, regularizer_ref, out_ref, system_ref, parts, x_ref, r_ref, p_ref, work = refs
    system_ref[...] = sum(ref[0] for ref in part_refs)
    users = regularizer_ref.shape[1]
    f32 = jnp.float32
    g = system_ref[:users, :]
    flipped = g.T
    row = lax.broadcasted_iota(jnp.int32, (users, users), 0)
    column = lax.broadcasted_iota(jnp.int32, (users, users), 1)
    eye = row == column
    re = 0.5 * (g + flipped)
    im = 0.5 * (g - flipped)
    re = jnp.where(eye, re + regularizer_ref[...], re)
    diagonal = jnp.where(eye, re, 0.0)
    across = lax.rsqrt(jnp.sum(diagonal, 0, keepdims=True))
    down = lax.rsqrt(jnp.sum(diagonal, 1, keepdims=True))
    for k, matrix in enumerate((re, im)):
        for at, part in enumerate(three_parts(matrix * across * down)):
            parts[k, at] = part
    right = system_ref[users:, :] * across

    def together(v):
        total = jnp.sum(v[:HALF] + v[HALF:], 1, keepdims=True)
        return jnp.concatenate([total, total], 0)

    def dot(a, b):
        return jnp.dot(a, b, preferred_element_type=f32)

    rows = 2 * HALF

    def applied(p):
        hi, mid, low = three_parts(p)
        left3 = jnp.concatenate([hi, mid, low], 0)
        left2 = jnp.concatenate([hi, mid], 0)
        result = []
        for k in range(2):
            a = dot(left3, parts[k, 0])
            b = dot(left2, parts[k, 1])
            c = dot(hi, parts[k, 2])
            small = a[2 * rows :] + b[rows:] + c
            result.append(a[:rows] + ((a[rows : 2 * rows] + b[:rows]) + small))
        s, i = result
        return jnp.concatenate([s[:HALF] + i[HALF:], s[HALF:] - i[:HALF]], 0)

    norm = together(right * right)
    goal = norm * (TOLERANCE * TOLERANCE)
    x_ref[...] = jnp.zeros_like(right)
    r_ref[...] = right
    p_ref[...] = right

    def advance(state):
        done, _, rr = state
        for _ in range(2):
            p = p_ref[...]
            q = applied(p)
            pq = together(p * q)
            alpha = jnp.where(pq > 0.0, rr / pq, 0.0)
            x_ref[...] += alpha * p
            r = r_ref[...] - alpha * q
            r_ref[...] = r
            latest = together(r * r)
            p_ref[...] = r + jnp.where(rr > 0.0, latest / rr, 0.0) * p
            rr = latest
        return done + 2, jnp.max(jnp.where(rr <= goal, 0, 1)), rr

    def unfinished(state):
        done, left, _ = state
        return (left > 0) & (done < SOLVE_STEPS)

    _, left, _ = lax.while_loop(unfinished, advance, (0, jnp.max(jnp.where(norm <= goal, 0, 1)), norm))
    out_ref[...] = x_ref[...] * across

    @pl.when(left > 0)
    def _():
        work[0, :users, :] = re
        work[1, :users, :] = -im
        work[0, users:, :] = system_ref[users : users + HALF, :]
        work[1, users:, :] = system_ref[users + HALF :, :]
        lane = lax.broadcasted_iota(jnp.int32, (1, users), 1)

        def eliminate(j, carry):
            a, b = work[0], work[1]
            here = lane == j
            row_re = work[0, pl.ds(j, 1), :]
            row_im = work[1, pl.ds(j, 1), :]
            pivot = 1.0 / jnp.sum(jnp.where(here, row_re, 0.0), 1, keepdims=True)
            col_re = jnp.sum(jnp.where(here, a, 0.0), 1, keepdims=True) * pivot
            col_im = jnp.sum(jnp.where(here, b, 0.0), 1, keepdims=True) * pivot
            work[0] = jnp.where(here, col_re, a - (col_re * row_re - col_im * row_im))
            work[1] = jnp.where(here, col_im, b - (col_re * row_im + col_im * row_re))
            return carry

        lax.fori_loop(0, users, eliminate, 0)
        out_ref[:HALF, :] = work[0, users:, :]
        out_ref[HALF:, :] = work[1, users:, :]


def solved(systems, regularizer):
    _, rows, users = systems[0].shape
    f32 = jnp.float32
    vmem = pl.BlockSpec(memory_space=pltpu.VMEM)
    pair = pltpu.VMEM((2 * HALF, users), f32)
    return pl.pallas_call(
        solve_kernel,
        in_specs=[vmem] * (len(systems) + 1),
        out_specs=vmem,
        out_shape=jax.ShapeDtypeStruct((2 * HALF, users), f32),
        scratch_shapes=[
            pltpu.VMEM((rows, users), f32),
            pltpu.VMEM((2, 3, users, users), jnp.bfloat16),
            pair,
            pair,
            pair,
            pltpu.VMEM((2, users + HALF, users), f32),
        ],
        compiler_params=pltpu.CompilerParams(vmem_limit_bytes=12 << 20),
        name="solved",
    )(*[in_vmem(s) for s in systems], regularizer.reshape(1, users))


def received_rows(observed_signal):
    _, samples, tones, antennas, width = observed_signal.shape
    y = jnp.moveaxis(observed_signal, 2, 0).reshape(tones, 2, samples, antennas * width)
    re, im = y[:, 0], y[:, 1]
    gap = ((0, 0), (0, HALF - samples), (0, 0))
    top = jnp.pad(jnp.concatenate([re, im], 2), gap)
    bottom = jnp.pad(jnp.concatenate([im, -re], 2), gap)
    return jnp.concatenate([top, bottom], 1)


def ap_at(z, y, core):
    return (z * Y_CHIPS + y % Y_CHIPS) * CORES + core


def over_ap(value, dz, dy, dcore):
    spots = [(z, y, c) for z in range(Z_CHIPS) for y in range(Y_CHIPS) for c in range(CORES)]
    pairs = [(ap_at(z, y, c), ap_at(z ^ dz, y + dy, c ^ dcore)) for z, y, c in spots]
    return lax.ppermute(value, "ap", pairs)


def over_sc(value, dz, dx):
    spots = [(z, x) for z in range(2) for x in range(X_CHIPS)]
    pairs = [(z * X_CHIPS + x, (z ^ dz) * X_CHIPS + (x + dx) % X_CHIPS) for z, x in spots]
    return lax.ppermute(value, "sc", pairs)


def gathered_tables(own):
    half = own.shape[0] // 2
    across = over_sc(own, 1, 0)
    up, down = over_sc(own, 0, 1), over_sc(own, 0, -1)
    up_twice, down_twice = over_sc(up[:half], 0, 1), over_sc(down[half:], 0, -1)
    across_up, across_down = over_sc(across, 0, 1), over_sc(across, 0, -1)
    far = over_sc(up_twice, 1, 0), over_sc(down_twice, 1, 0)
    return [own, across, up, down, up_twice, down_twice, across_up, across_down, *far]


def pack_kernel(*refs):
    *parts, out = refs
    at = 0
    for part in parts:
        out[at : at + part.shape[0]] = part[...]
        at += part.shape[0]


def packed_tables(parts):
    rows = sum(part.shape[0] for part in parts)
    vmem = pl.BlockSpec(memory_space=pltpu.VMEM)
    return pl.pallas_call(
        pack_kernel,
        in_specs=[vmem] * len(parts),
        out_specs=vmem,
        out_shape=pltpu.VMEM((rows, *parts[0].shape[1:]), jnp.float32),
        compiler_params=pltpu.CompilerParams(vmem_limit_bytes=4 << 20),
        name="packed_tables",
    )(*parts)


def on_device(observed_signal, delays, sines, path_gain_real, path_gain_imaginary, counts, regularizer):
    tones = observed_signal.shape[2]
    samples = observed_signal.shape[1]
    users = counts.shape[0]
    sc = lax.axis_index("sc")
    ap = lax.axis_index("ap")
    core = ap % CORES
    chip = ap // CORES
    place = jnp.stack([core, chip // Y_CHIPS, chip % Y_CHIPS, sc // X_CHIPS, sc % X_CHIPS]).astype(jnp.int32)
    first = (sc * tones).astype(jnp.float32)
    side = jnp.where(core == 0, -1.0, 1.0)
    centre = jnp.stack([(first + 0.5 * (tones - 1)) * (1.0 / FFT_LEN), side])
    own = packed_tables([delays, sines, path_gain_real, path_gain_imaginary])
    tables = gathered_tables(own)
    kept, sent = tone_systems(place, centre, tables, counts, received_rows(observed_signal))
    mine = kept + over_ap(sent, 0, 0, 1)
    steps = [(dz, dy) for dz in (1, 0) for dy in (2, 1, 3, 0) if dz or dy]
    parts = [over_ap(mine[dz * Y_CHIPS + dy][None], dz, dy, 0) for dz, dy in steps]
    own_tone = solved([mine[:1], *parts], regularizer)
    length = lax.axis_size("ap")
    every = lax.all_to_all(jnp.broadcast_to(own_tone[None], (length, *own_tone.shape)), "ap", 0, 0, tiled=True)
    every = every.reshape(length // CORES, CORES, 2, HALF, users)[:, :, :, :samples]
    every = jnp.concatenate([every[::-1, 0], every[:, 1]], 0)
    return jnp.transpose(every, (1, 2, 0, 3))


def solution(mesh):
    placed = (
        P(None, None, "sc", None, "ap"),
        P(None, "sc", "ap"),
        P(None, "sc", "ap"),
        P(None, "sc", "ap"),
        P(None, "sc", "ap"),
        P(None, "ap"),
        P(),
    )
    return jax.shard_map(
        on_device, mesh=mesh, in_specs=placed, out_specs=P(None, None, "sc", None), check_vma=False
    )
```

```python
import functools
import math

import jax
import jax.numpy as jnp
import numpy as np
from jax import lax
from jax.experimental import pallas as pl
from jax.experimental.pallas import tpu as pltpu
from jax.sharding import PartitionSpec as P

CORES = 2
OWNERS = 8
NEAR_SLOTS = [((0, 0), 0, 0, 0, 8), ((1, 0), 1, 0, 1, 8), ((0, 1), 2, 0, 2, 8), ((0, 3), 3, 0, 3, 8)]
FAR_SLOTS = [((0, 2), 0, 0, 1, 0), ((1, 1), 2, 0, 2, 8), ((1, 3), 3, 0, 3, 8), ((1, 2), 4, 0, 5, 0)]
Y_CHIPS = 4
Z_CHIPS = 2
X_CHIPS = 4
ANTENNAS = 4
PATHS = 4
FFT_LEN = 512
FIT_POINTS = 4001
ROWS = 16
HALF = 16
SOLVE_STEPS = 60
TOLERANCE = 2e-7


def turn_fit():
    u = 0.25 * np.cos(np.pi * (np.arange(FIT_POINTS) + 0.5) / FIT_POINTS)
    cheb = np.polynomial.chebyshev.Chebyshev
    poly = np.polynomial.Polynomial
    x = u * u
    fits = []
    for values, degree in ((np.sin(2 * np.pi * u) / u, 4), (np.cos(2 * np.pi * u), 5)):
        fits.append([float(c) for c in cheb.fit(x, values, degree, domain=[0, 0.0625]).convert(kind=poly).coef])
    return fits


SIN_FIT, COS_FIT = turn_fit()


def horner(x, coefs):
    total = jnp.full_like(x, coefs[-1])
    for c in coefs[-2::-1]:
        total = total * x + c
    return total


def small_turn(u):
    x = u * u
    return horner(x, COS_FIT), u * horner(x, SIN_FIT)


def doubled(c, s):
    return 1.0 - 2.0 * (s * s), 2.0 * (s * c)


def times(a, b):
    return a[0] * b[0] - a[1] * b[1], a[0] * b[1] + a[1] * b[0]


NT = (((1,), (1,)), ((), ()))


def product(a, b):
    return lax.dot_general(a, b, NT, preferred_element_type=jnp.float32)


def prepare_kernel(slots, pieces, place_ref, tone_ref, *refs):
    tab_refs, count_ref = refs[:pieces], refs[pieces]
    lead, turn, four = refs[-3:]
    per_block = count_ref.shape[0] // OWNERS
    sc_z, sc_x = place_ref[3], place_ref[4]
    centre = tone_ref[0]
    side = tone_ref[1]

    def prepare(slot, block, carry):
        (across, along), angles, a_at, gains, g_at = slot
        angles, gains = tab_refs[angles], tab_refs[gains]
        owner = jnp.abs(sc_z - across) * X_CHIPS + (sc_x - along + X_CHIPS) % X_CHIPS
        inside = pl.ds(pl.multiple_of(block * ROWS, ROWS), ROWS)
        here = pl.ds(pl.multiple_of(owner * per_block + block * ROWS, ROWS), ROWS)
        count = count_ref[here, :]
        for p in range(PATHS):
            delay = angles[a_at + p, inside, :]
            sine = angles[a_at + PATHS + p, inside, :]
            alive = p < count
            re = jnp.where(alive, gains[g_at + p, inside, :], 0.0)
            im = jnp.where(alive, gains[g_at + PATHS + p, inside, :], 0.0)
            tones = small_turn(delay * (side * (0.5 / FFT_LEN)))
            one = doubled(*tones)
            for y in range(Y_CHIPS):
                turn[y, p, 0, here, :], turn[y, p, 1, here, :] = tones
                if y + 1 < Y_CHIPS:
                    tones = times(tones, one)
            four[p, 0, here, :], four[p, 1, here, :] = doubled(*doubled(*one))
            turns = delay * centre
            turns = turns - jnp.round(turns)
            c, s = doubled(*small_turn(0.5 * turns))
            z = times((re, im), (c, -s))
            steer = doubled(*small_turn(0.25 * sine))
            for n in range(ANTENNAS):
                lead[n, p, 0, here, :], lead[n, p, 1, here, :] = z
                if n + 1 < ANTENNAS:
                    z = times(z, steer)
        return carry

    for slot in slots:
        lax.fori_loop(0, per_block // ROWS, functools.partial(prepare, slot), 0)


def in_vmem(x):
    return pltpu.with_memory_space_constraint(x, pltpu.VMEM)


def prepared(place, centre, slots, tables, counts, state=None):
    users, width = counts.shape
    f32 = jnp.float32
    vmem = pl.BlockSpec(memory_space=pltpu.VMEM)
    smem = pl.BlockSpec(memory_space=pltpu.SMEM)
    state = () if state is None else state
    first = 3 + len(tables)
    return pl.pallas_call(
        functools.partial(prepare_kernel, slots, len(tables)),
        in_specs=[smem, smem] + [vmem] * (len(tables) + 1 + len(state)),
        out_specs=[vmem] * 3,
        out_shape=[
            pltpu.VMEM((ANTENNAS, PATHS, 2, users, width), f32),
            pltpu.VMEM((Y_CHIPS, PATHS, 2, users, width), f32),
            pltpu.VMEM((PATHS, 2, users, width), f32),
        ],
        input_output_aliases={first + k: k for k in range(len(state))},
        compiler_params=pltpu.CompilerParams(vmem_limit_bytes=4 << 20),
        name="prepared",
    )(place, centre, *[in_vmem(t) for t in tables], in_vmem(counts), *state)


def tone_kernel(place_ref, y_ref, lead, turn, four, kept_ref, sent_ref, re_a, im_a, lo_a, re_b, im_b, lo_b):
    users, width = four.shape[2:]
    blocks = users // ROWS
    half = ANTENNAS * width
    pairs = Y_CHIPS * Z_CHIPS
    core, chip_z, target_y = place_ref[0], place_ref[1], place_ref[2]

    def build(buffers, block, second):
        with_re, with_im, lo = buffers
        here = pl.ds(block * ROWS, ROWS)
        below = pl.ds(users + block * ROWS, ROWS)
        cs = [(turn[target_y, p, 0, here, :], turn[target_y, p, 1, here, :]) for p in range(PATHS)]
        if second:
            cs = [times(cs[p], (four[p, 0, here, :], four[p, 1, here, :])) for p in range(PATHS)]
        for n in range(ANTENNAS):
            sums = None
            for p in range(PATHS):
                c, s = cs[p]
                re, im = lead[n, p, 0, here, :], lead[n, p, 1, here, :]
                products = (re * c, im * s, im * c, re * s)
                sums = products if sums is None else tuple(a + b for a, b in zip(sums, products))
            a, b, c, d = sums
            columns = slice(n * width, (n + 1) * width)
            for tone, (re, im) in enumerate(((a - b, c + d), (a + b, c - d))):
                for part, (value, top, bottom) in enumerate(((re, with_re, with_im), (im, with_im, with_re))):
                    packed = value.astype(jnp.bfloat16)
                    top[tone, here, columns] = packed
                    bottom[tone, below, columns] = packed
                    rest = (value - packed.astype(jnp.float32)).astype(jnp.bfloat16)
                    lo[tone, here, slice(part * half + n * width, part * half + (n + 1) * width)] = rest

    def multiply(buffers, z):
        with_re, with_im, lo = buffers
        pair = z * Y_CHIPS + target_y
        slot = jnp.abs(z - chip_z)
        plus, minus = pairs + pair, pairs - 1 - pair
        first = jnp.where(core == 0, plus, minus)
        for tone, (at, out_ref) in enumerate(((first, sent_ref), (plus + minus - first, kept_ref))):
            y = y_ref[at]
            y_hi = y.astype(jnp.bfloat16)
            y_lo = (y - y_hi.astype(jnp.float32)).astype(jnp.bfloat16)
            for part, ref in enumerate((with_re, with_im)):
                ref[tone, 2 * users : 2 * users + 2 * HALF] = y_hi[:, part * half : (part + 1) * half]
                ref[tone, 2 * users + 2 * HALF :] = y_lo[:, part * half : (part + 1) * half]
            by_re = product(with_re[tone], with_re[tone, :users])
            by_im = product(with_im[tone], with_im[tone, :users])
            plain, crossed = by_re[:users] + by_im[:users], by_im[users : 2 * users] - by_re[users : 2 * users]
            out_ref[slot, :users, :] = plain + crossed
            filtered = by_re[2 * users :] + by_im[2 * users :]
            rest = product(y_hi, lo[tone])
            out_ref[slot, users:, :] = filtered[: 2 * HALF] + (filtered[2 * HALF :] + rest)

    even, odd = (re_a, im_a, lo_a), (re_b, im_b, lo_b)

    def alone(block, carry):
        build(even, block, False)
        return carry

    lax.fori_loop(0, blocks, alone, 0, unroll=2)
    multiply(even, 0)
    for block in range(blocks):
        build(odd, block, True)
    multiply(odd, 1)


def tone_systems(place, received, state):
    users, width = state[2].shape[2:]
    wide = received.shape[2]
    f32, bf16 = jnp.float32, jnp.bfloat16
    vmem = pl.BlockSpec(memory_space=pltpu.VMEM)
    smem = pl.BlockSpec(memory_space=pltpu.SMEM)
    channel = pltpu.VMEM((2, 2 * users + 4 * HALF, wide // 2), bf16)
    rest = pltpu.VMEM((2, users, wide), bf16)
    return pl.pallas_call(
        tone_kernel,
        in_specs=[smem] + [vmem] * (1 + len(state)),
        out_specs=[vmem, vmem],
        out_shape=[pltpu.VMEM((Z_CHIPS, users + 2 * HALF, users), f32)] * 2,
        scratch_shapes=[channel, channel, rest] * 2,
        compiler_params=pltpu.CompilerParams(vmem_limit_bytes=16 << 20),
        name="tone_systems",
    )(place, in_vmem(received), *state)


def three_parts(x):
    hi = x.astype(jnp.bfloat16)
    rest = x - hi.astype(jnp.float32)
    mid = rest.astype(jnp.bfloat16)
    return hi, mid, (rest - mid.astype(jnp.float32)).astype(jnp.bfloat16)


def solve_kernel(*refs):
    *part_refs, regularizer_ref, out_ref, system_ref, parts, x_ref, r_ref, p_ref, work = refs
    system_ref[...] = sum(ref[0] for ref in part_refs)
    users = regularizer_ref.shape[1]
    f32 = jnp.float32
    g = system_ref[:users, :]
    flipped = g.T
    row = lax.broadcasted_iota(jnp.int32, (users, users), 0)
    column = lax.broadcasted_iota(jnp.int32, (users, users), 1)
    eye = row == column
    re = 0.5 * (g + flipped)
    im = 0.5 * (g - flipped)
    re = jnp.where(eye, re + regularizer_ref[...], re)
    diagonal = jnp.where(eye, re, 0.0)
    across = lax.rsqrt(jnp.sum(diagonal, 0, keepdims=True))
    down = lax.rsqrt(jnp.sum(diagonal, 1, keepdims=True))
    for k, matrix in enumerate((re, im)):
        for at, part in enumerate(three_parts(matrix * across * down)):
            parts[k, at] = part
    right = system_ref[users:, :] * across

    def together(v):
        total = jnp.sum(v[:HALF] + v[HALF:], 1, keepdims=True)
        return jnp.concatenate([total, total], 0)

    def dot(a, b):
        return jnp.dot(a, b, preferred_element_type=f32)

    rows = 2 * HALF

    def applied(p):
        hi, mid, low = three_parts(p)
        left3 = jnp.concatenate([hi, mid, low], 0)
        left2 = jnp.concatenate([hi, mid], 0)
        result = []
        for k in range(2):
            a = dot(left3, parts[k, 0])
            b = dot(left2, parts[k, 1])
            c = dot(hi, parts[k, 2])
            small = a[2 * rows :] + b[rows:] + c
            result.append(a[:rows] + ((a[rows : 2 * rows] + b[:rows]) + small))
        s, i = result
        return jnp.concatenate([s[:HALF] + i[HALF:], s[HALF:] - i[:HALF]], 0)

    norm = together(right * right)
    goal = norm * (TOLERANCE * TOLERANCE)
    x_ref[...] = jnp.zeros_like(right)
    r_ref[...] = right
    p_ref[...] = right

    def advance(state):
        done, _, rr = state
        for _ in range(2):
            p = p_ref[...]
            q = applied(p)
            pq = together(p * q)
            alpha = jnp.where(pq > 0.0, rr / pq, 0.0)
            x_ref[...] += alpha * p
            r = r_ref[...] - alpha * q
            r_ref[...] = r
            latest = together(r * r)
            p_ref[...] = r + jnp.where(rr > 0.0, latest / rr, 0.0) * p
            rr = latest
        return done + 2, jnp.max(jnp.where(rr <= goal, 0, 1)), rr

    def unfinished(state):
        done, left, _ = state
        return (left > 0) & (done < SOLVE_STEPS)

    _, left, _ = lax.while_loop(unfinished, advance, (0, jnp.max(jnp.where(norm <= goal, 0, 1)), norm))
    out_ref[...] = x_ref[...] * across

    @pl.when(left > 0)
    def _():
        work[0, :users, :] = re
        work[1, :users, :] = -im
        work[0, users:, :] = system_ref[users : users + HALF, :]
        work[1, users:, :] = system_ref[users + HALF :, :]
        lane = lax.broadcasted_iota(jnp.int32, (1, users), 1)

        def eliminate(j, carry):
            a, b = work[0], work[1]
            here = lane == j
            row_re = work[0, pl.ds(j, 1), :]
            row_im = work[1, pl.ds(j, 1), :]
            pivot = 1.0 / jnp.sum(jnp.where(here, row_re, 0.0), 1, keepdims=True)
            col_re = jnp.sum(jnp.where(here, a, 0.0), 1, keepdims=True) * pivot
            col_im = jnp.sum(jnp.where(here, b, 0.0), 1, keepdims=True) * pivot
            work[0] = jnp.where(here, col_re, a - (col_re * row_re - col_im * row_im))
            work[1] = jnp.where(here, col_im, b - (col_re * row_im + col_im * row_re))
            return carry

        lax.fori_loop(0, users, eliminate, 0)
        out_ref[:HALF, :] = work[0, users:, :]
        out_ref[HALF:, :] = work[1, users:, :]


def solved(systems, regularizer):
    _, rows, users = systems[0].shape
    f32 = jnp.float32
    vmem = pl.BlockSpec(memory_space=pltpu.VMEM)
    pair = pltpu.VMEM((2 * HALF, users), f32)
    return pl.pallas_call(
        solve_kernel,
        in_specs=[vmem] * (len(systems) + 1),
        out_specs=vmem,
        out_shape=jax.ShapeDtypeStruct((2 * HALF, users), f32),
        scratch_shapes=[
            pltpu.VMEM((rows, users), f32),
            pltpu.VMEM((2, 3, users, users), jnp.bfloat16),
            pair,
            pair,
            pair,
            pltpu.VMEM((2, users + HALF, users), f32),
        ],
        compiler_params=pltpu.CompilerParams(vmem_limit_bytes=12 << 20),
        name="solved",
    )(*[in_vmem(s) for s in systems], regularizer.reshape(1, users))


def received_rows(observed_signal):
    _, samples, tones, antennas, width = observed_signal.shape
    y = jnp.moveaxis(observed_signal, 2, 0).reshape(tones, 2, samples, antennas * width)
    re, im = y[:, 0], y[:, 1]
    gap = ((0, 0), (0, HALF - samples), (0, 0))
    top = jnp.pad(jnp.concatenate([re, im], 2), gap)
    bottom = jnp.pad(jnp.concatenate([im, -re], 2), gap)
    return jnp.concatenate([top, bottom], 1)


def ap_at(z, y, core):
    return (z * Y_CHIPS + y % Y_CHIPS) * CORES + core


def over_ap(value, dz, dy, dcore):
    spots = [(z, y, c) for z in range(Z_CHIPS) for y in range(Y_CHIPS) for c in range(CORES)]
    pairs = [(ap_at(z, y, c), ap_at(z ^ dz, y + dy, c ^ dcore)) for z, y, c in spots]
    return lax.ppermute(value, "ap", pairs)


def over_sc(value, dz, dx):
    spots = [(z, x) for z in range(2) for x in range(X_CHIPS)]
    pairs = [(z * X_CHIPS + x, (z ^ dz) * X_CHIPS + (x + dx) % X_CHIPS) for z, x in spots]
    return lax.ppermute(value, "sc", pairs)


def gathered_tables(own):
    half = own.shape[0] // 2
    across = over_sc(own, 1, 0)
    up, down = over_sc(own, 0, 1), over_sc(own, 0, -1)
    up_twice, down_twice = over_sc(up[:half], 0, 1), over_sc(down[half:], 0, -1)
    across_up, across_down = over_sc(across, 0, 1), over_sc(across, 0, -1)
    far = over_sc(up_twice, 1, 0), over_sc(down_twice, 1, 0)
    return [own, across, up, down], [up_twice, down_twice, across_up, across_down, *far]


def pack_kernel(*refs):
    *parts, out, sems = refs
    rows = out.shape[0] // len(parts)
    copies = [
        pltpu.make_async_copy(part, out.at[pl.ds(k * rows, rows)], sems.at[k]) for k, part in enumerate(parts)
    ]
    for copy in copies:
        copy.start()
    for copy in copies:
        copy.wait()


def packed_tables(parts):
    rows = sum(part.shape[0] for part in parts)
    vmem = pl.BlockSpec(memory_space=pltpu.VMEM)
    return pl.pallas_call(
        pack_kernel,
        in_specs=[pl.BlockSpec(memory_space=pltpu.HBM)] * len(parts),
        out_specs=vmem,
        out_shape=pltpu.VMEM((rows, *parts[0].shape[1:]), jnp.float32),
        scratch_shapes=[pltpu.SemaphoreType.DMA((len(parts),))],
        compiler_params=pltpu.CompilerParams(vmem_limit_bytes=4 << 20),
        name="packed_tables",
    )(*[pltpu.with_memory_space_constraint(p, pltpu.HBM) for p in parts])


def on_device(observed_signal, delays, sines, path_gain_real, path_gain_imaginary, counts, regularizer):
    tones = observed_signal.shape[2]
    samples = observed_signal.shape[1]
    users = counts.shape[0]
    sc = lax.axis_index("sc")
    ap = lax.axis_index("ap")
    core = ap % CORES
    chip = ap // CORES
    place = jnp.stack([core, chip // Y_CHIPS, chip % Y_CHIPS, sc // X_CHIPS, sc % X_CHIPS]).astype(jnp.int32)
    first = (sc * tones).astype(jnp.float32)
    side = jnp.where(core == 0, -1.0, 1.0)
    centre = jnp.stack([(first + 0.5 * (tones - 1)) * (1.0 / FFT_LEN), side])
    own = packed_tables([delays, sines, path_gain_real, path_gain_imaginary])
    near, far = gathered_tables(own)
    state = prepared(place, centre, NEAR_SLOTS, near, counts)
    state = prepared(place, centre, FAR_SLOTS, far, counts, state)
    received = received_rows(observed_signal)
    rows = users + 2 * HALF
    top = rows // 2

    def systems(distance, *after):
        where = jnp.stack([core, chip // Y_CHIPS, (chip + distance) % Y_CHIPS]).astype(jnp.int32)
        if after:
            where = lax.optimization_barrier((where, *after))[0]
        kept, sent = tone_systems(where, received, state)
        return kept, over_ap(sent, 0, 0, 1)

    kept, other = systems(2)
    next_kept, next_other = systems(1, kept)
    farthest = kept + other
    up, down = over_ap(farthest[:, :top], 0, 1, 0), over_ap(farthest[:, top:], 0, -1, 0)
    last_kept, last_other = systems(3, farthest)
    upward = next_kept + next_other
    upward = jnp.concatenate([upward[:, :top] + up, upward[:, top:]], 1)
    downward = last_kept + last_other
    downward = jnp.concatenate([downward[:, :top], downward[:, top:] + down], 1)
    up, down = over_ap(upward, 0, 1, 0), over_ap(downward, 0, -1, 0)
    kept, other = systems(0, upward, downward)
    mine = (kept + other) + (up + down)
    own_tone = solved([mine[:1], over_ap(mine[1:], 1, 0, 0)], regularizer)
    length = lax.axis_size("ap")
    every = lax.all_to_all(jnp.broadcast_to(own_tone[None], (length, *own_tone.shape)), "ap", 0, 0, tiled=True)
    every = every.reshape(length // CORES, CORES, 2, HALF, users)[:, :, :, :samples]
    every = jnp.concatenate([every[::-1, 0], every[:, 1]], 0)
    return jnp.transpose(every, (1, 2, 0, 3))


def solution(mesh):
    placed = (
        P(None, None, "sc", None, "ap"),
        P(None, "sc", "ap"),
        P(None, "sc", "ap"),
        P(None, "sc", "ap"),
        P(None, "sc", "ap"),
        P(None, "ap"),
        P(),
    )
    return jax.shard_map(
        on_device, mesh=mesh, in_specs=placed, out_specs=P(None, None, "sc", None), check_vma=False
    )
```

```python
import functools

import jax
import jax.numpy as jnp
import numpy as np
from jax import lax
from jax.experimental import pallas as pl
from jax.experimental.pallas import tpu as pltpu
from jax.sharding import PartitionSpec as P


CORES = 2
OWNERS = 8
NEAR_SLOTS = [((0, 0), 0, 0, 0, 8), ((1, 0), 1, 0, 1, 8), ((0, 1), 2, 0, 2, 8), ((0, 3), 3, 0, 3, 8)]
FAR_SLOTS = [((0, 2), 0, 0, 1, 0), ((1, 1), 2, 0, 2, 8), ((1, 3), 3, 0, 3, 8), ((1, 2), 4, 0, 5, 0)]
Y_CHIPS = 4
Z_CHIPS = 2
X_CHIPS = 4
ANTENNAS = 4
PATHS = 4
FFT_LEN = 512
FIT_POINTS = 4001
ROWS = 16
HALF = 16
SOLVE_STEPS = 60
TOLERANCE = 2e-7


def turn_fit():
    u = 0.25 * np.cos(np.pi * (np.arange(FIT_POINTS) + 0.5) / FIT_POINTS)
    cheb = np.polynomial.chebyshev.Chebyshev
    poly = np.polynomial.Polynomial
    x = u * u
    fits = []
    for values, degree in ((np.sin(2 * np.pi * u) / u, 4), (np.cos(2 * np.pi * u), 5)):
        fits.append([float(c) for c in cheb.fit(x, values, degree, domain=[0, 0.0625]).convert(kind=poly).coef])
    return fits


SIN_FIT, COS_FIT = turn_fit()


def horner(x, coefs):
    total = jnp.full_like(x, coefs[-1])
    for c in coefs[-2::-1]:
        total = total * x + c
    return total


def small_turn(u):
    x = u * u
    return horner(x, COS_FIT), u * horner(x, SIN_FIT)


def doubled(c, s):
    return 1.0 - 2.0 * (s * s), 2.0 * (s * c)


def times(a, b):
    return a[0] * b[0] - a[1] * b[1], a[0] * b[1] + a[1] * b[0]


NT = (((1,), (1,)), ((), ()))


def product(a, b):
    return lax.dot_general(a, b, NT, preferred_element_type=jnp.float32)


def prepare_kernel(slots, pieces, place_ref, tone_ref, *refs):
    tab_refs, count_ref = refs[:pieces], refs[pieces]
    lead, turn, four = refs[-3:]
    per_block = count_ref.shape[0] // OWNERS
    sc_z, sc_x = place_ref[3], place_ref[4]
    centre = tone_ref[0]
    side = tone_ref[1]

    def prepare(slot, block, carry):
        (across, along), angles, a_at, gains, g_at = slot
        angles, gains = tab_refs[angles], tab_refs[gains]
        owner = jnp.abs(sc_z - across) * X_CHIPS + (sc_x - along + X_CHIPS) % X_CHIPS
        inside = pl.ds(pl.multiple_of(block * ROWS, ROWS), ROWS)
        here = pl.ds(pl.multiple_of(owner * per_block + block * ROWS, ROWS), ROWS)
        count = count_ref[here, :]
        for p in range(PATHS):
            delay = angles[a_at + p, inside, :]
            sine = angles[a_at + PATHS + p, inside, :]
            alive = p < count
            re = jnp.where(alive, gains[g_at + p, inside, :], 0.0)
            im = jnp.where(alive, gains[g_at + PATHS + p, inside, :], 0.0)
            tones = small_turn(delay * (side * (0.5 / FFT_LEN)))
            one = doubled(*tones)
            for y in range(Y_CHIPS):
                turn[y, p, 0, here, :], turn[y, p, 1, here, :] = tones
                if y + 1 < Y_CHIPS:
                    tones = times(tones, one)
            four[p, 0, here, :], four[p, 1, here, :] = doubled(*doubled(*one))
            turns = delay * centre
            turns = turns - jnp.round(turns)
            c, s = doubled(*small_turn(0.5 * turns))
            z = times((re, im), (c, -s))
            steer = doubled(*small_turn(0.25 * sine))
            for n in range(ANTENNAS):
                lead[n, p, 0, here, :], lead[n, p, 1, here, :] = z
                if n + 1 < ANTENNAS:
                    z = times(z, steer)
        return carry

    for slot in slots:
        lax.fori_loop(0, per_block // ROWS, functools.partial(prepare, slot), 0)


def in_vmem(x):
    return pltpu.with_memory_space_constraint(x, pltpu.VMEM)


def prepared(place, centre, slots, tables, counts, state=None):
    users, width = counts.shape
    f32 = jnp.float32
    vmem = pl.BlockSpec(memory_space=pltpu.VMEM)
    smem = pl.BlockSpec(memory_space=pltpu.SMEM)
    state = () if state is None else state
    first = 3 + len(tables)
    return pl.pallas_call(
        functools.partial(prepare_kernel, slots, len(tables)),
        in_specs=[smem, smem] + [vmem] * (len(tables) + 1 + len(state)),
        out_specs=[vmem] * 3,
        out_shape=[
            pltpu.VMEM((ANTENNAS, PATHS, 2, users, width), f32),
            pltpu.VMEM((Y_CHIPS, PATHS, 2, users, width), f32),
            pltpu.VMEM((PATHS, 2, users, width), f32),
        ],
        input_output_aliases={first + k: k for k in range(len(state))},
        compiler_params=pltpu.CompilerParams(vmem_limit_bytes=4 << 20),
        name="prepared",
    )(place, centre, *[in_vmem(t) for t in tables], in_vmem(counts), *state)


def tone_kernel(place_ref, y_ref, lead, turn, four, kept_ref, sent_ref, re_a, im_a, lo_a, re_b, im_b, lo_b):
    users, width = four.shape[2:]
    blocks = users // ROWS
    half = ANTENNAS * width
    pairs = Y_CHIPS * Z_CHIPS
    core, chip_z, target_y = place_ref[0], place_ref[1], place_ref[2]

    def build(buffers, block, second):
        with_re, with_im, lo = buffers
        here = pl.ds(block * ROWS, ROWS)
        below = pl.ds(users + block * ROWS, ROWS)
        cs = [(turn[target_y, p, 0, here, :], turn[target_y, p, 1, here, :]) for p in range(PATHS)]
        if second:
            cs = [times(cs[p], (four[p, 0, here, :], four[p, 1, here, :])) for p in range(PATHS)]
        for n in range(ANTENNAS):
            sums = None
            for p in range(PATHS):
                c, s = cs[p]
                re, im = lead[n, p, 0, here, :], lead[n, p, 1, here, :]
                products = (re * c, im * s, im * c, re * s)
                sums = products if sums is None else tuple(a + b for a, b in zip(sums, products))
            a, b, c, d = sums
            columns = slice(n * width, (n + 1) * width)
            for tone, (re, im) in enumerate(((a - b, c + d), (a + b, c - d))):
                for part, (value, top, bottom) in enumerate(((re, with_re, with_im), (im, with_im, with_re))):
                    packed = value.astype(jnp.bfloat16)
                    top[tone, here, columns] = packed
                    bottom[tone, below, columns] = packed
                    rest = (value - packed.astype(jnp.float32)).astype(jnp.bfloat16)
                    lo[tone, here, slice(part * half + n * width, part * half + (n + 1) * width)] = rest

    def multiply(buffers, z):
        with_re, with_im, lo = buffers
        pair = z * Y_CHIPS + target_y
        slot = jnp.abs(z - chip_z)
        plus, minus = pairs + pair, pairs - 1 - pair
        first = jnp.where(core == 0, plus, minus)
        for tone, (at, out_ref) in enumerate(((first, sent_ref), (plus + minus - first, kept_ref))):
            y = y_ref[at]
            y_hi = y.astype(jnp.bfloat16)
            y_lo = (y - y_hi.astype(jnp.float32)).astype(jnp.bfloat16)
            for part, ref in enumerate((with_re, with_im)):
                ref[tone, 2 * users : 2 * users + 2 * HALF] = y_hi[:, part * half : (part + 1) * half]
                ref[tone, 2 * users + 2 * HALF :] = y_lo[:, part * half : (part + 1) * half]
            by_re = product(with_re[tone], with_re[tone, :users])
            by_im = product(with_im[tone], with_im[tone, :users])
            plain, crossed = by_re[:users] + by_im[:users], by_im[users : 2 * users] - by_re[users : 2 * users]
            out_ref[slot, :users, :] = plain + crossed
            filtered = by_re[2 * users :] + by_im[2 * users :]
            rest = product(y_hi, lo[tone])
            out_ref[slot, users:, :] = filtered[: 2 * HALF] + (filtered[2 * HALF :] + rest)

    even, odd = (re_a, im_a, lo_a), (re_b, im_b, lo_b)

    def alone(block, carry):
        build(even, block, False)
        return carry

    lax.fori_loop(0, blocks, alone, 0, unroll=2)
    multiply(even, 0)
    for block in range(blocks):
        build(odd, block, True)
    multiply(odd, 1)


def tone_systems(place, received, state):
    users, _ = state[2].shape[2:]
    wide = received.shape[2]
    f32, bf16 = jnp.float32, jnp.bfloat16
    vmem = pl.BlockSpec(memory_space=pltpu.VMEM)
    smem = pl.BlockSpec(memory_space=pltpu.SMEM)
    channel = pltpu.VMEM((2, 2 * users + 4 * HALF, wide // 2), bf16)
    rest = pltpu.VMEM((2, users, wide), bf16)
    return pl.pallas_call(
        tone_kernel,
        in_specs=[smem] + [vmem] * (1 + len(state)),
        out_specs=[vmem, vmem],
        out_shape=[pltpu.VMEM((Z_CHIPS, users + 2 * HALF, users), f32)] * 2,
        scratch_shapes=[channel, channel, rest] * 2,
        compiler_params=pltpu.CompilerParams(vmem_limit_bytes=16 << 20),
        name="tone_systems",
    )(place, in_vmem(received), *state)


def three_parts(x):
    hi = x.astype(jnp.bfloat16)
    rest = x - hi.astype(jnp.float32)
    mid = rest.astype(jnp.bfloat16)
    return hi, mid, (rest - mid.astype(jnp.float32)).astype(jnp.bfloat16)


def solve_kernel(*refs):
    *part_refs, regularizer_ref, out_ref, system_ref, parts, x_ref, r_ref, p_ref, work = refs
    system_ref[...] = sum(ref[0] for ref in part_refs)
    users = regularizer_ref.shape[1]
    f32 = jnp.float32
    g = system_ref[:users, :]
    flipped = g.T
    row = lax.broadcasted_iota(jnp.int32, (users, users), 0)
    column = lax.broadcasted_iota(jnp.int32, (users, users), 1)
    eye = row == column
    re = 0.5 * (g + flipped)
    im = 0.5 * (g - flipped)
    re = jnp.where(eye, re + regularizer_ref[...], re)
    diagonal = jnp.where(eye, re, 0.0)
    across = lax.rsqrt(jnp.sum(diagonal, 0, keepdims=True))
    down = lax.rsqrt(jnp.sum(diagonal, 1, keepdims=True))
    for k, matrix in enumerate((re, im)):
        for at, part in enumerate(three_parts(matrix * across * down)):
            parts[k, at] = part
    right = system_ref[users:, :] * across

    def together(v):
        total = jnp.sum(v[:HALF] + v[HALF:], 1, keepdims=True)
        return jnp.concatenate([total, total], 0)

    def dot(a, b):
        return jnp.dot(a, b, preferred_element_type=f32)

    rows = 2 * HALF

    def applied(p):
        hi, mid, low = three_parts(p)
        left3 = jnp.concatenate([hi, mid, low], 0)
        left2 = jnp.concatenate([hi, mid], 0)
        result = []
        for k in range(2):
            a = dot(left3, parts[k, 0])
            b = dot(left2, parts[k, 1])
            c = dot(hi, parts[k, 2])
            small = a[2 * rows :] + b[rows:] + c
            result.append(a[:rows] + ((a[rows : 2 * rows] + b[:rows]) + small))
        s, i = result
        return jnp.concatenate([s[:HALF] + i[HALF:], s[HALF:] - i[:HALF]], 0)

    norm = together(right * right)
    goal = norm * (TOLERANCE * TOLERANCE)
    x_ref[...] = jnp.zeros_like(right)
    r_ref[...] = right
    p_ref[...] = right

    def advance(state):
        done, _, rr = state
        for _ in range(2):
            p = p_ref[...]
            q = applied(p)
            pq = together(p * q)
            alpha = jnp.where(pq > 0.0, rr / pq, 0.0)
            x_ref[...] += alpha * p
            r = r_ref[...] - alpha * q
            r_ref[...] = r
            latest = together(r * r)
            p_ref[...] = r + jnp.where(rr > 0.0, latest / rr, 0.0) * p
            rr = latest
        return done + 2, jnp.max(jnp.where(rr <= goal, 0, 1)), rr

    def unfinished(state):
        done, left, _ = state
        return (left > 0) & (done < SOLVE_STEPS)

    _, left, _ = lax.while_loop(unfinished, advance, (0, jnp.max(jnp.where(norm <= goal, 0, 1)), norm))
    out_ref[...] = x_ref[...] * across

    @pl.when(left > 0)
    def _():
        work[0, :users, :] = re
        work[1, :users, :] = -im
        work[0, users:, :] = system_ref[users : users + HALF, :]
        work[1, users:, :] = system_ref[users + HALF :, :]
        lane = lax.broadcasted_iota(jnp.int32, (1, users), 1)

        def eliminate(j, carry):
            a, b = work[0], work[1]
            here = lane == j
            row_re = work[0, pl.ds(j, 1), :]
            row_im = work[1, pl.ds(j, 1), :]
            pivot = 1.0 / jnp.sum(jnp.where(here, row_re, 0.0), 1, keepdims=True)
            col_re = jnp.sum(jnp.where(here, a, 0.0), 1, keepdims=True) * pivot
            col_im = jnp.sum(jnp.where(here, b, 0.0), 1, keepdims=True) * pivot
            work[0] = jnp.where(here, col_re, a - (col_re * row_re - col_im * row_im))
            work[1] = jnp.where(here, col_im, b - (col_re * row_im + col_im * row_re))
            return carry

        lax.fori_loop(0, users, eliminate, 0)
        out_ref[:HALF, :] = work[0, users:, :]
        out_ref[HALF:, :] = work[1, users:, :]


def solved(systems, regularizer):
    _, rows, users = systems[0].shape
    f32 = jnp.float32
    vmem = pl.BlockSpec(memory_space=pltpu.VMEM)
    pair = pltpu.VMEM((2 * HALF, users), f32)
    return pl.pallas_call(
        solve_kernel,
        in_specs=[vmem] * (len(systems) + 1),
        out_specs=vmem,
        out_shape=jax.ShapeDtypeStruct((2 * HALF, users), f32),
        scratch_shapes=[
            pltpu.VMEM((rows, users), f32),
            pltpu.VMEM((2, 3, users, users), jnp.bfloat16),
            pair,
            pair,
            pair,
            pltpu.VMEM((2, users + HALF, users), f32),
        ],
        compiler_params=pltpu.CompilerParams(vmem_limit_bytes=12 << 20),
        name="solved",
    )(*[in_vmem(s) for s in systems], regularizer.reshape(1, users))


def received_rows(observed_signal):
    _, samples, tones, antennas, width = observed_signal.shape
    y = jnp.moveaxis(observed_signal, 2, 0).reshape(tones, 2, samples, antennas * width)
    re, im = y[:, 0], y[:, 1]
    gap = ((0, 0), (0, HALF - samples), (0, 0))
    top = jnp.pad(jnp.concatenate([re, im], 2), gap)
    bottom = jnp.pad(jnp.concatenate([im, -re], 2), gap)
    return jnp.concatenate([top, bottom], 1)


def ap_at(z, y, core):
    return (z * Y_CHIPS + y % Y_CHIPS) * CORES + core


def over_ap(value, dz, dy, dcore):
    spots = [(z, y, c) for z in range(Z_CHIPS) for y in range(Y_CHIPS) for c in range(CORES)]
    pairs = [(ap_at(z, y, c), ap_at(z ^ dz, y + dy, c ^ dcore)) for z, y, c in spots]
    return lax.ppermute(value, "ap", pairs)


def over_sc(value, dz, dx):
    spots = [(z, x) for z in range(2) for x in range(X_CHIPS)]
    pairs = [(z * X_CHIPS + x, (z ^ dz) * X_CHIPS + (x + dx) % X_CHIPS) for z, x in spots]
    return lax.ppermute(value, "sc", pairs)


def gathered_tables(own):
    half = own.shape[0] // 2
    across = over_sc(own, 1, 0)
    up, down = over_sc(own, 0, 1), over_sc(own, 0, -1)
    up_twice, down_twice = over_sc(up[:half], 0, 1), over_sc(down[half:], 0, -1)
    across_up, across_down = over_sc(across, 0, 1), over_sc(across, 0, -1)
    far = over_sc(up_twice, 1, 0), over_sc(down_twice, 1, 0)
    return [own, across, up, down], [up_twice, down_twice, across_up, across_down, *far]


def pack_kernel(*refs):
    *parts, out, sems = refs
    rows = out.shape[0] // len(parts)
    copies = [
        pltpu.make_async_copy(part, out.at[pl.ds(k * rows, rows)], sems.at[k]) for k, part in enumerate(parts)
    ]
    for copy in copies:
        copy.start()
    for copy in copies:
        copy.wait()


def packed_tables(parts):
    rows = sum(part.shape[0] for part in parts)
    vmem = pl.BlockSpec(memory_space=pltpu.VMEM)
    return pl.pallas_call(
        pack_kernel,
        in_specs=[pl.BlockSpec(memory_space=pltpu.HBM)] * len(parts),
        out_specs=vmem,
        out_shape=pltpu.VMEM((rows, *parts[0].shape[1:]), jnp.float32),
        scratch_shapes=[pltpu.SemaphoreType.DMA((len(parts),))],
        compiler_params=pltpu.CompilerParams(vmem_limit_bytes=4 << 20),
        name="packed_tables",
    )(*[pltpu.with_memory_space_constraint(p, pltpu.HBM) for p in parts])


def all_steps(observed_signal, delays, sines, path_gain_real, path_gain_imaginary, counts, regularizer):
    tones = observed_signal.shape[2]
    samples = observed_signal.shape[1]
    users = counts.shape[0]
    sc = lax.axis_index("sc")
    ap = lax.axis_index("ap")
    core = ap % CORES
    chip = ap // CORES
    place = jnp.stack([core, chip // Y_CHIPS, chip % Y_CHIPS, sc // X_CHIPS, sc % X_CHIPS]).astype(jnp.int32)
    first = (sc * tones).astype(jnp.float32)
    side = jnp.where(core == 0, -1.0, 1.0)
    centre = jnp.stack([(first + 0.5 * (tones - 1)) * (1.0 / FFT_LEN), side])
    own = packed_tables([delays, sines, path_gain_real, path_gain_imaginary])
    near, far = gathered_tables(own)
    state = prepared(place, centre, NEAR_SLOTS, near, counts)
    state = prepared(place, centre, FAR_SLOTS, far, counts, state)
    received = received_rows(observed_signal)
    rows = users + 2 * HALF
    top = rows // 2

    def systems(distance, *after):
        where = jnp.stack([core, chip // Y_CHIPS, (chip + distance) % Y_CHIPS]).astype(jnp.int32)
        if after:
            where = lax.optimization_barrier((where, *after))[0]
        kept, sent = tone_systems(where, received, state)
        return kept, over_ap(sent, 0, 0, 1)

    def around(value, step):
        return over_ap(value, 0, step, 0)

    kept, other = systems(2)
    next_kept, next_other = systems(1, kept)
    farthest = kept + other
    up, down = around(farthest[:, :top], 1), around(farthest[:, top:], -1)
    last_kept, last_other = systems(3, farthest)
    upward = next_kept + next_other
    upward = jnp.concatenate([upward[:, :top] + up, upward[:, top:]], 1)
    downward = last_kept + last_other
    downward = jnp.concatenate([downward[:, :top], downward[:, top:] + down], 1)
    up, down = around(upward, 1), around(downward, -1)
    kept, other = systems(0, upward, downward)
    mine = (kept + other) + (up + down)
    own_tone = solved([mine[:1], over_ap(mine[1:], 1, 0, 0)], regularizer)
    length = lax.axis_size("ap")
    every = lax.all_to_all(jnp.broadcast_to(own_tone[None], (length, *own_tone.shape)), "ap", 0, 0, tiled=True)
    every = every.reshape(length // CORES, CORES, 2, HALF, users)[:, :, :, :samples]
    every = jnp.concatenate([every[::-1, 0], every[:, 1]], 0)
    return jnp.transpose(every, (1, 2, 0, 3))


def solution(mesh):
    placed = (
        P(None, None, "sc", None, "ap"),
        P(None, "sc", "ap"),
        P(None, "sc", "ap"),
        P(None, "sc", "ap"),
        P(None, "sc", "ap"),
        P(None, "ap"),
        P(),
    )
    return jax.shard_map(all_steps, mesh=mesh, in_specs=placed, out_specs=P(None, None, "sc", None), check_vma=False)
```

```python
import functools

import jax
import jax.numpy as jnp
import numpy as np
from jax import lax
from jax.experimental import pallas as pl
from jax.experimental.pallas import tpu as pltpu
from jax.sharding import PartitionSpec as P


CORES = 2
OWNERS = 8
NEAR_SLOTS = [((0, 0), 0, 0, 0, 8), ((1, 0), 1, 0, 1, 8), ((0, 1), 2, 0, 2, 8), ((0, 3), 3, 0, 3, 8)]
MIDDLE_SLOTS = [((0, 2), 0, 0, 1, 0), ((1, 1), 2, 0, 2, 8), ((1, 3), 3, 0, 3, 8)]
FAR_SLOTS = [((1, 2), 0, 0, 1, 0)]
Y_CHIPS = 4
Z_CHIPS = 2
X_CHIPS = 4
ANTENNAS = 4
PATHS = 4
FFT_LEN = 512
FIT_POINTS = 4001
ROWS = 16
HALF = 16
SOLVE_STEPS = 60
TOLERANCE = 2e-7


def turn_fit():
    u = 0.25 * np.cos(np.pi * (np.arange(FIT_POINTS) + 0.5) / FIT_POINTS)
    cheb = np.polynomial.chebyshev.Chebyshev
    poly = np.polynomial.Polynomial
    x = u * u
    fits = []
    for values, degree in ((np.sin(2 * np.pi * u) / u, 4), (np.cos(2 * np.pi * u), 5)):
        fits.append([float(c) for c in cheb.fit(x, values, degree, domain=[0, 0.0625]).convert(kind=poly).coef])
    return fits


SIN_FIT, COS_FIT = turn_fit()


def horner(x, coefs):
    total = jnp.full_like(x, coefs[-1])
    for c in coefs[-2::-1]:
        total = total * x + c
    return total


def small_turn(u):
    x = u * u
    return horner(x, COS_FIT), u * horner(x, SIN_FIT)


def doubled(c, s):
    return 1.0 - 2.0 * (s * s), 2.0 * (s * c)


def times(a, b):
    return a[0] * b[0] - a[1] * b[1], a[0] * b[1] + a[1] * b[0]


NT = (((1,), (1,)), ((), ()))


def product(a, b):
    return lax.dot_general(a, b, NT, preferred_element_type=jnp.float32)


def prepare_kernel(slots, pieces, place_ref, tone_ref, *refs):
    tab_refs, count_ref = refs[:pieces], refs[pieces]
    lead, turn, four = refs[-3:]
    per_block = count_ref.shape[0] // OWNERS
    sc_z, sc_x = place_ref[3], place_ref[4]
    centre = tone_ref[0]
    side = tone_ref[1]

    def prepare(slot, block, carry):
        (across, along), angles, a_at, gains, g_at = slot
        angles, gains = tab_refs[angles], tab_refs[gains]
        owner = jnp.abs(sc_z - across) * X_CHIPS + (sc_x - along + X_CHIPS) % X_CHIPS
        inside = pl.ds(pl.multiple_of(block * ROWS, ROWS), ROWS)
        here = pl.ds(pl.multiple_of(owner * per_block + block * ROWS, ROWS), ROWS)
        count = count_ref[here, :]
        for p in range(PATHS):
            delay = angles[a_at + p, inside, :]
            sine = angles[a_at + PATHS + p, inside, :]
            alive = p < count
            re = jnp.where(alive, gains[g_at + p, inside, :], 0.0)
            im = jnp.where(alive, gains[g_at + PATHS + p, inside, :], 0.0)
            tones = small_turn(delay * (side * (0.5 / FFT_LEN)))
            one = doubled(*tones)
            for y in range(Y_CHIPS):
                turn[y, p, 0, here, :], turn[y, p, 1, here, :] = tones
                if y + 1 < Y_CHIPS:
                    tones = times(tones, one)
            four[p, 0, here, :], four[p, 1, here, :] = doubled(*doubled(*one))
            turns = delay * centre
            turns = turns - jnp.round(turns)
            c, s = doubled(*small_turn(0.5 * turns))
            z = times((re, im), (c, -s))
            steer = doubled(*small_turn(0.25 * sine))
            for n in range(ANTENNAS):
                lead[n, p, 0, here, :], lead[n, p, 1, here, :] = z
                if n + 1 < ANTENNAS:
                    z = times(z, steer)
        return carry

    for slot in slots:
        lax.fori_loop(0, per_block // ROWS, functools.partial(prepare, slot), 0)


def in_vmem(x):
    return pltpu.with_memory_space_constraint(x, pltpu.VMEM)


def prepared(place, centre, slots, tables, counts, state=None):
    users, width = counts.shape
    f32 = jnp.float32
    vmem = pl.BlockSpec(memory_space=pltpu.VMEM)
    smem = pl.BlockSpec(memory_space=pltpu.SMEM)
    state = () if state is None else state
    first = 3 + len(tables)
    return pl.pallas_call(
        functools.partial(prepare_kernel, slots, len(tables)),
        in_specs=[smem, smem] + [vmem] * (len(tables) + 1 + len(state)),
        out_specs=[vmem] * 3,
        out_shape=[
            pltpu.VMEM((ANTENNAS, PATHS, 2, users, width), f32),
            pltpu.VMEM((Y_CHIPS, PATHS, 2, users, width), f32),
            pltpu.VMEM((PATHS, 2, users, width), f32),
        ],
        input_output_aliases={first + k: k for k in range(len(state))},
        compiler_params=pltpu.CompilerParams(vmem_limit_bytes=4 << 20),
        name="prepared",
    )(place, centre, *[in_vmem(t) for t in tables], in_vmem(counts), *state)


def tone_kernel(place_ref, y_ref, lead, turn, four, kept_ref, sent_ref, re_a, im_a, lo_a, re_b, im_b, lo_b):
    users, width = four.shape[2:]
    blocks = users // ROWS
    half = ANTENNAS * width
    pairs = Y_CHIPS * Z_CHIPS
    core, chip_z, target_y = place_ref[0], place_ref[1], place_ref[2]

    def build(buffers, block, second):
        with_re, with_im, lo = buffers
        here = pl.ds(block * ROWS, ROWS)
        below = pl.ds(users + block * ROWS, ROWS)
        cs = [(turn[target_y, p, 0, here, :], turn[target_y, p, 1, here, :]) for p in range(PATHS)]
        if second:
            cs = [times(cs[p], (four[p, 0, here, :], four[p, 1, here, :])) for p in range(PATHS)]
        for n in range(ANTENNAS):
            sums = None
            for p in range(PATHS):
                c, s = cs[p]
                re, im = lead[n, p, 0, here, :], lead[n, p, 1, here, :]
                products = (re * c, im * s, im * c, re * s)
                sums = products if sums is None else tuple(a + b for a, b in zip(sums, products))
            a, b, c, d = sums
            columns = slice(n * width, (n + 1) * width)
            for tone, (re, im) in enumerate(((a - b, c + d), (a + b, c - d))):
                for part, (value, top, bottom) in enumerate(((re, with_re, with_im), (im, with_im, with_re))):
                    packed = value.astype(jnp.bfloat16)
                    top[tone, here, columns] = packed
                    bottom[tone, below, columns] = packed
                    rest = (value - packed.astype(jnp.float32)).astype(jnp.bfloat16)
                    lo[tone, here, slice(part * half + n * width, part * half + (n + 1) * width)] = rest

    def multiply(buffers, z):
        with_re, with_im, lo = buffers
        pair = z * Y_CHIPS + target_y
        slot = jnp.abs(z - chip_z)
        plus, minus = pairs + pair, pairs - 1 - pair
        first = jnp.where(core == 0, plus, minus)
        for tone, (at, out_ref) in enumerate(((first, sent_ref), (plus + minus - first, kept_ref))):
            y = y_ref[at]
            y_hi = y.astype(jnp.bfloat16)
            y_lo = (y - y_hi.astype(jnp.float32)).astype(jnp.bfloat16)
            for part, ref in enumerate((with_re, with_im)):
                ref[tone, 2 * users : 2 * users + 2 * HALF] = y_hi[:, part * half : (part + 1) * half]
                ref[tone, 2 * users + 2 * HALF :] = y_lo[:, part * half : (part + 1) * half]
            by_re = product(with_re[tone], with_re[tone, :users])
            by_im = product(with_im[tone], with_im[tone, :users])
            plain, crossed = by_re[:users] + by_im[:users], by_im[users : 2 * users] - by_re[users : 2 * users]
            out_ref[slot, :users, :] = plain + crossed
            filtered = by_re[2 * users :] + by_im[2 * users :]
            rest = product(y_hi, lo[tone])
            out_ref[slot, users:, :] = filtered[: 2 * HALF] + (filtered[2 * HALF :] + rest)

    even, odd = (re_a, im_a, lo_a), (re_b, im_b, lo_b)

    def alone(block, carry):
        build(even, block, False)
        return carry

    lax.fori_loop(0, blocks, alone, 0, unroll=2)
    multiply(even, 0)
    for block in range(blocks):
        build(odd, block, True)
    multiply(odd, 1)


def tone_systems(place, received, state):
    users, _ = state[2].shape[2:]
    wide = received.shape[2]
    f32, bf16 = jnp.float32, jnp.bfloat16
    vmem = pl.BlockSpec(memory_space=pltpu.VMEM)
    smem = pl.BlockSpec(memory_space=pltpu.SMEM)
    channel = pltpu.VMEM((2, 2 * users + 4 * HALF, wide // 2), bf16)
    rest = pltpu.VMEM((2, users, wide), bf16)
    return pl.pallas_call(
        tone_kernel,
        in_specs=[smem] + [vmem] * (1 + len(state)),
        out_specs=[vmem, vmem],
        out_shape=[pltpu.VMEM((Z_CHIPS, users + 2 * HALF, users), f32)] * 2,
        scratch_shapes=[channel, channel, rest] * 2,
        compiler_params=pltpu.CompilerParams(vmem_limit_bytes=16 << 20),
        name="tone_systems",
    )(place, in_vmem(received), *state)


def three_parts(x):
    hi = x.astype(jnp.bfloat16)
    rest = x - hi.astype(jnp.float32)
    mid = rest.astype(jnp.bfloat16)
    return hi, mid, (rest - mid.astype(jnp.float32)).astype(jnp.bfloat16)


def solve_kernel(*refs):
    *part_refs, regularizer_ref, out_ref, system_ref, parts, x_ref, r_ref, p_ref, work = refs
    system_ref[...] = sum(ref[0] for ref in part_refs)
    users = regularizer_ref.shape[1]
    f32 = jnp.float32
    g = system_ref[:users, :]
    flipped = g.T
    row = lax.broadcasted_iota(jnp.int32, (users, users), 0)
    column = lax.broadcasted_iota(jnp.int32, (users, users), 1)
    eye = row == column
    re = 0.5 * (g + flipped)
    im = 0.5 * (g - flipped)
    re = jnp.where(eye, re + regularizer_ref[...], re)
    diagonal = jnp.where(eye, re, 0.0)
    across = lax.rsqrt(jnp.sum(diagonal, 0, keepdims=True))
    down = lax.rsqrt(jnp.sum(diagonal, 1, keepdims=True))
    for k, matrix in enumerate((re, im)):
        for at, part in enumerate(three_parts(matrix * across * down)):
            parts[k, at] = part
    right = system_ref[users:, :] * across

    def together(v):
        total = jnp.sum(v[:HALF] + v[HALF:], 1, keepdims=True)
        return jnp.concatenate([total, total], 0)

    def dot(a, b):
        return jnp.dot(a, b, preferred_element_type=f32)

    rows = 2 * HALF

    def applied(p):
        hi, mid, low = three_parts(p)
        left3 = jnp.concatenate([hi, mid, low], 0)
        left2 = jnp.concatenate([hi, mid], 0)
        result = []
        for k in range(2):
            a = dot(left3, parts[k, 0])
            b = dot(left2, parts[k, 1])
            c = dot(hi, parts[k, 2])
            small = a[2 * rows :] + b[rows:] + c
            result.append(a[:rows] + ((a[rows : 2 * rows] + b[:rows]) + small))
        s, i = result
        return jnp.concatenate([s[:HALF] + i[HALF:], s[HALF:] - i[:HALF]], 0)

    norm = together(right * right)
    goal = norm * (TOLERANCE * TOLERANCE)
    x_ref[...] = jnp.zeros_like(right)
    r_ref[...] = right
    p_ref[...] = right

    def advance(state):
        done, _, rr = state
        for _ in range(2):
            p = p_ref[...]
            q = applied(p)
            pq = together(p * q)
            alpha = jnp.where(pq > 0.0, rr / pq, 0.0)
            x_ref[...] += alpha * p
            r = r_ref[...] - alpha * q
            r_ref[...] = r
            latest = together(r * r)
            p_ref[...] = r + jnp.where(rr > 0.0, latest / rr, 0.0) * p
            rr = latest
        return done + 2, jnp.max(jnp.where(rr <= goal, 0, 1)), rr

    def unfinished(state):
        done, left, _ = state
        return (left > 0) & (done < SOLVE_STEPS)

    _, left, _ = lax.while_loop(unfinished, advance, (0, jnp.max(jnp.where(norm <= goal, 0, 1)), norm))
    out_ref[...] = x_ref[...] * across

    @pl.when(left > 0)
    def _():
        work[0, :users, :] = re
        work[1, :users, :] = -im
        work[0, users:, :] = system_ref[users : users + HALF, :]
        work[1, users:, :] = system_ref[users + HALF :, :]
        lane = lax.broadcasted_iota(jnp.int32, (1, users), 1)

        def eliminate(j, carry):
            a, b = work[0], work[1]
            here = lane == j
            row_re = work[0, pl.ds(j, 1), :]
            row_im = work[1, pl.ds(j, 1), :]
            pivot = 1.0 / jnp.sum(jnp.where(here, row_re, 0.0), 1, keepdims=True)
            col_re = jnp.sum(jnp.where(here, a, 0.0), 1, keepdims=True) * pivot
            col_im = jnp.sum(jnp.where(here, b, 0.0), 1, keepdims=True) * pivot
            work[0] = jnp.where(here, col_re, a - (col_re * row_re - col_im * row_im))
            work[1] = jnp.where(here, col_im, b - (col_re * row_im + col_im * row_re))
            return carry

        lax.fori_loop(0, users, eliminate, 0)
        out_ref[:HALF, :] = work[0, users:, :]
        out_ref[HALF:, :] = work[1, users:, :]


def solved(systems, regularizer):
    _, rows, users = systems[0].shape
    f32 = jnp.float32
    vmem = pl.BlockSpec(memory_space=pltpu.VMEM)
    pair = pltpu.VMEM((2 * HALF, users), f32)
    return pl.pallas_call(
        solve_kernel,
        in_specs=[vmem] * (len(systems) + 1),
        out_specs=vmem,
        out_shape=jax.ShapeDtypeStruct((2 * HALF, users), f32),
        scratch_shapes=[
            pltpu.VMEM((rows, users), f32),
            pltpu.VMEM((2, 3, users, users), jnp.bfloat16),
            pair,
            pair,
            pair,
            pltpu.VMEM((2, users + HALF, users), f32),
        ],
        compiler_params=pltpu.CompilerParams(vmem_limit_bytes=12 << 20),
        name="solved",
    )(*[in_vmem(s) for s in systems], regularizer.reshape(1, users))


def received_rows(observed_signal):
    _, samples, tones, antennas, width = observed_signal.shape
    y = jnp.moveaxis(observed_signal, 2, 0).reshape(tones, 2, samples, antennas * width)
    re, im = y[:, 0], y[:, 1]
    gap = ((0, 0), (0, HALF - samples), (0, 0))
    top = jnp.pad(jnp.concatenate([re, im], 2), gap)
    bottom = jnp.pad(jnp.concatenate([im, -re], 2), gap)
    return jnp.concatenate([top, bottom], 1)


def ap_at(z, y, core):
    return (z * Y_CHIPS + y % Y_CHIPS) * CORES + core


def over_ap(value, dz, dy, dcore):
    spots = [(z, y, c) for z in range(Z_CHIPS) for y in range(Y_CHIPS) for c in range(CORES)]
    pairs = [(ap_at(z, y, c), ap_at(z ^ dz, y + dy, c ^ dcore)) for z, y, c in spots]
    return lax.ppermute(value, "ap", pairs)


def over_sc(value, dz, dx):
    spots = [(z, x) for z in range(2) for x in range(X_CHIPS)]
    pairs = [(z * X_CHIPS + x, (z ^ dz) * X_CHIPS + (x + dx) % X_CHIPS) for z, x in spots]
    return lax.ppermute(value, "sc", pairs)


def gathered_tables(own):
    half = own.shape[0] // 2

    across = over_sc(own, 1, 0)
    up, down = over_sc(own, 0, 1), over_sc(own, 0, -1)
    across_up, across_down = over_sc(across, 0, 1), over_sc(across, 0, -1)
    up_twice, down_twice = over_sc(up[:half], 0, 1), over_sc(down[half:], 0, -1)
    far = over_sc(up_twice, 1, 0), over_sc(down_twice, 1, 0)
    return [own, across, up, down], [up_twice, down_twice, across_up, across_down], list(far)


def pack_kernel(*refs):
    *parts, out, sems = refs
    rows = out.shape[0] // len(parts)
    copies = [
        pltpu.make_async_copy(part, out.at[pl.ds(k * rows, rows)], sems.at[k]) for k, part in enumerate(parts)
    ]
    for copy in copies:
        copy.start()
    for copy in copies:
        copy.wait()


def packed_tables(parts):
    rows = sum(part.shape[0] for part in parts)
    vmem = pl.BlockSpec(memory_space=pltpu.VMEM)
    return pl.pallas_call(
        pack_kernel,
        in_specs=[pl.BlockSpec(memory_space=pltpu.HBM)] * len(parts),
        out_specs=vmem,
        out_shape=pltpu.VMEM((rows, *parts[0].shape[1:]), jnp.float32),
        scratch_shapes=[pltpu.SemaphoreType.DMA((len(parts),))],
        compiler_params=pltpu.CompilerParams(vmem_limit_bytes=4 << 20),
        name="packed_tables",
    )(*[pltpu.with_memory_space_constraint(p, pltpu.HBM) for p in parts])


def all_steps(observed_signal, delays, sines, path_gain_real, path_gain_imaginary, counts, regularizer):
    tones = observed_signal.shape[2]
    samples = observed_signal.shape[1]
    users = counts.shape[0]
    sc = lax.axis_index("sc")
    ap = lax.axis_index("ap")
    core = ap % CORES
    chip = ap // CORES
    place = jnp.stack([core, chip // Y_CHIPS, chip % Y_CHIPS, sc // X_CHIPS, sc % X_CHIPS]).astype(jnp.int32)
    first = (sc * tones).astype(jnp.float32)
    side = jnp.where(core == 0, -1.0, 1.0)
    centre = jnp.stack([(first + 0.5 * (tones - 1)) * (1.0 / FFT_LEN), side])
    own = packed_tables([delays, sines, path_gain_real, path_gain_imaginary])
    near, middle, far = gathered_tables(own)
    state = prepared(place, centre, NEAR_SLOTS, near, counts)
    state = prepared(place, centre, MIDDLE_SLOTS, middle, counts, state)
    state = prepared(place, centre, FAR_SLOTS, far, counts, state)
    received = received_rows(observed_signal)
    rows = users + 2 * HALF
    top = rows // 2

    def systems(distance, *after):
        where = jnp.stack([core, chip // Y_CHIPS, (chip + distance) % Y_CHIPS]).astype(jnp.int32)
        if after:
            where = lax.optimization_barrier((where, *after))[0]
        kept, sent = tone_systems(where, received, state)
        return kept, over_ap(sent, 0, 0, 1)

    def around(value, step):
        return over_ap(value, 0, step, 0)

    kept, other = systems(2)
    farthest = kept + other
    up, down = around(farthest[:, :top], 1), around(farthest[:, top:], -1)
    next_kept, next_other = systems(1, farthest)
    last_kept, last_other = systems(3, next_kept)
    upward = next_kept + next_other
    upward = jnp.concatenate([upward[:, :top] + up, upward[:, top:]], 1)
    downward = last_kept + last_other
    downward = jnp.concatenate([downward[:, :top], downward[:, top:] + down], 1)
    up, down = around(upward, 1), around(downward, -1)
    kept, other = systems(0, upward, downward)
    mine = (kept + other) + (up + down)
    own_tone = solved([mine[:1], over_ap(mine[1:], 1, 0, 0)], regularizer)
    chips = lax.axis_size("ap") // CORES
    same = [[chip * CORES + c for chip in range(chips)] for c in range(CORES)]
    same_core = lax.all_to_all(
        jnp.broadcast_to(own_tone[None], (chips, *own_tone.shape)), "ap", 0, 0, tiled=True, axis_index_groups=same
    )
    other_core = over_ap(same_core, 0, 0, 1)
    first = jnp.where(core == 0, same_core, other_core)[::-1]
    second = jnp.where(core == 0, other_core, same_core)
    every = jnp.concatenate([first, second], 0).reshape(tones, 2, HALF, users)[:, :, :samples]
    return jnp.transpose(every, (1, 2, 0, 3))


def solution(mesh):
    placed = (
        P(None, None, "sc", None, "ap"),
        P(None, "sc", "ap"),
        P(None, "sc", "ap"),
        P(None, "sc", "ap"),
        P(None, "sc", "ap"),
        P(None, "ap"),
        P(),
    )
    return jax.shard_map(all_steps, mesh=mesh, in_specs=placed, out_specs=P(None, None, "sc", None), check_vma=False)
```

```python
import functools

import jax
import jax.numpy as jnp
import numpy as np
from jax import lax
from jax.experimental import pallas as pl
from jax.experimental.pallas import tpu as pltpu
from jax.sharding import PartitionSpec as P


CORES = 2
OWNERS = 8
NEAR_SLOTS = [((0, 0), 0, 0, 0, 8), ((1, 0), 1, 0, 1, 8), ((0, 1), 2, 0, 2, 8), ((0, 3), 3, 0, 3, 8)]
FAR_SLOTS = [((0, 2), 0, 0, 0, 8), ((1, 1), 1, 0, 1, 8), ((1, 3), 2, 0, 2, 8), ((1, 2), 3, 0, 3, 8)]
Y_CHIPS = 4
Z_CHIPS = 2
X_CHIPS = 4
ANTENNAS = 4
PATHS = 4
FFT_LEN = 512
FIT_POINTS = 4001
ROWS = 16
HALF = 16
SOLVE_STEPS = 60
TOLERANCE = 1e-6


def turn_fit():
    u = 0.25 * np.cos(np.pi * (np.arange(FIT_POINTS) + 0.5) / FIT_POINTS)
    cheb = np.polynomial.chebyshev.Chebyshev
    poly = np.polynomial.Polynomial
    x = u * u
    fits = []
    for values, degree in ((np.sin(2 * np.pi * u) / u, 4), (np.cos(2 * np.pi * u), 5)):
        fits.append([float(c) for c in cheb.fit(x, values, degree, domain=[0, 0.0625]).convert(kind=poly).coef])
    return fits


SIN_FIT, COS_FIT = turn_fit()


def horner(x, coefs):
    total = jnp.full_like(x, coefs[-1])
    for c in coefs[-2::-1]:
        total = total * x + c
    return total


def small_turn(u):
    x = u * u
    return horner(x, COS_FIT), u * horner(x, SIN_FIT)


def doubled(c, s):
    return 1.0 - 2.0 * (s * s), 2.0 * (s * c)


def times(a, b):
    return a[0] * b[0] - a[1] * b[1], a[0] * b[1] + a[1] * b[0]


NT = (((1,), (1,)), ((), ()))


def product(a, b):
    return lax.dot_general(a, b, NT, preferred_element_type=jnp.float32)


def prepare_kernel(slots, pieces, place_ref, tone_ref, *refs):
    tab_refs, count_ref = refs[:pieces], refs[pieces]
    lead, turn, four = refs[-3:]
    per_block = count_ref.shape[0] // OWNERS
    sc_z, sc_x = place_ref[3], place_ref[4]
    centre = tone_ref[0]
    side = tone_ref[1]

    def prepare(slot, block, carry):
        (across, along), angles, a_at, gains, g_at = slot
        angles, gains = tab_refs[angles], tab_refs[gains]
        owner = jnp.abs(sc_z - across) * X_CHIPS + (sc_x - along + X_CHIPS) % X_CHIPS
        inside = pl.ds(pl.multiple_of(block * ROWS, ROWS), ROWS)
        here = pl.ds(pl.multiple_of(owner * per_block + block * ROWS, ROWS), ROWS)
        count = count_ref[here, :]
        for p in range(PATHS):
            delay = angles[a_at + p, inside, :]
            sine = angles[a_at + PATHS + p, inside, :]
            alive = p < count
            re = jnp.where(alive, gains[g_at + p, inside, :], 0.0)
            im = jnp.where(alive, gains[g_at + PATHS + p, inside, :], 0.0)
            tones = small_turn(delay * (side * (0.5 / FFT_LEN)))
            one = doubled(*tones)
            for y in range(Y_CHIPS):
                turn[y, p, 0, here, :], turn[y, p, 1, here, :] = tones
                if y + 1 < Y_CHIPS:
                    tones = times(tones, one)
            four[p, 0, here, :], four[p, 1, here, :] = doubled(*doubled(*one))
            turns = delay * centre
            turns = turns - jnp.round(turns)
            c, s = doubled(*small_turn(0.5 * turns))
            z = times((re, im), (c, -s))
            steer = doubled(*small_turn(0.25 * sine))
            for n in range(ANTENNAS):
                lead[n, p, 0, here, :], lead[n, p, 1, here, :] = z
                if n + 1 < ANTENNAS:
                    z = times(z, steer)
        return carry

    for slot in slots:
        lax.fori_loop(0, per_block // ROWS, functools.partial(prepare, slot), 0)


def in_vmem(x):
    return pltpu.with_memory_space_constraint(x, pltpu.VMEM)


def prepared(place, centre, slots, tables, counts, state=None):
    users, width = counts.shape
    f32 = jnp.float32
    vmem = pl.BlockSpec(memory_space=pltpu.VMEM)
    smem = pl.BlockSpec(memory_space=pltpu.SMEM)
    state = () if state is None else state
    first = 3 + len(tables)
    return pl.pallas_call(
        functools.partial(prepare_kernel, slots, len(tables)),
        in_specs=[smem, smem] + [vmem] * (len(tables) + 1 + len(state)),
        out_specs=[vmem] * 3,
        out_shape=[
            pltpu.VMEM((ANTENNAS, PATHS, 2, users, width), f32),
            pltpu.VMEM((Y_CHIPS, PATHS, 2, users, width), f32),
            pltpu.VMEM((PATHS, 2, users, width), f32),
        ],
        input_output_aliases={first + k: k for k in range(len(state))},
        compiler_params=pltpu.CompilerParams(vmem_limit_bytes=4 << 20),
        name="prepared",
    )(place, centre, *[in_vmem(t) for t in tables], in_vmem(counts), *state)


def tone_kernel(place_ref, y_ref, lead, turn, four, kept_ref, sent_ref, re_a, im_a, lo_a, re_b, im_b, lo_b):
    users, width = four.shape[2:]
    blocks = users // ROWS
    half = ANTENNAS * width
    pairs = Y_CHIPS * Z_CHIPS
    core, chip_z, target_y = place_ref[0], place_ref[1], place_ref[2]

    def build(buffers, block, second):
        with_re, with_im, lo = buffers
        here = pl.ds(block * ROWS, ROWS)
        below = pl.ds(users + block * ROWS, ROWS)
        cs = [(turn[target_y, p, 0, here, :], turn[target_y, p, 1, here, :]) for p in range(PATHS)]
        if second:
            cs = [times(cs[p], (four[p, 0, here, :], four[p, 1, here, :])) for p in range(PATHS)]
        for n in range(ANTENNAS):
            sums = None
            for p in range(PATHS):
                c, s = cs[p]
                re, im = lead[n, p, 0, here, :], lead[n, p, 1, here, :]
                products = (re * c, im * s, im * c, re * s)
                sums = products if sums is None else tuple(a + b for a, b in zip(sums, products))
            a, b, c, d = sums
            columns = slice(n * width, (n + 1) * width)
            for tone, (re, im) in enumerate(((a - b, c + d), (a + b, c - d))):
                for part, (value, top, bottom) in enumerate(((re, with_re, with_im), (im, with_im, with_re))):
                    packed = value.astype(jnp.bfloat16)
                    top[tone, here, columns] = packed
                    bottom[tone, below, columns] = packed
                    rest = (value - packed.astype(jnp.float32)).astype(jnp.bfloat16)
                    lo[tone, here, slice(part * half + n * width, part * half + (n + 1) * width)] = rest

    def multiply(buffers, z):
        with_re, with_im, lo = buffers
        pair = z * Y_CHIPS + target_y
        slot = jnp.abs(z - chip_z)
        plus, minus = pairs + pair, pairs - 1 - pair
        first = jnp.where(core == 0, plus, minus)
        for tone, (at, out_ref) in enumerate(((first, sent_ref), (plus + minus - first, kept_ref))):
            y = y_ref[at]
            y_hi = y.astype(jnp.bfloat16)
            y_lo = (y - y_hi.astype(jnp.float32)).astype(jnp.bfloat16)
            for part, ref in enumerate((with_re, with_im)):
                ref[tone, 2 * users : 2 * users + 2 * HALF] = y_hi[:, part * half : (part + 1) * half]
                ref[tone, 2 * users + 2 * HALF :] = y_lo[:, part * half : (part + 1) * half]
            by_re = product(with_re[tone], with_re[tone, :users])
            by_im = product(with_im[tone], with_im[tone, :users])
            plain, crossed = by_re[:users] + by_im[:users], by_im[users : 2 * users] - by_re[users : 2 * users]
            out_ref[slot, :users, :] = plain + crossed
            filtered = by_re[2 * users :] + by_im[2 * users :]
            rest = product(y_hi, lo[tone])
            out_ref[slot, users:, :] = filtered[: 2 * HALF] + (filtered[2 * HALF :] + rest)

    even, odd = (re_a, im_a, lo_a), (re_b, im_b, lo_b)

    def alone(block, carry):
        build(even, block, False)
        return carry

    lax.fori_loop(0, blocks, alone, 0, unroll=2)
    multiply(even, 0)
    for block in range(blocks):
        build(odd, block, True)
    multiply(odd, 1)


def tone_systems(place, received, state):
    users, _ = state[2].shape[2:]
    wide = received.shape[2]
    f32, bf16 = jnp.float32, jnp.bfloat16
    vmem = pl.BlockSpec(memory_space=pltpu.VMEM)
    smem = pl.BlockSpec(memory_space=pltpu.SMEM)
    channel = pltpu.VMEM((2, 2 * users + 4 * HALF, wide // 2), bf16)
    rest = pltpu.VMEM((2, users, wide), bf16)
    return pl.pallas_call(
        tone_kernel,
        in_specs=[smem] + [vmem] * (1 + len(state)),
        out_specs=[vmem, vmem],
        out_shape=[pltpu.VMEM((Z_CHIPS, users + 2 * HALF, users), f32)] * 2,
        scratch_shapes=[channel, channel, rest] * 2,
        compiler_params=pltpu.CompilerParams(vmem_limit_bytes=16 << 20),
        name="tone_systems",
    )(place, in_vmem(received), *state)


def three_parts(x):
    hi = x.astype(jnp.bfloat16)
    rest = x - hi.astype(jnp.float32)
    mid = rest.astype(jnp.bfloat16)
    return hi, mid, (rest - mid.astype(jnp.float32)).astype(jnp.bfloat16)


def solve_kernel(*refs):
    *part_refs, regularizer_ref, out_ref, system_ref, parts, x_ref, r_ref, p_ref, work = refs
    system_ref[...] = sum(ref[0] for ref in part_refs)
    users = regularizer_ref.shape[1]
    f32 = jnp.float32
    g = system_ref[:users, :]
    flipped = g.T
    row = lax.broadcasted_iota(jnp.int32, (users, users), 0)
    column = lax.broadcasted_iota(jnp.int32, (users, users), 1)
    eye = row == column
    re = 0.5 * (g + flipped)
    im = 0.5 * (g - flipped)
    re = jnp.where(eye, re + regularizer_ref[...], re)
    diagonal = jnp.where(eye, re, 0.0)
    across = lax.rsqrt(jnp.sum(diagonal, 0, keepdims=True))
    down = lax.rsqrt(jnp.sum(diagonal, 1, keepdims=True))
    for k, matrix in enumerate((re, im)):
        for at, part in enumerate(three_parts(matrix * across * down)):
            parts[k, at] = part
    right = system_ref[users:, :] * across

    def together(v):
        total = jnp.sum(v[:HALF] + v[HALF:], 1, keepdims=True)
        return jnp.concatenate([total, total], 0)

    def dot(a, b):
        return jnp.dot(a, b, preferred_element_type=f32)

    rows = 2 * HALF

    def applied(p):
        hi, mid, low = three_parts(p)
        left3 = jnp.concatenate([hi, mid, low], 0)
        left2 = jnp.concatenate([hi, mid], 0)
        result = []
        for k in range(2):
            a = dot(left3, parts[k, 0])
            b = dot(left2, parts[k, 1])
            c = dot(hi, parts[k, 2])
            small = a[2 * rows :] + b[rows:] + c
            result.append(a[:rows] + ((a[rows : 2 * rows] + b[:rows]) + small))
        s, i = result
        return jnp.concatenate([s[:HALF] + i[HALF:], s[HALF:] - i[:HALF]], 0)

    norm = together(right * right)
    goal = norm * (TOLERANCE * TOLERANCE)
    x_ref[...] = jnp.zeros_like(right)
    r_ref[...] = right
    p_ref[...] = right

    def advance(state):
        done, _, rr = state
        for _ in range(2):
            p = p_ref[...]
            q = applied(p)
            pq = together(p * q)
            alpha = jnp.where(pq > 0.0, rr / pq, 0.0)
            x_ref[...] += alpha * p
            r = r_ref[...] - alpha * q
            r_ref[...] = r
            latest = together(r * r)
            p_ref[...] = r + jnp.where(rr > 0.0, latest / rr, 0.0) * p
            rr = latest
        return done + 2, jnp.max(jnp.where(rr <= goal, 0, 1)), rr

    def unfinished(state):
        done, left, _ = state
        return (left > 0) & (done < SOLVE_STEPS)

    _, left, _ = lax.while_loop(unfinished, advance, (0, jnp.max(jnp.where(norm <= goal, 0, 1)), norm))
    out_ref[...] = x_ref[...] * across

    @pl.when(left > 0)
    def _():
        work[0, :users, :] = re
        work[1, :users, :] = -im
        work[0, users:, :] = system_ref[users : users + HALF, :]
        work[1, users:, :] = system_ref[users + HALF :, :]
        lane = lax.broadcasted_iota(jnp.int32, (1, users), 1)

        def eliminate(j, carry):
            a, b = work[0], work[1]
            here = lane == j
            row_re = work[0, pl.ds(j, 1), :]
            row_im = work[1, pl.ds(j, 1), :]
            pivot = 1.0 / jnp.sum(jnp.where(here, row_re, 0.0), 1, keepdims=True)
            col_re = jnp.sum(jnp.where(here, a, 0.0), 1, keepdims=True) * pivot
            col_im = jnp.sum(jnp.where(here, b, 0.0), 1, keepdims=True) * pivot
            work[0] = jnp.where(here, col_re, a - (col_re * row_re - col_im * row_im))
            work[1] = jnp.where(here, col_im, b - (col_re * row_im + col_im * row_re))
            return carry

        lax.fori_loop(0, users, eliminate, 0)
        out_ref[:HALF, :] = work[0, users:, :]
        out_ref[HALF:, :] = work[1, users:, :]


def solved(systems, regularizer):
    _, rows, users = systems[0].shape
    f32 = jnp.float32
    vmem = pl.BlockSpec(memory_space=pltpu.VMEM)
    pair = pltpu.VMEM((2 * HALF, users), f32)
    return pl.pallas_call(
        solve_kernel,
        in_specs=[vmem] * (len(systems) + 1),
        out_specs=vmem,
        out_shape=jax.ShapeDtypeStruct((2 * HALF, users), f32),
        scratch_shapes=[
            pltpu.VMEM((rows, users), f32),
            pltpu.VMEM((2, 3, users, users), jnp.bfloat16),
            pair,
            pair,
            pair,
            pltpu.VMEM((2, users + HALF, users), f32),
        ],
        compiler_params=pltpu.CompilerParams(vmem_limit_bytes=12 << 20),
        name="solved",
    )(*[in_vmem(s) for s in systems], regularizer.reshape(1, users))


def received_rows(observed_signal):
    _, samples, tones, antennas, width = observed_signal.shape
    y = jnp.moveaxis(observed_signal, 2, 0).reshape(tones, 2, samples, antennas * width)
    re, im = y[:, 0], y[:, 1]
    gap = ((0, 0), (0, HALF - samples), (0, 0))
    top = jnp.pad(jnp.concatenate([re, im], 2), gap)
    bottom = jnp.pad(jnp.concatenate([im, -re], 2), gap)
    return jnp.concatenate([top, bottom], 1)


def ap_at(z, y, core):
    return (z * Y_CHIPS + y % Y_CHIPS) * CORES + core


def over_ap(value, dz, dy, dcore):
    spots = [(z, y, c) for z in range(Z_CHIPS) for y in range(Y_CHIPS) for c in range(CORES)]
    pairs = [(ap_at(z, y, c), ap_at(z ^ dz, y + dy, c ^ dcore)) for z, y, c in spots]
    return lax.ppermute(value, "ap", pairs)


def over_ap_by_core(value):
    spots = [(z, y, c) for z in range(Z_CHIPS) for y in range(Y_CHIPS) for c in range(CORES)]
    pairs = [(ap_at(z, y, c), ap_at(z, y + (1 if c == 0 else -1), c)) for z, y, c in spots]
    return lax.ppermute(value, "ap", pairs)


def over_sc(value, dz, dx):
    spots = [(z, x) for z in range(2) for x in range(X_CHIPS)]
    pairs = [(z * X_CHIPS + x, (z ^ dz) * X_CHIPS + (x + dx) % X_CHIPS) for z, x in spots]
    return lax.ppermute(value, "sc", pairs)


def over_sc_by_core(value):
    owners = Z_CHIPS * X_CHIPS
    pairs = []
    for ap in range(Z_CHIPS * Y_CHIPS * CORES):
        step = 1 if ap % CORES == 0 else -1
        for z in range(Z_CHIPS):
            for x in range(X_CHIPS):
                at = ap * owners + z * X_CHIPS
                pairs.append((at + x, at + (x + step) % X_CHIPS))
    return lax.ppermute(value, ("ap", "sc"), pairs)


def gathered_tables(own, core):
    across = over_sc(own, 1, 0)
    up, down = over_sc(own, 0, 1), over_sc(own, 0, -1)
    opposite = over_sc_by_core(jnp.where(core == 0, up, down))
    across_up, across_down = over_sc(across, 0, 1), over_sc(across, 0, -1)
    far = over_sc(opposite, 1, 0)
    return [own, across, up, down], [opposite, across_up, across_down, far]


def pack_kernel(*refs):
    *parts, out, sems = refs
    rows = out.shape[0] // len(parts)
    copies = [
        pltpu.make_async_copy(part, out.at[pl.ds(k * rows, rows)], sems.at[k]) for k, part in enumerate(parts)
    ]
    for copy in copies:
        copy.start()
    for copy in copies:
        copy.wait()


def packed_tables(parts):
    rows = sum(part.shape[0] for part in parts)
    vmem = pl.BlockSpec(memory_space=pltpu.VMEM)
    return pl.pallas_call(
        pack_kernel,
        in_specs=[pl.BlockSpec(memory_space=pltpu.HBM)] * len(parts),
        out_specs=vmem,
        out_shape=pltpu.VMEM((rows, *parts[0].shape[1:]), jnp.float32),
        scratch_shapes=[pltpu.SemaphoreType.DMA((len(parts),))],
        compiler_params=pltpu.CompilerParams(vmem_limit_bytes=4 << 20),
        name="packed_tables",
    )(*[pltpu.with_memory_space_constraint(p, pltpu.HBM) for p in parts])


def all_steps(observed_signal, delays, sines, path_gain_real, path_gain_imaginary, counts, regularizer):
    tones = observed_signal.shape[2]
    samples = observed_signal.shape[1]
    users = counts.shape[0]
    sc = lax.axis_index("sc")
    ap = lax.axis_index("ap")
    core = ap % CORES
    chip = ap // CORES
    place = jnp.stack([core, chip // Y_CHIPS, chip % Y_CHIPS, sc // X_CHIPS, sc % X_CHIPS]).astype(jnp.int32)
    first = (sc * tones).astype(jnp.float32)
    side = jnp.where(core == 0, -1.0, 1.0)
    centre = jnp.stack([(first + 0.5 * (tones - 1)) * (1.0 / FFT_LEN), side])
    own = packed_tables([delays, sines, path_gain_real, path_gain_imaginary])
    near, far = gathered_tables(own, core)
    state = prepared(place, centre, NEAR_SLOTS, near, counts)
    state = prepared(place, centre, FAR_SLOTS, far, counts, state)
    received = received_rows(observed_signal)

    def systems(distance, *after):
        where = jnp.stack([core, chip // Y_CHIPS, (chip + distance) % Y_CHIPS]).astype(jnp.int32)
        if after:
            where = lax.optimization_barrier((where, *after))[0]
        kept, sent = tone_systems(where, received, state)
        return kept, over_ap(sent, 0, 0, 1)

    def around(value, step):
        return over_ap(value, 0, step, 0)

    kept, other = systems(2)
    next_kept, next_other = systems(1, kept)
    farthest = kept + other
    passing = over_ap_by_core(farthest)
    last_kept, last_other = systems(3, farthest)
    upward = next_kept + next_other + jnp.where(core == 0, passing, 0.0)
    downward = last_kept + last_other + jnp.where(core == 0, 0.0, passing)
    up, down = around(upward, 1), around(downward, -1)
    kept, other = systems(0, upward, downward)
    mine = (kept + other) + (up + down)
    own_tone = solved([mine[:1], over_ap(mine[1:], 1, 0, 0)], regularizer)
    chips = lax.axis_size("ap") // CORES
    same = [[chip * CORES + c for chip in range(chips)] for c in range(CORES)]
    same_core = lax.all_to_all(
        jnp.broadcast_to(own_tone[None], (chips, *own_tone.shape)), "ap", 0, 0, tiled=True, axis_index_groups=same
    )
    other_core = over_ap(same_core, 0, 0, 1)
    first = jnp.where(core == 0, same_core, other_core)[::-1]
    second = jnp.where(core == 0, other_core, same_core)
    every = jnp.concatenate([first, second], 0).reshape(tones, 2, HALF, users)[:, :, :samples]
    return jnp.transpose(every, (1, 2, 0, 3))


def solution(mesh):
    placed = (
        P(None, None, "sc", None, "ap"),
        P(None, "sc", "ap"),
        P(None, "sc", "ap"),
        P(None, "sc", "ap"),
        P(None, "sc", "ap"),
        P(None, "ap"),
        P(),
    )
    return jax.shard_map(all_steps, mesh=mesh, in_specs=placed, out_specs=P(None, None, "sc", None), check_vma=False)
```

```python
import functools

import jax
import jax.numpy as jnp
import numpy as np
from jax import lax
from jax.experimental import pallas as pl
from jax.experimental.pallas import tpu as pltpu
from jax.sharding import PartitionSpec as P


CORES = 2
OWNERS = 8
NEAR_SLOTS = [((0, 0), 0, 0, 0, 8), ((1, 0), 1, 0, 1, 8), ((0, 1), 2, 0, 2, 8), ((0, 3), 3, 0, 3, 8)]
FAR_SLOTS = [((0, 2), 0, 0, 1, 0), ((1, 1), 2, 0, 2, 8), ((1, 3), 3, 0, 3, 8), ((1, 2), 4, 0, 5, 0)]
Y_CHIPS = 4
Z_CHIPS = 2
X_CHIPS = 4
ANTENNAS = 4
PATHS = 4
FFT_LEN = 512
FIT_POINTS = 4001
ROWS = 16
HALF = 16
SOLVE_STEPS = 60
TOLERANCE = 1e-6


def turn_fit():
    u = 0.25 * np.cos(np.pi * (np.arange(FIT_POINTS) + 0.5) / FIT_POINTS)
    cheb = np.polynomial.chebyshev.Chebyshev
    poly = np.polynomial.Polynomial
    x = u * u
    fits = []
    for values, degree in ((np.sin(2 * np.pi * u) / u, 4), (np.cos(2 * np.pi * u), 5)):
        fits.append([float(c) for c in cheb.fit(x, values, degree, domain=[0, 0.0625]).convert(kind=poly).coef])
    return fits


SIN_FIT, COS_FIT = turn_fit()


def horner(x, coefs):
    total = jnp.full_like(x, coefs[-1])
    for c in coefs[-2::-1]:
        total = total * x + c
    return total


def small_turn(u):
    x = u * u
    return horner(x, COS_FIT), u * horner(x, SIN_FIT)


def doubled(c, s):
    return 1.0 - 2.0 * (s * s), 2.0 * (s * c)


def times(a, b):
    return a[0] * b[0] - a[1] * b[1], a[0] * b[1] + a[1] * b[0]


NT = (((1,), (1,)), ((), ()))


def product(a, b):
    return lax.dot_general(a, b, NT, preferred_element_type=jnp.float32)


def prepare_kernel(slots, pieces, place_ref, tone_ref, *refs):
    tab_refs, count_ref = refs[:pieces], refs[pieces]
    lead, turn, four = refs[-3:]
    per_block = count_ref.shape[0] // OWNERS
    sc_z, sc_x = place_ref[3], place_ref[4]
    centre = tone_ref[0]
    side = tone_ref[1]

    def prepare(slot, block, carry):
        (across, along), angles, a_at, gains, g_at = slot
        angles, gains = tab_refs[angles], tab_refs[gains]
        owner = jnp.abs(sc_z - across) * X_CHIPS + (sc_x - along + X_CHIPS) % X_CHIPS
        inside = pl.ds(pl.multiple_of(block * ROWS, ROWS), ROWS)
        here = pl.ds(pl.multiple_of(owner * per_block + block * ROWS, ROWS), ROWS)
        count = count_ref[here, :]
        for p in range(PATHS):
            delay = angles[a_at + p, inside, :]
            sine = angles[a_at + PATHS + p, inside, :]
            alive = p < count
            re = jnp.where(alive, gains[g_at + p, inside, :], 0.0)
            im = jnp.where(alive, gains[g_at + PATHS + p, inside, :], 0.0)
            tones = small_turn(delay * (side * (0.5 / FFT_LEN)))
            one = doubled(*tones)
            for y in range(Y_CHIPS):
                turn[y, p, 0, here, :], turn[y, p, 1, here, :] = tones
                if y + 1 < Y_CHIPS:
                    tones = times(tones, one)
            four[p, 0, here, :], four[p, 1, here, :] = doubled(*doubled(*one))
            turns = delay * centre
            turns = turns - jnp.round(turns)
            c, s = doubled(*small_turn(0.5 * turns))
            z = times((re, im), (c, -s))
            steer = doubled(*small_turn(0.25 * sine))
            for n in range(ANTENNAS):
                lead[n, p, 0, here, :], lead[n, p, 1, here, :] = z
                if n + 1 < ANTENNAS:
                    z = times(z, steer)
        return carry

    for slot in slots:
        lax.fori_loop(0, per_block // ROWS, functools.partial(prepare, slot), 0)


def in_vmem(x):
    return pltpu.with_memory_space_constraint(x, pltpu.VMEM)


def prepared(place, centre, slots, tables, counts, state=None):
    users, width = counts.shape
    f32 = jnp.float32
    vmem = pl.BlockSpec(memory_space=pltpu.VMEM)
    smem = pl.BlockSpec(memory_space=pltpu.SMEM)
    state = () if state is None else state
    first = 3 + len(tables)
    return pl.pallas_call(
        functools.partial(prepare_kernel, slots, len(tables)),
        in_specs=[smem, smem] + [vmem] * (len(tables) + 1 + len(state)),
        out_specs=[vmem] * 3,
        out_shape=[
            pltpu.VMEM((ANTENNAS, PATHS, 2, users, width), f32),
            pltpu.VMEM((Y_CHIPS, PATHS, 2, users, width), f32),
            pltpu.VMEM((PATHS, 2, users, width), f32),
        ],
        input_output_aliases={first + k: k for k in range(len(state))},
        compiler_params=pltpu.CompilerParams(vmem_limit_bytes=4 << 20),
        name="prepared",
    )(place, centre, *[in_vmem(t) for t in tables], in_vmem(counts), *state)


def tone_kernel(place_ref, y_ref, lead, turn, four, kept_ref, sent_ref, re_a, im_a, lo_a, re_b, im_b, lo_b):
    users, width = four.shape[2:]
    blocks = users // ROWS
    half = ANTENNAS * width
    pairs = Y_CHIPS * Z_CHIPS
    core, chip_z, target_y = place_ref[0], place_ref[1], place_ref[2]

    def build(buffers, block, second):
        with_re, with_im, lo = buffers
        here = pl.ds(block * ROWS, ROWS)
        below = pl.ds(users + block * ROWS, ROWS)
        cs = [(turn[target_y, p, 0, here, :], turn[target_y, p, 1, here, :]) for p in range(PATHS)]
        if second:
            cs = [times(cs[p], (four[p, 0, here, :], four[p, 1, here, :])) for p in range(PATHS)]
        for n in range(ANTENNAS):
            sums = None
            for p in range(PATHS):
                c, s = cs[p]
                re, im = lead[n, p, 0, here, :], lead[n, p, 1, here, :]
                products = (re * c, im * s, im * c, re * s)
                sums = products if sums is None else tuple(a + b for a, b in zip(sums, products))
            a, b, c, d = sums
            columns = slice(n * width, (n + 1) * width)
            for tone, (re, im) in enumerate(((a - b, c + d), (a + b, c - d))):
                for part, (value, top, bottom) in enumerate(((re, with_re, with_im), (im, with_im, with_re))):
                    packed = value.astype(jnp.bfloat16)
                    top[tone, here, columns] = packed
                    bottom[tone, below, columns] = packed
                    rest = (value - packed.astype(jnp.float32)).astype(jnp.bfloat16)
                    lo[tone, here, slice(part * half + n * width, part * half + (n + 1) * width)] = rest

    def multiply(buffers, z):
        with_re, with_im, lo = buffers
        pair = z * Y_CHIPS + target_y
        slot = jnp.abs(z - chip_z)
        plus, minus = pairs + pair, pairs - 1 - pair
        first = jnp.where(core == 0, plus, minus)
        for tone, (at, out_ref) in enumerate(((first, sent_ref), (plus + minus - first, kept_ref))):
            y = y_ref[at]
            y_hi = y.astype(jnp.bfloat16)
            y_lo = (y - y_hi.astype(jnp.float32)).astype(jnp.bfloat16)
            for part, ref in enumerate((with_re, with_im)):
                ref[tone, 2 * users : 2 * users + 2 * HALF] = y_hi[:, part * half : (part + 1) * half]
                ref[tone, 2 * users + 2 * HALF :] = y_lo[:, part * half : (part + 1) * half]
            by_re = product(with_re[tone], with_re[tone, :users])
            by_im = product(with_im[tone], with_im[tone, :users])
            plain, crossed = by_re[:users] + by_im[:users], by_im[users : 2 * users] - by_re[users : 2 * users]
            out_ref[slot, :users, :] = plain + crossed
            filtered = by_re[2 * users :] + by_im[2 * users :]
            rest = product(y_hi, lo[tone])
            out_ref[slot, users:, :] = filtered[: 2 * HALF] + (filtered[2 * HALF :] + rest)

    even, odd = (re_a, im_a, lo_a), (re_b, im_b, lo_b)

    def alone(block, carry):
        build(even, block, False)
        return carry

    lax.fori_loop(0, blocks, alone, 0, unroll=2)
    multiply(even, 0)
    for block in range(blocks):
        build(odd, block, True)
    multiply(odd, 1)


def tone_systems(place, received, state):
    users, _ = state[2].shape[2:]
    wide = received.shape[2]
    f32, bf16 = jnp.float32, jnp.bfloat16
    vmem = pl.BlockSpec(memory_space=pltpu.VMEM)
    smem = pl.BlockSpec(memory_space=pltpu.SMEM)
    channel = pltpu.VMEM((2, 2 * users + 4 * HALF, wide // 2), bf16)
    rest = pltpu.VMEM((2, users, wide), bf16)
    return pl.pallas_call(
        tone_kernel,
        in_specs=[smem] + [vmem] * (1 + len(state)),
        out_specs=[vmem, vmem],
        out_shape=[pltpu.VMEM((Z_CHIPS, users + 2 * HALF, users), f32)] * 2,
        scratch_shapes=[channel, channel, rest] * 2,
        compiler_params=pltpu.CompilerParams(vmem_limit_bytes=16 << 20),
        name="tone_systems",
    )(place, in_vmem(received), *state)


def three_parts(x):
    hi = x.astype(jnp.bfloat16)
    rest = x - hi.astype(jnp.float32)
    mid = rest.astype(jnp.bfloat16)
    return hi, mid, (rest - mid.astype(jnp.float32)).astype(jnp.bfloat16)


def solve_kernel(*refs):
    *part_refs, regularizer_ref, out_ref, system_ref, parts, x_ref, r_ref, p_ref, work = refs
    system_ref[...] = sum(ref[0] for ref in part_refs)
    users = regularizer_ref.shape[1]
    f32 = jnp.float32
    g = system_ref[:users, :]
    flipped = g.T
    row = lax.broadcasted_iota(jnp.int32, (users, users), 0)
    column = lax.broadcasted_iota(jnp.int32, (users, users), 1)
    eye = row == column
    re = 0.5 * (g + flipped)
    im = 0.5 * (g - flipped)
    re = jnp.where(eye, re + regularizer_ref[...], re)
    diagonal = jnp.where(eye, re, 0.0)
    across = lax.rsqrt(jnp.sum(diagonal, 0, keepdims=True))
    down = lax.rsqrt(jnp.sum(diagonal, 1, keepdims=True))
    for k, matrix in enumerate((re, im)):
        for at, part in enumerate(three_parts(matrix * across * down)):
            parts[k, at] = part
    right = system_ref[users:, :] * across

    def together(v):
        total = jnp.sum(v[:HALF] + v[HALF:], 1, keepdims=True)
        return jnp.concatenate([total, total], 0)

    def dot(a, b):
        return jnp.dot(a, b, preferred_element_type=f32)

    rows = 2 * HALF

    def applied(p):
        hi, mid, low = three_parts(p)
        left3 = jnp.concatenate([hi, mid, low], 0)
        left2 = jnp.concatenate([hi, mid], 0)
        result = []
        for k in range(2):
            a = dot(left3, parts[k, 0])
            b = dot(left2, parts[k, 1])
            c = dot(hi, parts[k, 2])
            small = a[2 * rows :] + b[rows:] + c
            result.append(a[:rows] + ((a[rows : 2 * rows] + b[:rows]) + small))
        s, i = result
        return jnp.concatenate([s[:HALF] + i[HALF:], s[HALF:] - i[:HALF]], 0)

    norm = together(right * right)
    goal = norm * (TOLERANCE * TOLERANCE)
    x_ref[...] = jnp.zeros_like(right)
    r_ref[...] = right
    p_ref[...] = right

    def advance(state):
        done, _, rr = state
        for _ in range(2):
            p = p_ref[...]
            q = applied(p)
            pq = together(p * q)
            alpha = jnp.where(pq > 0.0, rr / pq, 0.0)
            x_ref[...] += alpha * p
            r = r_ref[...] - alpha * q
            r_ref[...] = r
            latest = together(r * r)
            p_ref[...] = r + jnp.where(rr > 0.0, latest / rr, 0.0) * p
            rr = latest
        return done + 2, jnp.max(jnp.where(rr <= goal, 0, 1)), rr

    def unfinished(state):
        done, left, _ = state
        return (left > 0) & (done < SOLVE_STEPS)

    _, left, _ = lax.while_loop(unfinished, advance, (0, jnp.max(jnp.where(norm <= goal, 0, 1)), norm))
    out_ref[...] = x_ref[...] * across

    @pl.when(left > 0)
    def _():
        work[0, :users, :] = re
        work[1, :users, :] = -im
        work[0, users:, :] = system_ref[users : users + HALF, :]
        work[1, users:, :] = system_ref[users + HALF :, :]
        lane = lax.broadcasted_iota(jnp.int32, (1, users), 1)

        def eliminate(j, carry):
            a, b = work[0], work[1]
            here = lane == j
            row_re = work[0, pl.ds(j, 1), :]
            row_im = work[1, pl.ds(j, 1), :]
            pivot = 1.0 / jnp.sum(jnp.where(here, row_re, 0.0), 1, keepdims=True)
            col_re = jnp.sum(jnp.where(here, a, 0.0), 1, keepdims=True) * pivot
            col_im = jnp.sum(jnp.where(here, b, 0.0), 1, keepdims=True) * pivot
            work[0] = jnp.where(here, col_re, a - (col_re * row_re - col_im * row_im))
            work[1] = jnp.where(here, col_im, b - (col_re * row_im + col_im * row_re))
            return carry

        lax.fori_loop(0, users, eliminate, 0)
        out_ref[:HALF, :] = work[0, users:, :]
        out_ref[HALF:, :] = work[1, users:, :]


def solved(systems, regularizer):
    _, rows, users = systems[0].shape
    f32 = jnp.float32
    vmem = pl.BlockSpec(memory_space=pltpu.VMEM)
    pair = pltpu.VMEM((2 * HALF, users), f32)
    return pl.pallas_call(
        solve_kernel,
        in_specs=[vmem] * (len(systems) + 1),
        out_specs=vmem,
        out_shape=jax.ShapeDtypeStruct((2 * HALF, users), f32),
        scratch_shapes=[
            pltpu.VMEM((rows, users), f32),
            pltpu.VMEM((2, 3, users, users), jnp.bfloat16),
            pair,
            pair,
            pair,
            pltpu.VMEM((2, users + HALF, users), f32),
        ],
        compiler_params=pltpu.CompilerParams(vmem_limit_bytes=12 << 20),
        name="solved",
    )(*[in_vmem(s) for s in systems], regularizer.reshape(1, users))


def received_rows(observed_signal):
    _, samples, tones, antennas, width = observed_signal.shape
    y = jnp.moveaxis(observed_signal, 2, 0).reshape(tones, 2, samples, antennas * width)
    re, im = y[:, 0], y[:, 1]
    gap = ((0, 0), (0, HALF - samples), (0, 0))
    top = jnp.pad(jnp.concatenate([re, im], 2), gap)
    bottom = jnp.pad(jnp.concatenate([im, -re], 2), gap)
    return jnp.concatenate([top, bottom], 1)


def ap_at(z, y, core):
    return (z * Y_CHIPS + y % Y_CHIPS) * CORES + core


def over_ap(value, dz, dy, dcore):
    spots = [(z, y, c) for z in range(Z_CHIPS) for y in range(Y_CHIPS) for c in range(CORES)]
    pairs = [(ap_at(z, y, c), ap_at(z ^ dz, y + dy, c ^ dcore)) for z, y, c in spots]
    return lax.ppermute(value, "ap", pairs)


def over_sc(value, dz, dx):
    spots = [(z, x) for z in range(2) for x in range(X_CHIPS)]
    pairs = [(z * X_CHIPS + x, (z ^ dz) * X_CHIPS + (x + dx) % X_CHIPS) for z, x in spots]
    return lax.ppermute(value, "sc", pairs)


def gathered_tables(own):
    half = own.shape[0] // 2
    across = over_sc(own, 1, 0)
    up, down = over_sc(own, 0, 1), over_sc(own, 0, -1)
    up_twice, down_twice = over_sc(up[:half], 0, 1), over_sc(down[half:], 0, -1)
    across_up, across_down = over_sc(across, 0, 1), over_sc(across, 0, -1)
    far = over_sc(up_twice, 1, 0), over_sc(down_twice, 1, 0)
    return [own, across, up, down], [up_twice, down_twice, across_up, across_down, *far]


def pack_kernel(*refs):
    *parts, out, sems = refs
    rows = out.shape[0] // len(parts)
    copies = [
        pltpu.make_async_copy(part, out.at[pl.ds(k * rows, rows)], sems.at[k]) for k, part in enumerate(parts)
    ]
    for copy in copies:
        copy.start()
    for copy in copies:
        copy.wait()


def packed_tables(parts):
    rows = sum(part.shape[0] for part in parts)
    vmem = pl.BlockSpec(memory_space=pltpu.VMEM)
    return pl.pallas_call(
        pack_kernel,
        in_specs=[pl.BlockSpec(memory_space=pltpu.HBM)] * len(parts),
        out_specs=vmem,
        out_shape=pltpu.VMEM((rows, *parts[0].shape[1:]), jnp.float32),
        scratch_shapes=[pltpu.SemaphoreType.DMA((len(parts),))],
        compiler_params=pltpu.CompilerParams(vmem_limit_bytes=4 << 20),
        name="packed_tables",
    )(*[pltpu.with_memory_space_constraint(p, pltpu.HBM) for p in parts])


def all_steps(observed_signal, delays, sines, path_gain_real, path_gain_imaginary, counts, regularizer):
    tones = observed_signal.shape[2]
    samples = observed_signal.shape[1]
    users = counts.shape[0]
    sc = lax.axis_index("sc")
    ap = lax.axis_index("ap")
    core = ap % CORES
    chip = ap // CORES
    place = jnp.stack([core, chip // Y_CHIPS, chip % Y_CHIPS, sc // X_CHIPS, sc % X_CHIPS]).astype(jnp.int32)
    first = (sc * tones).astype(jnp.float32)
    side = jnp.where(core == 0, -1.0, 1.0)
    centre = jnp.stack([(first + 0.5 * (tones - 1)) * (1.0 / FFT_LEN), side])
    own = packed_tables([delays, sines, path_gain_real, path_gain_imaginary])
    near, far = gathered_tables(own)
    state = prepared(place, centre, NEAR_SLOTS, near, counts)
    state = prepared(place, centre, FAR_SLOTS, far, counts, state)
    received = received_rows(observed_signal)
    rows = users + 2 * HALF
    top = rows // 2

    def systems(distance, *after):
        where = jnp.stack([core, chip // Y_CHIPS, (chip + distance) % Y_CHIPS]).astype(jnp.int32)
        if after:
            where = lax.optimization_barrier((where, *after))[0]
        kept, sent = tone_systems(where, received, state)
        return kept, over_ap(sent, 0, 0, 1)

    def around(value, step):
        return over_ap(value, 0, step, 0)

    kept, other = systems(2)
    next_kept, next_other = systems(1, kept)
    farthest = kept + other
    up, down = around(farthest[:, :top], 1), around(farthest[:, top:], -1)
    last_kept, last_other = systems(3, farthest)
    upward = next_kept + next_other
    upward = jnp.concatenate([upward[:, :top] + up, upward[:, top:]], 1)
    downward = last_kept + last_other
    downward = jnp.concatenate([downward[:, :top], downward[:, top:] + down], 1)
    up, down = around(upward[1:], 1), around(downward[1:], -1)
    kept, other = systems(0, upward, downward)
    upward, downward, kept = lax.optimization_barrier((upward[:1], downward[:1], kept))
    own_up, own_down = around(upward, 1), around(downward, -1)
    across = kept[1:] + other[1:] + (up + down)
    across = over_ap(across, 1, 0, 0)
    own_tone = solved([kept[:1], other[:1], own_up, own_down, across], regularizer)
    chips = lax.axis_size("ap") // CORES
    same = [[chip * CORES + c for chip in range(chips)] for c in range(CORES)]
    same_core = lax.all_to_all(
        jnp.broadcast_to(own_tone[None], (chips, *own_tone.shape)), "ap", 0, 0, tiled=True, axis_index_groups=same
    )
    other_core = over_ap(same_core, 0, 0, 1)
    first = jnp.where(core == 0, same_core, other_core)[::-1]
    second = jnp.where(core == 0, other_core, same_core)
    every = jnp.concatenate([first, second], 0).reshape(tones, 2, HALF, users)[:, :, :samples]
    return jnp.transpose(every, (1, 2, 0, 3))


def solution(mesh):
    placed = (
        P(None, None, "sc", None, "ap"),
        P(None, "sc", "ap"),
        P(None, "sc", "ap"),
        P(None, "sc", "ap"),
        P(None, "sc", "ap"),
        P(None, "ap"),
        P(),
    )
    return jax.shard_map(all_steps, mesh=mesh, in_specs=placed, out_specs=P(None, None, "sc", None), check_vma=False)
```

```python
import functools

import jax
import jax.numpy as jnp
import numpy as np
from jax import lax
from jax.experimental import pallas as pl
from jax.experimental.pallas import tpu as pltpu
from jax.sharding import PartitionSpec as P


CORES = 2
OWNERS = 8
NEAR_SLOTS = [((0, 0), 0, 0, 0, 8), ((1, 0), 1, 0, 1, 8), ((0, 1), 2, 0, 2, 8), ((0, 3), 3, 0, 3, 8)]
FAR_SLOTS = [((0, 2), 0, 0, 0, 8), ((1, 1), 1, 0, 1, 8), ((1, 3), 2, 0, 2, 8), ((1, 2), 3, 0, 3, 8)]
Y_CHIPS = 4
Z_CHIPS = 2
X_CHIPS = 4
ANTENNAS = 4
PATHS = 4
FFT_LEN = 512
FIT_POINTS = 4001
ROWS = 16
HALF = 16
SOLVE_STEPS = 60
TOLERANCE = 1e-6


def turn_fit():
    u = 0.25 * np.cos(np.pi * (np.arange(FIT_POINTS) + 0.5) / FIT_POINTS)
    cheb = np.polynomial.chebyshev.Chebyshev
    poly = np.polynomial.Polynomial
    x = u * u
    fits = []
    for values, degree in ((np.sin(2 * np.pi * u) / u, 4), (np.cos(2 * np.pi * u), 5)):
        fits.append([float(c) for c in cheb.fit(x, values, degree, domain=[0, 0.0625]).convert(kind=poly).coef])
    return fits


SIN_FIT, COS_FIT = turn_fit()


def horner(x, coefs):
    total = jnp.full_like(x, coefs[-1])
    for c in coefs[-2::-1]:
        total = total * x + c
    return total


def small_turn(u):
    x = u * u
    return horner(x, COS_FIT), u * horner(x, SIN_FIT)


def doubled(c, s):
    return 1.0 - 2.0 * (s * s), 2.0 * (s * c)


def times(a, b):
    return a[0] * b[0] - a[1] * b[1], a[0] * b[1] + a[1] * b[0]


NT = (((1,), (1,)), ((), ()))


def product(a, b):
    return lax.dot_general(a, b, NT, preferred_element_type=jnp.float32)


def prepare_kernel(slots, pieces, tones, *refs):
    tab_refs, count_ref = refs[:pieces], refs[pieces]
    lead, turn = refs[-2:]
    per_block = count_ref.shape[0] // OWNERS
    sc = lax.axis_index("sc")
    sc_z, sc_x = sc // X_CHIPS, sc % X_CHIPS
    centre = ((sc * tones).astype(jnp.float32) + 0.5 * (tones - 1)) * (1.0 / FFT_LEN)
    side = jnp.where(lax.axis_index("ap") % CORES == 0, -1.0, 1.0)

    def prepare(slot, block, carry):
        (across, along), angles, a_at, gains, g_at = slot
        angles, gains = tab_refs[angles], tab_refs[gains]
        owner = jnp.abs(sc_z - across) * X_CHIPS + (sc_x - along + X_CHIPS) % X_CHIPS
        inside = pl.ds(pl.multiple_of(block * ROWS, ROWS), ROWS)
        here = pl.ds(pl.multiple_of(owner * per_block + block * ROWS, ROWS), ROWS)
        count = count_ref[here, :]
        for p in range(PATHS):
            delay = angles[a_at + p, inside, :]
            sine = angles[a_at + PATHS + p, inside, :]
            alive = p < count
            re = jnp.where(alive, gains[g_at + p, inside, :], 0.0)
            im = jnp.where(alive, gains[g_at + PATHS + p, inside, :], 0.0)
            angle = small_turn(delay * (side * (0.5 / FFT_LEN)))
            one = doubled(*angle)
            for pair in range(tones // 2):
                turn[pair, p, 0, here, :], turn[pair, p, 1, here, :] = angle
                if pair + 1 < tones // 2:
                    angle = times(angle, one)
            turns = delay * centre
            turns = turns - jnp.round(turns)
            c, s = doubled(*small_turn(0.5 * turns))
            z = times((re, im), (c, -s))
            steer = doubled(*small_turn(0.25 * sine))
            for n in range(ANTENNAS):
                lead[n, p, 0, here, :], lead[n, p, 1, here, :] = z
                if n + 1 < ANTENNAS:
                    z = times(z, steer)
        return carry

    for slot in slots:
        lax.fori_loop(0, per_block // ROWS, functools.partial(prepare, slot), 0)


def in_vmem(x):
    return pltpu.with_memory_space_constraint(x, pltpu.VMEM)


def prepared(tones, slots, tables, counts, state=()):
    users, width = counts.shape
    f32 = jnp.float32
    vmem = pl.BlockSpec(memory_space=pltpu.VMEM)
    first = len(tables) + 1
    return pl.pallas_call(
        functools.partial(prepare_kernel, slots, len(tables), tones),
        in_specs=[vmem] * (first + len(state)),
        out_specs=[vmem] * 2,
        out_shape=[
            pltpu.VMEM((ANTENNAS, PATHS, 2, users, width), f32),
            pltpu.VMEM((tones // 2, PATHS, 2, users, width), f32),
        ],
        input_output_aliases={first + k: k for k in range(len(state))},
        compiler_params=pltpu.CompilerParams(vmem_limit_bytes=4 << 20),
        name="prepared",
    )(*[in_vmem(t) for t in tables], in_vmem(counts), *state)


def tone_kernel(distance, planes, y_ref, lead, turn, kept_ref, sent_ref, *buffers):
    users, width = lead.shape[3:]
    blocks = users // ROWS
    half = ANTENNAS * width
    pairs = Y_CHIPS * Z_CHIPS
    ap = lax.axis_index("ap")
    core, chip = ap % CORES, ap // CORES
    chip_z, target_y = chip // Y_CHIPS, (chip + distance) % Y_CHIPS

    def pair_of(plane):
        return jnp.abs(chip_z - plane) * Y_CHIPS + target_y

    def build(buffers, block, plane):
        pair = pair_of(plane)
        with_re, with_im, lo = buffers
        here = pl.ds(block * ROWS, ROWS)
        below = pl.ds(users + block * ROWS, ROWS)
        cs = [(turn[pair, p, 0, here, :], turn[pair, p, 1, here, :]) for p in range(PATHS)]
        for n in range(ANTENNAS):
            sums = None
            for p in range(PATHS):
                c, s = cs[p]
                re, im = lead[n, p, 0, here, :], lead[n, p, 1, here, :]
                products = (re * c, im * s, im * c, re * s)
                sums = products if sums is None else tuple(a + b for a, b in zip(sums, products))
            a, b, c, d = sums
            columns = slice(n * width, (n + 1) * width)
            for tone, (re, im) in enumerate(((a - b, c + d), (a + b, c - d))):
                for part, (value, top, bottom) in enumerate(((re, with_re, with_im), (im, with_im, with_re))):
                    packed = value.astype(jnp.bfloat16)
                    top[tone, here, columns] = packed
                    bottom[tone, below, columns] = packed
                    rest = (value - packed.astype(jnp.float32)).astype(jnp.bfloat16)
                    lo[tone, here, slice(part * half + n * width, part * half + (n + 1) * width)] = rest

    def multiply(buffers, plane, slot):
        with_re, with_im, lo = buffers
        pair = pair_of(plane)
        plus, minus = pairs + pair, pairs - 1 - pair
        first = jnp.where(core == 0, plus, minus)
        for tone, (at, out_ref) in enumerate(((first, sent_ref), (plus + minus - first, kept_ref))):
            y = y_ref[at]
            y_hi = y.astype(jnp.bfloat16)
            y_lo = (y - y_hi.astype(jnp.float32)).astype(jnp.bfloat16)
            for part, ref in enumerate((with_re, with_im)):
                ref[tone, 2 * users : 2 * users + 2 * HALF] = y_hi[:, part * half : (part + 1) * half]
                ref[tone, 2 * users + 2 * HALF :] = y_lo[:, part * half : (part + 1) * half]
            by_re = product(with_re[tone], with_re[tone, :users])
            by_im = product(with_im[tone], with_im[tone, :users])
            plain, crossed = by_re[:users] + by_im[:users], by_im[users : 2 * users] - by_re[users : 2 * users]
            out_ref[slot, :users, :] = plain + crossed
            filtered = by_re[2 * users :] + by_im[2 * users :]
            rest = product(y_hi, lo[tone])
            out_ref[slot, users:, :] = filtered[: 2 * HALF] + (filtered[2 * HALF :] + rest)

    sides = [buffers[3 * k : 3 * k + 3] for k in range(len(planes))]

    def alone(block, carry):
        build(sides[0], block, planes[0])
        return carry

    lax.fori_loop(0, blocks, alone, 0, unroll=2)
    for slot, plane in enumerate(planes):
        multiply(sides[slot], plane, slot)
        if slot + 1 < len(planes):
            for block in range(blocks):
                build(sides[slot + 1], block, planes[slot + 1])


def tone_systems(distance, planes, received, state):
    users, _ = state[0].shape[3:]
    wide = received.shape[2]
    f32, bf16 = jnp.float32, jnp.bfloat16
    vmem = pl.BlockSpec(memory_space=pltpu.VMEM)
    channel = pltpu.VMEM((2, 2 * users + 4 * HALF, wide // 2), bf16)
    rest = pltpu.VMEM((2, users, wide), bf16)
    return pl.pallas_call(
        functools.partial(tone_kernel, distance, planes),
        in_specs=[vmem] * (1 + len(state)),
        out_specs=[vmem, vmem],
        out_shape=[pltpu.VMEM((len(planes), users + 2 * HALF, users), f32)] * 2,
        scratch_shapes=[channel, channel, rest] * len(planes),
        compiler_params=pltpu.CompilerParams(vmem_limit_bytes=16 << 20),
        name="tone_systems",
    )(in_vmem(received), *state)


def three_parts(x):
    hi = x.astype(jnp.bfloat16)
    rest = x - hi.astype(jnp.float32)
    mid = rest.astype(jnp.bfloat16)
    return hi, mid, (rest - mid.astype(jnp.float32)).astype(jnp.bfloat16)


def solve_kernel(*refs):
    *part_refs, regularizer_ref, out_ref, system_ref, parts, x_ref, r_ref, p_ref, work = refs
    system_ref[...] = sum(ref[0] for ref in part_refs)
    users = regularizer_ref.shape[1]
    f32 = jnp.float32
    g = system_ref[:users, :]
    flipped = g.T
    row = lax.broadcasted_iota(jnp.int32, (users, users), 0)
    column = lax.broadcasted_iota(jnp.int32, (users, users), 1)
    eye = row == column
    re = 0.5 * (g + flipped)
    im = 0.5 * (g - flipped)
    re = jnp.where(eye, re + regularizer_ref[...], re)
    diagonal = jnp.where(eye, re, 0.0)
    across = lax.rsqrt(jnp.sum(diagonal, 0, keepdims=True))
    down = lax.rsqrt(jnp.sum(diagonal, 1, keepdims=True))
    for k, matrix in enumerate((re, im)):
        for at, part in enumerate(three_parts(matrix * across * down)):
            parts[k, at] = part
    right = system_ref[users:, :] * across

    def together(v):
        total = jnp.sum(v[:HALF] + v[HALF:], 1, keepdims=True)
        return jnp.concatenate([total, total], 0)

    def dot(a, b):
        return jnp.dot(a, b, preferred_element_type=f32)

    rows = 2 * HALF

    def applied(p):
        hi, mid, low = three_parts(p)
        left3 = jnp.concatenate([hi, mid, low], 0)
        left2 = jnp.concatenate([hi, mid], 0)
        result = []
        for k in range(2):
            a = dot(left3, parts[k, 0])
            b = dot(left2, parts[k, 1])
            c = dot(hi, parts[k, 2])
            small = a[2 * rows :] + b[rows:] + c
            result.append(a[:rows] + ((a[rows : 2 * rows] + b[:rows]) + small))
        s, i = result
        return jnp.concatenate([s[:HALF] + i[HALF:], s[HALF:] - i[:HALF]], 0)

    norm = together(right * right)
    goal = norm * (TOLERANCE * TOLERANCE)
    x_ref[...] = jnp.zeros_like(right)
    r_ref[...] = right
    p_ref[...] = right

    def advance(state):
        done, _, rr = state
        for _ in range(2):
            p = p_ref[...]
            q = applied(p)
            pq = together(p * q)
            alpha = jnp.where(pq > 0.0, rr / pq, 0.0)
            x_ref[...] += alpha * p
            r = r_ref[...] - alpha * q
            r_ref[...] = r
            latest = together(r * r)
            p_ref[...] = r + jnp.where(rr > 0.0, latest / rr, 0.0) * p
            rr = latest
        return done + 2, jnp.max(jnp.where(rr <= goal, 0, 1)), rr

    def unfinished(state):
        done, left, _ = state
        return (left > 0) & (done < SOLVE_STEPS)

    _, left, _ = lax.while_loop(unfinished, advance, (0, jnp.max(jnp.where(norm <= goal, 0, 1)), norm))
    out_ref[...] = x_ref[...] * across

    @pl.when(left > 0)
    def _():
        work[0, :users, :] = re
        work[1, :users, :] = -im
        work[0, users:, :] = system_ref[users : users + HALF, :]
        work[1, users:, :] = system_ref[users + HALF :, :]
        lane = lax.broadcasted_iota(jnp.int32, (1, users), 1)

        def eliminate(j, carry):
            a, b = work[0], work[1]
            here = lane == j
            row_re = work[0, pl.ds(j, 1), :]
            row_im = work[1, pl.ds(j, 1), :]
            pivot = 1.0 / jnp.sum(jnp.where(here, row_re, 0.0), 1, keepdims=True)
            col_re = jnp.sum(jnp.where(here, a, 0.0), 1, keepdims=True) * pivot
            col_im = jnp.sum(jnp.where(here, b, 0.0), 1, keepdims=True) * pivot
            work[0] = jnp.where(here, col_re, a - (col_re * row_re - col_im * row_im))
            work[1] = jnp.where(here, col_im, b - (col_re * row_im + col_im * row_re))
            return carry

        lax.fori_loop(0, users, eliminate, 0)
        out_ref[:HALF, :] = work[0, users:, :]
        out_ref[HALF:, :] = work[1, users:, :]


def solved(systems, regularizer):
    _, rows, users = systems[0].shape
    f32 = jnp.float32
    vmem = pl.BlockSpec(memory_space=pltpu.VMEM)
    pair = pltpu.VMEM((2 * HALF, users), f32)
    return pl.pallas_call(
        solve_kernel,
        in_specs=[vmem] * (len(systems) + 1),
        out_specs=vmem,
        out_shape=jax.ShapeDtypeStruct((2 * HALF, users), f32),
        scratch_shapes=[
            pltpu.VMEM((rows, users), f32),
            pltpu.VMEM((2, 3, users, users), jnp.bfloat16),
            pair,
            pair,
            pair,
            pltpu.VMEM((2, users + HALF, users), f32),
        ],
        compiler_params=pltpu.CompilerParams(vmem_limit_bytes=12 << 20),
        name="solved",
    )(*[in_vmem(s) for s in systems], regularizer.reshape(1, users))


def received_rows(observed_signal):
    _, samples, tones, antennas, width = observed_signal.shape
    y = jnp.moveaxis(observed_signal, 2, 0).reshape(tones, 2, samples, antennas * width)
    re, im = y[:, 0], y[:, 1]
    gap = ((0, 0), (0, HALF - samples), (0, 0))
    top = jnp.pad(jnp.concatenate([re, im], 2), gap)
    bottom = jnp.pad(jnp.concatenate([im, -re], 2), gap)
    return jnp.concatenate([top, bottom], 1)


def ap_at(z, y, core):
    return (z * Y_CHIPS + y % Y_CHIPS) * CORES + core


def over_ap(value, dz, dy, dcore):
    spots = [(z, y, c) for z in range(Z_CHIPS) for y in range(Y_CHIPS) for c in range(CORES)]
    pairs = [(ap_at(z, y, c), ap_at(z ^ dz, y + dy, c ^ dcore)) for z, y, c in spots]
    return lax.ppermute(value, "ap", pairs)


def over_sc(value, dz, dx):
    spots = [(z, x) for z in range(2) for x in range(X_CHIPS)]
    pairs = [(z * X_CHIPS + x, (z ^ dz) * X_CHIPS + (x + dx) % X_CHIPS) for z, x in spots]
    return lax.ppermute(value, "sc", pairs)


def gathered_tables(own):
    half = own.shape[0] // 2
    across = over_sc(own, 1, 0)
    up, down = over_sc(own, 0, 1), over_sc(own, 0, -1)
    up_twice, down_twice = over_sc(up[:half], 0, 1), over_sc(down[half:], 0, -1)
    across_up, across_down = over_sc(across, 0, 1), over_sc(across, 0, -1)
    opposite = jnp.concatenate([up_twice, down_twice], 0)
    return [own, across, up, down], [opposite, across_up, across_down, over_sc(opposite, 1, 0)]


def pack_kernel(*refs):
    *parts, out, sems = refs
    rows = out.shape[0] // len(parts)
    copies = [
        pltpu.make_async_copy(part, out.at[pl.ds(k * rows, rows)], sems.at[k]) for k, part in enumerate(parts)
    ]
    for copy in copies:
        copy.start()
    for copy in copies:
        copy.wait()


def packed_tables(parts):
    rows = sum(part.shape[0] for part in parts)
    vmem = pl.BlockSpec(memory_space=pltpu.VMEM)
    return pl.pallas_call(
        pack_kernel,
        in_specs=[pl.BlockSpec(memory_space=pltpu.HBM)] * len(parts),
        out_specs=vmem,
        out_shape=pltpu.VMEM((rows, *parts[0].shape[1:]), jnp.float32),
        scratch_shapes=[pltpu.SemaphoreType.DMA((len(parts),))],
        compiler_params=pltpu.CompilerParams(vmem_limit_bytes=4 << 20),
        name="packed_tables",
    )(*[pltpu.with_memory_space_constraint(p, pltpu.HBM) for p in parts])


def all_steps(observed_signal, delays, sines, path_gain_real, path_gain_imaginary, counts, regularizer):
    tones = observed_signal.shape[2]
    samples = observed_signal.shape[1]
    users = counts.shape[0]
    core = lax.axis_index("ap") % CORES
    own = packed_tables([delays, sines, path_gain_real, path_gain_imaginary])
    near, far = gathered_tables(own)
    state = prepared(tones, NEAR_SLOTS, near, counts)
    state = prepared(tones, FAR_SLOTS, far, counts, state)
    received = received_rows(observed_signal)
    rows = users + 2 * HALF
    top = rows // 2

    def systems(distance, planes, *after):
        y = lax.optimization_barrier((received, *after))[0] if after else received
        kept, sent = tone_systems(distance, planes, y, state)
        return kept, over_ap(sent, 0, 0, 1)

    def around(value, step):
        return over_ap(value, 0, step, 0)

    def joined(pieces, passed, at):
        total = pieces[0] + pieces[1]
        if at == 0:
            return jnp.concatenate([total[:, :top] + passed, total[:, top:]], 1)
        return jnp.concatenate([total[:, :top], total[:, top:] + passed], 1)

    kept, other = systems(2, (0, 1))
    up_far = systems(1, (1,), kept)
    farthest = kept + other
    up, down = around(farthest[:, :top], 1), around(farthest[:, top:], -1)
    up_own = systems(1, (0,), farthest, up_far[0])
    kept, other = systems(3, (0, 1), up_own[0])
    up_far, up_own = joined(up_far, up[1:], 0), joined(up_own, up[:1], 0)
    down_far, down_own = joined((kept[1:], other[1:]), down[1:], 1), joined((kept[:1], other[:1]), down[:1], 1)
    up, down = around(up_far, 1), around(down_far, -1)
    kept, other = systems(0, (1,), up_far, down_far)
    up_own, down_own, kept = lax.optimization_barrier((up_own, down_own, kept))
    own_up, own_down = around(up_own, 1), around(down_own, -1)
    across = (kept + other) + (up + down)
    kept, other = systems(0, (0,), across)
    across = over_ap(across, 1, 0, 0)
    own_tone = solved([kept, other, own_up, own_down, across], regularizer)
    chips = lax.axis_size("ap") // CORES
    same = [[chip * CORES + c for chip in range(chips)] for c in range(CORES)]
    same_core = lax.all_to_all(
        jnp.broadcast_to(own_tone[None], (chips, *own_tone.shape)), "ap", 0, 0, tiled=True, axis_index_groups=same
    )
    other_core = over_ap(same_core, 0, 0, 1)
    first = jnp.where(core == 0, same_core, other_core)[::-1]
    second = jnp.where(core == 0, other_core, same_core)
    every = jnp.concatenate([first, second], 0).reshape(tones, 2, HALF, users)[:, :, :samples]
    return jnp.transpose(every, (1, 2, 0, 3))


def solution(mesh):
    placed = (
        P(None, None, "sc", None, "ap"),
        P(None, "sc", "ap"),
        P(None, "sc", "ap"),
        P(None, "sc", "ap"),
        P(None, "sc", "ap"),
        P(None, "ap"),
        P(),
    )
    return jax.shard_map(all_steps, mesh=mesh, in_specs=placed, out_specs=P(None, None, "sc", None), check_vma=False)
```

```python
import functools

import jax
import jax.numpy as jnp
import numpy as np
from jax import lax
from jax.experimental import pallas as pl
from jax.experimental.pallas import tpu as pltpu
from jax.sharding import PartitionSpec as P


CORES = 2
OWNERS = 8
NEAR_SLOTS = [((0, 0), 0, 0, 0, 8), ((1, 0), 1, 0, 1, 8), ((0, 1), 2, 0, 2, 8), ((0, 3), 3, 0, 3, 8)]
FAR_SLOTS = [((0, 2), 0, 0, 0, 8), ((1, 1), 1, 0, 1, 8), ((1, 3), 2, 0, 2, 8), ((1, 2), 3, 0, 3, 8)]
Y_CHIPS = 4
Z_CHIPS = 2
X_CHIPS = 4
ANTENNAS = 4
PATHS = 4
FFT_LEN = 512
FIT_POINTS = 4001
ROWS = 16
HALF = 16
SOLVE_STEPS = 40
TOLERANCE = 1e-6


def turn_fit():
    u = 0.25 * np.cos(np.pi * (np.arange(FIT_POINTS) + 0.5) / FIT_POINTS)
    cheb = np.polynomial.chebyshev.Chebyshev
    poly = np.polynomial.Polynomial
    x = u * u
    fits = []
    for values, degree in ((np.sin(2 * np.pi * u) / u, 4), (np.cos(2 * np.pi * u), 5)):
        fits.append([float(c) for c in cheb.fit(x, values, degree, domain=[0, 0.0625]).convert(kind=poly).coef])
    return fits


SIN_FIT, COS_FIT = turn_fit()


def horner(x, coefs):
    total = jnp.full_like(x, coefs[-1])
    for c in coefs[-2::-1]:
        total = total * x + c
    return total


def small_turn(u):
    x = u * u
    return horner(x, COS_FIT), u * horner(x, SIN_FIT)


def doubled(c, s):
    return 1.0 - 2.0 * (s * s), 2.0 * (s * c)


def times(a, b):
    return a[0] * b[0] - a[1] * b[1], a[0] * b[1] + a[1] * b[0]


NT = (((1,), (1,)), ((), ()))


def product(a, b):
    return lax.dot_general(a, b, NT, preferred_element_type=jnp.float32)


def prepare_kernel(slots, pieces, tones, *refs):
    tab_refs, count_ref = refs[:pieces], refs[pieces]
    lead, turn = refs[-2:]
    per_block = count_ref.shape[0] // OWNERS
    sc = lax.axis_index("sc")
    sc_z, sc_x = sc // X_CHIPS, sc % X_CHIPS
    centre = ((sc * tones).astype(jnp.float32) + 0.5 * (tones - 1)) * (1.0 / FFT_LEN)
    side = jnp.where(lax.axis_index("ap") % CORES == 0, -1.0, 1.0)

    def prepare(slot, block, carry):
        (across, along), angles, a_at, gains, g_at = slot
        angles, gains = tab_refs[angles], tab_refs[gains]
        owner = jnp.abs(sc_z - across) * X_CHIPS + (sc_x - along + X_CHIPS) % X_CHIPS
        inside = pl.ds(pl.multiple_of(block * ROWS, ROWS), ROWS)
        here = pl.ds(pl.multiple_of(owner * per_block + block * ROWS, ROWS), ROWS)
        count = count_ref[here, :]
        for p in range(PATHS):
            delay = angles[a_at + p, inside, :]
            sine = angles[a_at + PATHS + p, inside, :]
            alive = p < count
            re = jnp.where(alive, gains[g_at + p, inside, :], 0.0)
            im = jnp.where(alive, gains[g_at + PATHS + p, inside, :], 0.0)
            angle = small_turn(delay * (side * (0.5 / FFT_LEN)))
            one = doubled(*angle)
            for pair in range(tones // 2):
                turn[pair, p, 0, here, :], turn[pair, p, 1, here, :] = angle
                if pair + 1 < tones // 2:
                    angle = times(angle, one)
            turns = delay * centre
            turns = turns - jnp.round(turns)
            c, s = doubled(*small_turn(0.5 * turns))
            z = times((re, im), (c, -s))
            steer = doubled(*small_turn(0.25 * sine))
            for n in range(ANTENNAS):
                lead[n, p, 0, here, :], lead[n, p, 1, here, :] = z
                if n + 1 < ANTENNAS:
                    z = times(z, steer)
        return carry

    for slot in slots:
        lax.fori_loop(0, per_block // ROWS, functools.partial(prepare, slot), 0)


def in_vmem(x):
    return pltpu.with_memory_space_constraint(x, pltpu.VMEM)


def prepared(tones, slots, tables, counts, state=()):
    users, width = counts.shape
    f32 = jnp.float32
    vmem = pl.BlockSpec(memory_space=pltpu.VMEM)
    first = len(tables) + 1
    return pl.pallas_call(
        functools.partial(prepare_kernel, slots, len(tables), tones),
        in_specs=[vmem] * (first + len(state)),
        out_specs=[vmem] * 2,
        out_shape=[
            pltpu.VMEM((ANTENNAS, PATHS, 2, users, width), f32),
            pltpu.VMEM((tones // 2, PATHS, 2, users, width), f32),
        ],
        input_output_aliases={first + k: k for k in range(len(state))},
        compiler_params=pltpu.CompilerParams(vmem_limit_bytes=4 << 20),
        name="prepared",
    )(*[in_vmem(t) for t in tables], in_vmem(counts), *state)


def tone_kernel(distance, planes, y_ref, lead, turn, kept_ref, sent_ref, *buffers):
    users, width = lead.shape[3:]
    blocks = users // ROWS
    half = ANTENNAS * width
    pairs = Y_CHIPS * Z_CHIPS
    ap = lax.axis_index("ap")
    core, chip = ap % CORES, ap // CORES
    chip_z, target_y = chip // Y_CHIPS, (chip + distance) % Y_CHIPS

    def pair_of(plane):
        return jnp.abs(chip_z - plane) * Y_CHIPS + target_y

    def build(buffers, block, plane):
        pair = pair_of(plane)
        with_re, with_im, lo = buffers
        here = pl.ds(block * ROWS, ROWS)
        below = pl.ds(users + block * ROWS, ROWS)
        cs = [(turn[pair, p, 0, here, :], turn[pair, p, 1, here, :]) for p in range(PATHS)]
        for n in range(ANTENNAS):
            sums = None
            for p in range(PATHS):
                c, s = cs[p]
                re, im = lead[n, p, 0, here, :], lead[n, p, 1, here, :]
                products = (re * c, im * s, im * c, re * s)
                sums = products if sums is None else tuple(a + b for a, b in zip(sums, products))
            a, b, c, d = sums
            columns = slice(n * width, (n + 1) * width)
            for tone, (re, im) in enumerate(((a - b, c + d), (a + b, c - d))):
                for part, (value, ref) in enumerate(((re, with_re), (im, with_im))):
                    packed = value.astype(jnp.bfloat16)
                    ref[tone, here, columns] = packed
                    if part == 0:
                        with_im[tone, below, columns] = packed
                    rest = (value - packed.astype(jnp.float32)).astype(jnp.bfloat16)
                    lo[tone, here, slice(part * half + n * width, part * half + (n + 1) * width)] = rest

    def multiply(buffers, plane, slot):
        with_re, with_im, lo = buffers
        pair = pair_of(plane)
        plus, minus = pairs + pair, pairs - 1 - pair
        first = jnp.where(core == 0, plus, minus)
        for tone, (at, out_ref) in enumerate(((first, sent_ref), (plus + minus - first, kept_ref))):
            y = y_ref[at]
            y_hi = y.astype(jnp.bfloat16)
            y_lo = (y - y_hi.astype(jnp.float32)).astype(jnp.bfloat16)
            for part, ref in enumerate((with_re, with_im)):
                end = ref.shape[1]
                ref[tone, end - 4 * HALF : end - 2 * HALF] = y_hi[:, part * half : (part + 1) * half]
                ref[tone, end - 2 * HALF :] = y_lo[:, part * half : (part + 1) * half]
            by_re = product(with_re[tone], with_re[tone, :users])
            by_im = product(with_im[tone], with_im[tone, :users])
            crossed = by_im[users : 2 * users]
            out_ref[slot, :users, :] = (by_re[:users] + by_im[:users]) + (crossed - crossed.T)
            filtered = by_re[users:] + by_im[2 * users :]
            rest = product(y_hi, lo[tone])
            out_ref[slot, users:, :] = filtered[: 2 * HALF] + (filtered[2 * HALF :] + rest)

    sides = [buffers[3 * k : 3 * k + 3] for k in range(len(planes))]

    def alone(block, carry):
        build(sides[0], block, planes[0])
        return carry

    lax.fori_loop(0, blocks, alone, 0, unroll=2)
    for slot, plane in enumerate(planes):
        multiply(sides[slot], plane, slot)
        if slot + 1 < len(planes):
            for block in range(blocks):
                build(sides[slot + 1], block, planes[slot + 1])


def tone_systems(distance, planes, received, state):
    users, _ = state[0].shape[3:]
    wide = received.shape[2]
    f32, bf16 = jnp.float32, jnp.bfloat16
    vmem = pl.BlockSpec(memory_space=pltpu.VMEM)
    channel_re = pltpu.VMEM((2, users + 4 * HALF, wide // 2), bf16)
    channel_im = pltpu.VMEM((2, 2 * users + 4 * HALF, wide // 2), bf16)
    rest = pltpu.VMEM((2, users, wide), bf16)
    return pl.pallas_call(
        functools.partial(tone_kernel, distance, planes),
        in_specs=[vmem] * (1 + len(state)),
        out_specs=[vmem, vmem],
        out_shape=[pltpu.VMEM((len(planes), users + 2 * HALF, users), f32)] * 2,
        scratch_shapes=[channel_re, channel_im, rest] * len(planes),
        compiler_params=pltpu.CompilerParams(vmem_limit_bytes=16 << 20),
        name="tone_systems",
    )(in_vmem(received), *state)


def three_parts(x):
    hi = x.astype(jnp.bfloat16)
    rest = x - hi.astype(jnp.float32)
    mid = rest.astype(jnp.bfloat16)
    return hi, mid, (rest - mid.astype(jnp.float32)).astype(jnp.bfloat16)


def solve_kernel(*refs):
    *part_refs, regularizer_ref, out_ref, system_ref, parts, x_ref, r_ref, p_ref, q_ref, work = refs
    system_ref[...] = sum(ref[0] for ref in part_refs)
    users = regularizer_ref.shape[1]
    f32 = jnp.float32
    g = system_ref[:users, :]
    flipped = g.T
    row = lax.broadcasted_iota(jnp.int32, (users, users), 0)
    column = lax.broadcasted_iota(jnp.int32, (users, users), 1)
    eye = row == column
    re = 0.5 * (g + flipped)
    im = 0.5 * (g - flipped)
    re = jnp.where(eye, re + regularizer_ref[...], re)
    diagonal = jnp.where(eye, re, 0.0)
    across = lax.rsqrt(jnp.sum(diagonal, 0, keepdims=True))
    down = lax.rsqrt(jnp.sum(diagonal, 1, keepdims=True))
    for k, matrix in enumerate((re, im)):
        for at, part in enumerate(three_parts(matrix * across * down)):
            parts[k, at] = part
    right = system_ref[users:, :] * across

    def together(v):
        total = jnp.sum(v[:HALF] + v[HALF:], 1, keepdims=True)
        return jnp.concatenate([total, total], 0)

    def dot(a, b):
        return jnp.dot(a, b, preferred_element_type=f32)

    rows = 2 * HALF

    def applied(p):
        hi, mid, low = three_parts(p)
        left3 = jnp.concatenate([hi, mid, low], 0)
        left2 = jnp.concatenate([hi, mid], 0)
        result = []
        for k in range(2):
            a = dot(left3, parts[k, 0])
            b = dot(left2, parts[k, 1])
            c = dot(hi, parts[k, 2])
            small = a[2 * rows :] + b[rows:] + c
            result.append(a[:rows] + ((a[rows : 2 * rows] + b[:rows]) + small))
        s, i = result
        return jnp.concatenate([s[:HALF] + i[HALF:], s[HALF:] - i[:HALF]], 0)

    norm = together(right * right)
    goal = norm * (TOLERANCE * TOLERANCE)
    nothing = jnp.zeros_like(right)
    x_ref[...], p_ref[...], q_ref[...] = nothing, nothing, nothing
    r_ref[...] = right

    def advance(state):
        done, _, earlier, alpha = state
        for _ in range(2):
            r = r_ref[...]
            applied_r = applied(r)
            rr = together(r * r)
            curvature = together(r * applied_r)
            beta = jnp.where(earlier > 0.0, rr / earlier, 0.0)
            curvature = curvature - jnp.where(alpha > 0.0, beta * rr / alpha, 0.0)
            alpha = jnp.where(curvature > 0.0, rr / curvature, 0.0)
            p = r + beta * p_ref[...]
            q = applied_r + beta * q_ref[...]
            p_ref[...], q_ref[...] = p, q
            x_ref[...] += alpha * p
            r_ref[...] = r - alpha * q
            earlier = rr
        r = r_ref[...]
        return done + 2, jnp.max(jnp.where(together(r * r) <= goal, 0, 1)), earlier, alpha

    def unfinished(state):
        return (state[1] > 0) & (state[0] < SOLVE_STEPS)

    zero = jnp.zeros_like(norm)
    _, left, _, _ = lax.while_loop(unfinished, advance, (0, jnp.max(jnp.where(norm <= goal, 0, 1)), zero, zero))
    out_ref[...] = x_ref[...] * across

    @pl.when(left > 0)
    def _():
        work[0, :users, :] = re
        work[1, :users, :] = -im
        work[0, users:, :] = system_ref[users : users + HALF, :]
        work[1, users:, :] = system_ref[users + HALF :, :]
        lane = lax.broadcasted_iota(jnp.int32, (1, users), 1)

        def eliminate(j, carry):
            a, b = work[0], work[1]
            here = lane == j
            row_re = work[0, pl.ds(j, 1), :]
            row_im = work[1, pl.ds(j, 1), :]
            pivot = 1.0 / jnp.sum(jnp.where(here, row_re, 0.0), 1, keepdims=True)
            col_re = jnp.sum(jnp.where(here, a, 0.0), 1, keepdims=True) * pivot
            col_im = jnp.sum(jnp.where(here, b, 0.0), 1, keepdims=True) * pivot
            work[0] = jnp.where(here, col_re, a - (col_re * row_re - col_im * row_im))
            work[1] = jnp.where(here, col_im, b - (col_re * row_im + col_im * row_re))
            return carry

        lax.fori_loop(0, users, eliminate, 0)
        out_ref[:HALF, :] = work[0, users:, :]
        out_ref[HALF:, :] = work[1, users:, :]


def solved(systems, regularizer):
    _, rows, users = systems[0].shape
    f32 = jnp.float32
    vmem = pl.BlockSpec(memory_space=pltpu.VMEM)
    pair = pltpu.VMEM((2 * HALF, users), f32)
    return pl.pallas_call(
        solve_kernel,
        in_specs=[vmem] * (len(systems) + 1),
        out_specs=vmem,
        out_shape=jax.ShapeDtypeStruct((2 * HALF, users), f32),
        scratch_shapes=[
            pltpu.VMEM((rows, users), f32),
            pltpu.VMEM((2, 3, users, users), jnp.bfloat16),
            pair,
            pair,
            pair,
            pair,
            pltpu.VMEM((2, users + HALF, users), f32),
        ],
        compiler_params=pltpu.CompilerParams(vmem_limit_bytes=12 << 20),
        name="solved",
    )(*[in_vmem(s) for s in systems], regularizer.reshape(1, users))


def received_rows(observed_signal):
    _, samples, tones, antennas, width = observed_signal.shape
    y = jnp.moveaxis(observed_signal, 2, 0).reshape(tones, 2, samples, antennas * width)
    re, im = y[:, 0], y[:, 1]
    gap = ((0, 0), (0, HALF - samples), (0, 0))
    top = jnp.pad(jnp.concatenate([re, im], 2), gap)
    bottom = jnp.pad(jnp.concatenate([im, -re], 2), gap)
    return jnp.concatenate([top, bottom], 1)


def ap_at(z, y, core):
    return (z * Y_CHIPS + y % Y_CHIPS) * CORES + core


def over_ap(value, dz, dy, dcore):
    spots = [(z, y, c) for z in range(Z_CHIPS) for y in range(Y_CHIPS) for c in range(CORES)]
    pairs = [(ap_at(z, y, c), ap_at(z ^ dz, y + dy, c ^ dcore)) for z, y, c in spots]
    return lax.ppermute(value, "ap", pairs)


def over_sc(value, dz, dx):
    spots = [(z, x) for z in range(2) for x in range(X_CHIPS)]
    pairs = [(z * X_CHIPS + x, (z ^ dz) * X_CHIPS + (x + dx) % X_CHIPS) for z, x in spots]
    return lax.ppermute(value, "sc", pairs)


def gathered_tables(own):
    half = own.shape[0] // 2

    across = over_sc(own, 1, 0)
    up, down = over_sc(own, 0, 1), over_sc(own, 0, -1)
    up_twice, down_twice = over_sc(up[:half], 0, 1), over_sc(down[half:], 0, -1)
    across_up, across_down = over_sc(across, 0, 1), over_sc(across, 0, -1)
    opposite = jnp.concatenate([up_twice, down_twice], 0)
    return [own, across, up, down], [opposite, across_up, across_down, over_sc(opposite, 1, 0)]


def pack_kernel(*refs):
    *parts, out, sems = refs
    rows = out.shape[0] // len(parts)
    copies = [
        pltpu.make_async_copy(part, out.at[pl.ds(k * rows, rows)], sems.at[k]) for k, part in enumerate(parts)
    ]
    for copy in copies:
        copy.start()
    for copy in copies:
        copy.wait()


def packed_tables(parts):
    rows = sum(part.shape[0] for part in parts)
    vmem = pl.BlockSpec(memory_space=pltpu.VMEM)
    return pl.pallas_call(
        pack_kernel,
        in_specs=[pl.BlockSpec(memory_space=pltpu.HBM)] * len(parts),
        out_specs=vmem,
        out_shape=pltpu.VMEM((rows, *parts[0].shape[1:]), jnp.float32),
        scratch_shapes=[pltpu.SemaphoreType.DMA((len(parts),))],
        compiler_params=pltpu.CompilerParams(vmem_limit_bytes=4 << 20),
        name="packed_tables",
    )(*[pltpu.with_memory_space_constraint(p, pltpu.HBM) for p in parts])


def all_steps(observed_signal, delays, sines, path_gain_real, path_gain_imaginary, counts, regularizer):
    tones = observed_signal.shape[2]
    samples = observed_signal.shape[1]
    users = counts.shape[0]
    core = lax.axis_index("ap") % CORES
    own = packed_tables([delays, sines, path_gain_real, path_gain_imaginary])
    near, far = gathered_tables(own)
    state = prepared(tones, NEAR_SLOTS, near, counts)
    state = prepared(tones, FAR_SLOTS, far, counts, state)
    received = received_rows(observed_signal)
    rows = users + 2 * HALF
    top = rows // 2

    def systems(distance, planes, *after):
        y = lax.optimization_barrier((received, *after))[0] if after else received
        kept, sent = tone_systems(distance, planes, y, state)
        return kept, over_ap(sent, 0, 0, 1)

    def around(value, step):
        return over_ap(value, 0, step, 0)

    def joined(pieces, passed, at):
        total = pieces[0] + pieces[1]
        if at == 0:
            return jnp.concatenate([total[:, :top] + passed, total[:, top:]], 1)
        return jnp.concatenate([total[:, :top], total[:, top:] + passed], 1)

    kept, other = systems(2, (0, 1))
    up_far = systems(1, (1,), kept)
    farthest = kept + other
    up, down = around(farthest[:, :top], 1), around(farthest[:, top:], -1)
    up_own = systems(1, (0,), farthest, up_far[0])
    kept, other = systems(3, (0, 1), up_own[0])
    last_kept, last_other = systems(0, (1,), kept)
    up_far, up_own = joined(up_far, up[1:], 0), joined(up_own, up[:1], 0)
    down_far, down_own = joined((kept[1:], other[1:]), down[1:], 1), joined((kept[:1], other[:1]), down[:1], 1)
    up, down = around(up_far, 1), around(down_far, -1)
    own_up, own_down = around(up_own, 1), around(down_own, -1)
    across = (last_kept + last_other) + (up + down)
    kept, other = systems(0, (0,), across)
    across = over_ap(across, 1, 0, 0)
    own_tone = solved([kept, other, own_up, own_down, across], regularizer)
    chips = lax.axis_size("ap") // CORES
    same = [[chip * CORES + c for chip in range(chips)] for c in range(CORES)]
    same_core = lax.all_to_all(
        jnp.broadcast_to(own_tone[None], (chips, *own_tone.shape)), "ap", 0, 0, tiled=True, axis_index_groups=same
    )
    other_core = over_ap(same_core, 0, 0, 1)
    first = jnp.where(core == 0, same_core, other_core)[::-1]
    second = jnp.where(core == 0, other_core, same_core)
    every = jnp.concatenate([first, second], 0).reshape(tones, 2, HALF, users)[:, :, :samples]
    return jnp.transpose(every, (1, 2, 0, 3))


def solution(mesh):
    placed = (
        P(None, None, "sc", None, "ap"),
        P(None, "sc", "ap"),
        P(None, "sc", "ap"),
        P(None, "sc", "ap"),
        P(None, "sc", "ap"),
        P(None, "ap"),
        P(),
    )
    return jax.shard_map(all_steps, mesh=mesh, in_specs=placed, out_specs=P(None, None, "sc", None), check_vma=False)
```

```python
import functools

import jax
import jax.numpy as jnp
import numpy as np
from jax import lax
from jax.experimental import pallas as pl
from jax.experimental.pallas import tpu as pltpu
from jax.sharding import PartitionSpec as P


CORES = 2
OWNERS = 8
NEAR_SLOTS = [((0, 0), 0, 0, 0, 8), ((1, 0), 1, 0, 1, 8), ((0, 1), 2, 0, 2, 8), ((0, 3), 3, 0, 3, 8)]
FAR_SLOTS = [((0, 2), 0, 0, 0, 8), ((1, 1), 1, 0, 1, 8), ((1, 3), 2, 0, 2, 8), ((1, 2), 3, 0, 3, 8)]
Y_CHIPS = 4
Z_CHIPS = 2
X_CHIPS = 4
ANTENNAS = 4
PATHS = 4
FFT_LEN = 512
FIT_POINTS = 4001
ROWS = 16
HALF = 16
SOLVE_STEPS = 40
TOLERANCE = 1e-6


def turn_fit():
    u = 0.25 * np.cos(np.pi * (np.arange(FIT_POINTS) + 0.5) / FIT_POINTS)
    cheb = np.polynomial.chebyshev.Chebyshev
    poly = np.polynomial.Polynomial
    x = u * u
    fits = []
    for values, degree in ((np.sin(2 * np.pi * u) / u, 4), (np.cos(2 * np.pi * u), 5)):
        fits.append([float(c) for c in cheb.fit(x, values, degree, domain=[0, 0.0625]).convert(kind=poly).coef])
    return fits


SIN_FIT, COS_FIT = turn_fit()


def horner(x, coefs):
    total = jnp.full_like(x, coefs[-1])
    for c in coefs[-2::-1]:
        total = total * x + c
    return total


def small_turn(u):
    x = u * u
    return horner(x, COS_FIT), u * horner(x, SIN_FIT)


def doubled(c, s):
    return 1.0 - 2.0 * (s * s), 2.0 * (s * c)


def times(a, b):
    return a[0] * b[0] - a[1] * b[1], a[0] * b[1] + a[1] * b[0]


NT = (((1,), (1,)), ((), ()))


def product(a, b):
    return lax.dot_general(a, b, NT, preferred_element_type=jnp.float32)


def prepare_kernel(slots, pieces, tones, *refs):
    tab_refs, count_ref = refs[:pieces], refs[pieces]
    lead, turn = refs[-2:]
    per_block = count_ref.shape[0] // OWNERS
    sc = lax.axis_index("sc")
    sc_z, sc_x = sc // X_CHIPS, sc % X_CHIPS
    centre = ((sc * tones).astype(jnp.float32) + 0.5 * (tones - 1)) * (1.0 / FFT_LEN)
    side = jnp.where(lax.axis_index("ap") % CORES == 0, -1.0, 1.0)

    def prepare(slot, block, carry):
        (across, along), angles, a_at, gains, g_at = slot
        angles, gains = tab_refs[angles], tab_refs[gains]
        owner = jnp.abs(sc_z - across) * X_CHIPS + (sc_x - along + X_CHIPS) % X_CHIPS
        inside = pl.ds(pl.multiple_of(block * ROWS, ROWS), ROWS)
        here = pl.ds(pl.multiple_of(owner * per_block + block * ROWS, ROWS), ROWS)
        count = count_ref[here, :]
        for p in range(PATHS):
            delay = angles[a_at + p, inside, :]
            sine = angles[a_at + PATHS + p, inside, :]
            alive = p < count
            re = jnp.where(alive, gains[g_at + p, inside, :], 0.0)
            im = jnp.where(alive, gains[g_at + PATHS + p, inside, :], 0.0)
            angle = small_turn(delay * (side * (0.5 / FFT_LEN)))
            one = doubled(*angle)
            for pair in range(tones // 2):
                turn[pair, p, 0, here, :], turn[pair, p, 1, here, :] = angle
                if pair + 1 < tones // 2:
                    angle = times(angle, one)
            turns = delay * centre
            turns = turns - jnp.round(turns)
            c, s = doubled(*small_turn(0.5 * turns))
            z = times((re, im), (c, -s))
            steer = doubled(*small_turn(0.25 * sine))
            for n in range(ANTENNAS):
                lead[n, p, 0, here, :], lead[n, p, 1, here, :] = z
                if n + 1 < ANTENNAS:
                    z = times(z, steer)
        return carry

    for slot in slots:
        lax.fori_loop(0, per_block // ROWS, functools.partial(prepare, slot), 0)


def in_vmem(x):
    return pltpu.with_memory_space_constraint(x, pltpu.VMEM)


def prepared(tones, slots, tables, counts, state=()):
    users, width = counts.shape
    f32 = jnp.float32
    vmem = pl.BlockSpec(memory_space=pltpu.VMEM)
    first = len(tables) + 1
    return pl.pallas_call(
        functools.partial(prepare_kernel, slots, len(tables), tones),
        in_specs=[vmem] * (first + len(state)),
        out_specs=[vmem] * 2,
        out_shape=[
            pltpu.VMEM((ANTENNAS, PATHS, 2, users, width), f32),
            pltpu.VMEM((tones // 2, PATHS, 2, users, width), f32),
        ],
        input_output_aliases={first + k: k for k in range(len(state))},
        compiler_params=pltpu.CompilerParams(vmem_limit_bytes=4 << 20),
        name="prepared",
    )(*[in_vmem(t) for t in tables], in_vmem(counts), *state)


def tone_kernel(distance, planes, y_ref, lead, turn, kept_ref, sent_ref, *buffers):
    users, width = lead.shape[3:]
    blocks = users // ROWS
    half = ANTENNAS * width
    pairs = Y_CHIPS * Z_CHIPS
    ap = lax.axis_index("ap")
    core, chip = ap % CORES, ap // CORES
    chip_z, target_y = chip // Y_CHIPS, (chip + distance) % Y_CHIPS

    def pair_of(plane):
        return jnp.abs(chip_z - plane) * Y_CHIPS + target_y

    def build(buffers, block, plane):
        pair = pair_of(plane)
        with_re, with_im, lo = buffers
        here = pl.ds(block * ROWS, ROWS)
        below = pl.ds(users + block * ROWS, ROWS)
        cs = [(turn[pair, p, 0, here, :], turn[pair, p, 1, here, :]) for p in range(PATHS)]
        for n in range(ANTENNAS):
            sums = None
            for p in range(PATHS):
                c, s = cs[p]
                re, im = lead[n, p, 0, here, :], lead[n, p, 1, here, :]
                products = (re * c, im * s, im * c, re * s)
                sums = products if sums is None else tuple(a + b for a, b in zip(sums, products))
            a, b, c, d = sums
            columns = slice(n * width, (n + 1) * width)
            for tone, (re, im) in enumerate(((a - b, c + d), (a + b, c - d))):
                for part, (value, ref) in enumerate(((re, with_re), (im, with_im))):
                    packed = value.astype(jnp.bfloat16)
                    ref[tone, here, columns] = packed
                    if part == 0:
                        with_im[tone, below, columns] = packed
                    rest = (value - packed.astype(jnp.float32)).astype(jnp.bfloat16)
                    lo[tone, here, slice(part * half + n * width, part * half + (n + 1) * width)] = rest

    def multiply(buffers, plane, slot):
        with_re, with_im, lo = buffers
        pair = pair_of(plane)
        plus, minus = pairs + pair, pairs - 1 - pair
        first = jnp.where(core == 0, plus, minus)
        for tone, (at, out_ref) in enumerate(((first, sent_ref), (plus + minus - first, kept_ref))):
            y = y_ref[at]
            y_hi = y.astype(jnp.bfloat16)
            y_lo = (y - y_hi.astype(jnp.float32)).astype(jnp.bfloat16)
            for part, ref in enumerate((with_re, with_im)):
                end = ref.shape[1]
                ref[tone, end - 4 * HALF : end - 2 * HALF] = y_hi[:, part * half : (part + 1) * half]
                ref[tone, end - 2 * HALF :] = y_lo[:, part * half : (part + 1) * half]
            by_re = product(with_re[tone], with_re[tone, :users])
            by_im = product(with_im[tone], with_im[tone, :users])
            crossed = by_im[users : 2 * users]
            out_ref[slot, :users, :] = (by_re[:users] + by_im[:users]) + (crossed - crossed.T)
            filtered = by_re[users:] + by_im[2 * users :]
            rest = product(y_hi, lo[tone])
            out_ref[slot, users:, :] = filtered[: 2 * HALF] + (filtered[2 * HALF :] + rest)

    sides = [buffers[3 * k : 3 * k + 3] for k in range(len(planes))]

    def alone(block, carry):
        build(sides[0], block, planes[0])
        return carry

    lax.fori_loop(0, blocks, alone, 0, unroll=2)
    for slot, plane in enumerate(planes):
        multiply(sides[slot], plane, slot)
        if slot + 1 < len(planes):
            for block in range(blocks):
                build(sides[slot + 1], block, planes[slot + 1])


def tone_systems(distance, planes, received, state):
    users, _ = state[0].shape[3:]
    wide = received.shape[2]
    f32, bf16 = jnp.float32, jnp.bfloat16
    vmem = pl.BlockSpec(memory_space=pltpu.VMEM)
    channel_re = pltpu.VMEM((2, users + 4 * HALF, wide // 2), bf16)
    channel_im = pltpu.VMEM((2, 2 * users + 4 * HALF, wide // 2), bf16)
    rest = pltpu.VMEM((2, users, wide), bf16)
    return pl.pallas_call(
        functools.partial(tone_kernel, distance, planes),
        in_specs=[vmem] * (1 + len(state)),
        out_specs=[vmem, vmem],
        out_shape=[pltpu.VMEM((len(planes), users + 2 * HALF, users), f32)] * 2,
        scratch_shapes=[channel_re, channel_im, rest] * len(planes),
        compiler_params=pltpu.CompilerParams(vmem_limit_bytes=16 << 20),
        name="tone_systems",
    )(in_vmem(received), *state)


def three_parts(x):
    hi = x.astype(jnp.bfloat16)
    rest = x - hi.astype(jnp.float32)
    mid = rest.astype(jnp.bfloat16)
    return hi, mid, (rest - mid.astype(jnp.float32)).astype(jnp.bfloat16)


def solve_kernel(*refs):
    *part_refs, regularizer_ref, out_ref, system_ref, parts, x_ref, r_ref, p_ref, q_ref, work = refs
    system_ref[...] = sum(ref[0] for ref in part_refs)
    users = regularizer_ref.shape[1]
    f32 = jnp.float32
    g = system_ref[:users, :]
    flipped = g.T
    row = lax.broadcasted_iota(jnp.int32, (users, users), 0)
    column = lax.broadcasted_iota(jnp.int32, (users, users), 1)
    eye = row == column
    re = 0.5 * (g + flipped)
    im = 0.5 * (g - flipped)
    re = jnp.where(eye, re + regularizer_ref[...], re)
    diagonal = jnp.where(eye, re, 0.0)
    across = lax.rsqrt(jnp.sum(diagonal, 0, keepdims=True))
    down = lax.rsqrt(jnp.sum(diagonal, 1, keepdims=True))
    for k, matrix in enumerate((re, im)):
        for at, part in enumerate(three_parts(matrix * across * down)):
            parts[k, at] = part
    right = system_ref[users:, :] * across

    def together(v):
        total = jnp.sum(v[:HALF] + v[HALF:], 1, keepdims=True)
        return jnp.concatenate([total, total], 0)

    def dot(a, b):
        return jnp.dot(a, b, preferred_element_type=f32)

    rows = 2 * HALF

    def applied(p):
        hi, mid, low = three_parts(p)
        left3 = jnp.concatenate([hi, mid, low], 0)
        left2 = jnp.concatenate([hi, mid], 0)
        result = []
        for k in range(2):
            a = dot(left3, parts[k, 0])
            b = dot(left2, parts[k, 1])
            c = dot(hi, parts[k, 2])
            small = a[2 * rows :] + b[rows:] + c
            result.append(a[:rows] + ((a[rows : 2 * rows] + b[:rows]) + small))
        s, i = result
        return jnp.concatenate([s[:HALF] + i[HALF:], s[HALF:] - i[:HALF]], 0)

    norm = together(right * right)
    goal = norm * (TOLERANCE * TOLERANCE)
    nothing = jnp.zeros_like(right)
    x_ref[...], p_ref[...], q_ref[...] = nothing, nothing, nothing
    r_ref[...] = right

    def advance(state):
        done, _, earlier, alpha = state
        for _ in range(2):
            r = r_ref[...]
            applied_r = applied(r)
            rr = together(r * r)
            curvature = together(r * applied_r)
            beta = jnp.where(earlier > 0.0, rr / earlier, 0.0)
            curvature = curvature - jnp.where(alpha > 0.0, beta * rr / alpha, 0.0)
            alpha = jnp.where(curvature > 0.0, rr / curvature, 0.0)
            p = r + beta * p_ref[...]
            q = applied_r + beta * q_ref[...]
            p_ref[...], q_ref[...] = p, q
            x_ref[...] += alpha * p
            r_ref[...] = r - alpha * q
            earlier = rr
        r = r_ref[...]
        return done + 2, jnp.max(jnp.where(together(r * r) <= goal, 0, 1)), earlier, alpha

    def unfinished(state):
        return (state[1] > 0) & (state[0] < SOLVE_STEPS)

    zero = jnp.zeros_like(norm)
    _, left, _, _ = lax.while_loop(unfinished, advance, (0, jnp.max(jnp.where(norm <= goal, 0, 1)), zero, zero))
    out_ref[...] = x_ref[...] * across

    @pl.when(left > 0)
    def _():
        work[0, :users, :] = re
        work[1, :users, :] = -im
        work[0, users:, :] = system_ref[users : users + HALF, :]
        work[1, users:, :] = system_ref[users + HALF :, :]
        lane = lax.broadcasted_iota(jnp.int32, (1, users), 1)

        def eliminate(j, carry):
            a, b = work[0], work[1]
            here = lane == j
            row_re = work[0, pl.ds(j, 1), :]
            row_im = work[1, pl.ds(j, 1), :]
            pivot = 1.0 / jnp.sum(jnp.where(here, row_re, 0.0), 1, keepdims=True)
            col_re = jnp.sum(jnp.where(here, a, 0.0), 1, keepdims=True) * pivot
            col_im = jnp.sum(jnp.where(here, b, 0.0), 1, keepdims=True) * pivot
            work[0] = jnp.where(here, col_re, a - (col_re * row_re - col_im * row_im))
            work[1] = jnp.where(here, col_im, b - (col_re * row_im + col_im * row_re))
            return carry

        lax.fori_loop(0, users, eliminate, 0)
        out_ref[:HALF, :] = work[0, users:, :]
        out_ref[HALF:, :] = work[1, users:, :]


def solved(systems, regularizer):
    _, rows, users = systems[0].shape
    f32 = jnp.float32
    vmem = pl.BlockSpec(memory_space=pltpu.VMEM)
    pair = pltpu.VMEM((2 * HALF, users), f32)
    return pl.pallas_call(
        solve_kernel,
        in_specs=[vmem] * (len(systems) + 1),
        out_specs=vmem,
        out_shape=jax.ShapeDtypeStruct((2 * HALF, users), f32),
        scratch_shapes=[
            pltpu.VMEM((rows, users), f32),
            pltpu.VMEM((2, 3, users, users), jnp.bfloat16),
            pair,
            pair,
            pair,
            pair,
            pltpu.VMEM((2, users + HALF, users), f32),
        ],
        compiler_params=pltpu.CompilerParams(vmem_limit_bytes=12 << 20),
        name="solved",
    )(*[in_vmem(s) for s in systems], regularizer.reshape(1, users))


def received_rows(observed_signal):
    _, samples, tones, antennas, width = observed_signal.shape
    y = jnp.moveaxis(observed_signal, 2, 0).reshape(tones, 2, samples, antennas * width)
    re, im = y[:, 0], y[:, 1]
    gap = ((0, 0), (0, HALF - samples), (0, 0))
    top = jnp.pad(jnp.concatenate([re, im], 2), gap)
    bottom = jnp.pad(jnp.concatenate([im, -re], 2), gap)
    return jnp.concatenate([top, bottom], 1)


def ap_at(z, y, core):
    return (z * Y_CHIPS + y % Y_CHIPS) * CORES + core


def over_ap(value, dz, dy, dcore):
    spots = [(z, y, c) for z in range(Z_CHIPS) for y in range(Y_CHIPS) for c in range(CORES)]
    pairs = [(ap_at(z, y, c), ap_at(z ^ dz, y + dy, c ^ dcore)) for z, y, c in spots]
    return lax.ppermute(value, "ap", pairs)


def over_sc(value, dz, dx):
    spots = [(z, x) for z in range(2) for x in range(X_CHIPS)]
    pairs = [(z * X_CHIPS + x, (z ^ dz) * X_CHIPS + (x + dx) % X_CHIPS) for z, x in spots]
    return lax.ppermute(value, "sc", pairs)


def gathered_tables(own):
    half = own.shape[0] // 2

    across = over_sc(own, 1, 0)
    up, down = over_sc(own, 0, 1), over_sc(own, 0, -1)
    up_twice, down_twice = over_sc(up[:half], 0, 1), over_sc(down[half:], 0, -1)
    across_up, across_down = over_sc(across, 0, 1), over_sc(across, 0, -1)
    opposite = jnp.concatenate([up_twice, down_twice], 0)
    return [own, across, up, down], [opposite, across_up, across_down, over_sc(opposite, 1, 0)]


def pack_kernel(*refs):
    *parts, out, sems = refs
    rows = out.shape[0] // len(parts)
    copies = [
        pltpu.make_async_copy(part, out.at[pl.ds(k * rows, rows)], sems.at[k]) for k, part in enumerate(parts)
    ]
    for copy in copies:
        copy.start()
    for copy in copies:
        copy.wait()


def packed_tables(parts):
    rows = sum(part.shape[0] for part in parts)
    vmem = pl.BlockSpec(memory_space=pltpu.VMEM)
    return pl.pallas_call(
        pack_kernel,
        in_specs=[pl.BlockSpec(memory_space=pltpu.HBM)] * len(parts),
        out_specs=vmem,
        out_shape=pltpu.VMEM((rows, *parts[0].shape[1:]), jnp.float32),
        scratch_shapes=[pltpu.SemaphoreType.DMA((len(parts),))],
        compiler_params=pltpu.CompilerParams(vmem_limit_bytes=4 << 20),
        name="packed_tables",
    )(*[pltpu.with_memory_space_constraint(p, pltpu.HBM) for p in parts])


def all_steps(observed_signal, delays, sines, path_gain_real, path_gain_imaginary, counts, regularizer):
    tones = observed_signal.shape[2]
    samples = observed_signal.shape[1]
    users = counts.shape[0]
    core = lax.axis_index("ap") % CORES
    own = packed_tables([delays, sines, path_gain_real, path_gain_imaginary])
    near, far = gathered_tables(own)
    state = prepared(tones, NEAR_SLOTS, near, counts)
    state = prepared(tones, FAR_SLOTS, far, counts, state)
    received = received_rows(observed_signal)
    rows = users + 2 * HALF
    top = rows // 2

    def systems(distance, planes, *after):
        y = lax.optimization_barrier((received, *after))[0] if after else received
        kept, sent = tone_systems(distance, planes, y, state)
        return kept, over_ap(sent, 0, 0, 1)

    def around(value, step):
        return over_ap(value, 0, step, 0)

    def joined(pieces, passed, at):
        total = pieces[0] + pieces[1]
        if at == 0:
            return jnp.concatenate([total[:, :top] + passed, total[:, top:]], 1)
        return jnp.concatenate([total[:, :top], total[:, top:] + passed], 1)

    def across_z(value):
        return over_ap(value, 1, 0, 0)

    kept, other = systems(2, (0, 1))
    up_far = systems(1, (1,), kept)
    farthest = kept + other
    up, down = around(farthest[:, :top], 1), around(farthest[:, top:], -1)
    up_own = systems(1, (0,), farthest, up_far[0])
    up_across = across_z(up_far[0] + up_far[1])
    down_far = systems(3, (1,), up_own[0])
    down_own = systems(3, (0,), down_far[0])
    down_across = across_z(down_far[0] + down_far[1])
    far_kept, far_other = systems(0, (1,), down_own[0])
    far_up, far_down = around(up[1:], 1), around(down[1:], -1)
    kept, other = systems(0, (0,), far_kept)
    up_own = joined(up_own, up[:1], 0) + up_across
    down_own = joined(down_own, down[:1], 1) + down_across
    up_own, kept = lax.optimization_barrier((up_own, kept))
    own_up, own_down = around(up_own, 1), around(down_own, -1)
    across = across_z((far_kept + far_other) + jnp.concatenate([far_up, far_down], 1))
    own_tone = solved([kept, other, own_up, own_down, across], regularizer)
    chips = lax.axis_size("ap") // CORES
    same = [[chip * CORES + c for chip in range(chips)] for c in range(CORES)]
    same_core = lax.all_to_all(
        jnp.broadcast_to(own_tone[None], (chips, *own_tone.shape)), "ap", 0, 0, tiled=True, axis_index_groups=same
    )
    other_core = over_ap(same_core, 0, 0, 1)
    first = jnp.where(core == 0, same_core, other_core)[::-1]
    second = jnp.where(core == 0, other_core, same_core)
    every = jnp.concatenate([first, second], 0).reshape(tones, 2, HALF, users)[:, :, :samples]
    return jnp.transpose(every, (1, 2, 0, 3))


def solution(mesh):
    placed = (
        P(None, None, "sc", None, "ap"),
        P(None, "sc", "ap"),
        P(None, "sc", "ap"),
        P(None, "sc", "ap"),
        P(None, "sc", "ap"),
        P(None, "ap"),
        P(),
    )
    return jax.shard_map(all_steps, mesh=mesh, in_specs=placed, out_specs=P(None, None, "sc", None), check_vma=False)
```

```python
import functools

import jax
import jax.numpy as jnp
import numpy as np
from jax import lax
from jax.experimental import pallas as pl
from jax.experimental.pallas import tpu as pltpu
from jax.sharding import PartitionSpec as P


CORES = 2
OWNERS = 8
NEAR_SLOTS = [((0, 0), 0, 0, 0, 8), ((1, 0), 1, 0, 1, 8), ((0, 1), 2, 0, 2, 8), ((0, 3), 3, 0, 3, 8)]
FAR_SLOTS = [((0, 2), 0, 0, 0, 8), ((1, 1), 1, 0, 1, 8), ((1, 3), 2, 0, 2, 8), ((1, 2), 3, 0, 3, 8)]
Y_CHIPS = 4
Z_CHIPS = 2
X_CHIPS = 4
ANTENNAS = 4
PATHS = 4
FFT_LEN = 512
FIT_POINTS = 4001
ROWS = 16
HALF = 16
SOLVE_STEPS = 42
STEPS_A_CHECK = 3
TOLERANCE = 1e-6


def turn_fit():
    u = 0.25 * np.cos(np.pi * (np.arange(FIT_POINTS) + 0.5) / FIT_POINTS)
    cheb = np.polynomial.chebyshev.Chebyshev
    poly = np.polynomial.Polynomial
    x = u * u
    fits = []
    for values, degree in ((np.sin(2 * np.pi * u) / u, 4), (np.cos(2 * np.pi * u), 5)):
        fits.append([float(c) for c in cheb.fit(x, values, degree, domain=[0, 0.0625]).convert(kind=poly).coef])
    return fits


SIN_FIT, COS_FIT = turn_fit()


def horner(x, coefs):
    total = jnp.full_like(x, coefs[-1])
    for c in coefs[-2::-1]:
        total = total * x + c
    return total


def small_turn(u):
    x = u * u
    return horner(x, COS_FIT), u * horner(x, SIN_FIT)


def doubled(c, s):
    return 1.0 - 2.0 * (s * s), 2.0 * (s * c)


def times(a, b):
    return a[0] * b[0] - a[1] * b[1], a[0] * b[1] + a[1] * b[0]


NT = (((1,), (1,)), ((), ()))


def product(a, b):
    return lax.dot_general(a, b, NT, preferred_element_type=jnp.float32)


def prepare_kernel(slots, pieces, tones, *refs):
    tab_refs, count_ref = refs[:pieces], refs[pieces]
    lead, turn = refs[-2:]
    per_block = count_ref.shape[0] // OWNERS
    sc = lax.axis_index("sc")
    sc_z, sc_x = sc // X_CHIPS, sc % X_CHIPS
    centre = ((sc * tones).astype(jnp.float32) + 0.5 * (tones - 1)) * (1.0 / FFT_LEN)
    side = jnp.where(lax.axis_index("ap") % CORES == 0, -1.0, 1.0)

    def prepare(slot, block, carry):
        (across, along), angles, a_at, gains, g_at = slot
        angles, gains = tab_refs[angles], tab_refs[gains]
        owner = jnp.abs(sc_z - across) * X_CHIPS + (sc_x - along + X_CHIPS) % X_CHIPS
        inside = pl.ds(pl.multiple_of(block * ROWS, ROWS), ROWS)
        here = pl.ds(pl.multiple_of(owner * per_block + block * ROWS, ROWS), ROWS)
        count = count_ref[here, :]
        for p in range(PATHS):
            delay = angles[a_at + p, inside, :]
            sine = angles[a_at + PATHS + p, inside, :]
            alive = p < count
            re = jnp.where(alive, gains[g_at + p, inside, :], 0.0)
            im = jnp.where(alive, gains[g_at + PATHS + p, inside, :], 0.0)
            angle = small_turn(delay * (side * (0.5 / FFT_LEN)))
            one = doubled(*angle)
            for pair in range(tones // 2):
                turn[pair, p, 0, here, :], turn[pair, p, 1, here, :] = angle
                if pair + 1 < tones // 2:
                    angle = times(angle, one)
            turns = delay * centre
            turns = turns - jnp.round(turns)
            c, s = doubled(*small_turn(0.5 * turns))
            z = times((re, im), (c, -s))
            steer = doubled(*small_turn(0.25 * sine))
            for n in range(ANTENNAS):
                lead[n, p, 0, here, :], lead[n, p, 1, here, :] = z
                if n + 1 < ANTENNAS:
                    z = times(z, steer)
        return carry

    for slot in slots:
        lax.fori_loop(0, per_block // ROWS, functools.partial(prepare, slot), 0)


def in_vmem(x):
    return pltpu.with_memory_space_constraint(x, pltpu.VMEM)


def prepared(tones, slots, tables, counts, state=()):
    users, width = counts.shape
    f32 = jnp.float32
    vmem = pl.BlockSpec(memory_space=pltpu.VMEM)
    first = len(tables) + 1
    return pl.pallas_call(
        functools.partial(prepare_kernel, slots, len(tables), tones),
        in_specs=[vmem] * (first + len(state)),
        out_specs=[vmem] * 2,
        out_shape=[
            pltpu.VMEM((ANTENNAS, PATHS, 2, users, width), f32),
            pltpu.VMEM((tones // 2, PATHS, 2, users, width), f32),
        ],
        input_output_aliases={first + k: k for k in range(len(state))},
        compiler_params=pltpu.CompilerParams(vmem_limit_bytes=4 << 20),
        name="prepared",
    )(*[in_vmem(t) for t in tables], in_vmem(counts), *state)


def tone_kernel(distance, planes, y_ref, lead, turn, kept_ref, sent_ref, *buffers):
    users, width = lead.shape[3:]
    blocks = users // ROWS
    half = ANTENNAS * width
    pairs = Y_CHIPS * Z_CHIPS
    ap = lax.axis_index("ap")
    core, chip = ap % CORES, ap // CORES
    chip_z, target_y = chip // Y_CHIPS, (chip + distance) % Y_CHIPS

    def pair_of(plane):
        return jnp.abs(chip_z - plane) * Y_CHIPS + target_y

    def build(buffers, block, plane):
        pair = pair_of(plane)
        with_re, with_im, lo = buffers
        here = pl.ds(block * ROWS, ROWS)
        below = pl.ds(users + block * ROWS, ROWS)
        cs = [(turn[pair, p, 0, here, :], turn[pair, p, 1, here, :]) for p in range(PATHS)]
        for n in range(ANTENNAS):
            sums = None
            for p in range(PATHS):
                c, s = cs[p]
                re, im = lead[n, p, 0, here, :], lead[n, p, 1, here, :]
                products = (re * c, im * s, im * c, re * s)
                sums = products if sums is None else tuple(a + b for a, b in zip(sums, products))
            a, b, c, d = sums
            columns = slice(n * width, (n + 1) * width)
            for tone, (re, im) in enumerate(((a - b, c + d), (a + b, c - d))):
                for part, (value, ref) in enumerate(((re, with_re), (im, with_im))):
                    packed = value.astype(jnp.bfloat16)
                    ref[tone, here, columns] = packed
                    if part == 0:
                        with_im[tone, below, columns] = packed
                    rest = (value - packed.astype(jnp.float32)).astype(jnp.bfloat16)
                    lo[tone, here, slice(part * half + n * width, part * half + (n + 1) * width)] = rest

    def multiply(buffers, plane, slot):
        with_re, with_im, lo = buffers
        pair = pair_of(plane)
        plus, minus = pairs + pair, pairs - 1 - pair
        first = jnp.where(core == 0, plus, minus)
        for tone, (at, out_ref) in enumerate(((first, sent_ref), (plus + minus - first, kept_ref))):
            y = y_ref[at]
            y_hi = y.astype(jnp.bfloat16)
            y_lo = (y - y_hi.astype(jnp.float32)).astype(jnp.bfloat16)
            for part, ref in enumerate((with_re, with_im)):
                end = ref.shape[1]
                ref[tone, end - 4 * HALF : end - 2 * HALF] = y_hi[:, part * half : (part + 1) * half]
                ref[tone, end - 2 * HALF :] = y_lo[:, part * half : (part + 1) * half]
            by_re = product(with_re[tone], with_re[tone, :users])
            by_im = product(with_im[tone], with_im[tone, :users])
            crossed = by_im[users : 2 * users]
            out_ref[slot, :users, :] = (by_re[:users] + by_im[:users]) + (crossed - crossed.T)
            filtered = by_re[users:] + by_im[2 * users :]
            rest = product(y_hi, lo[tone])
            out_ref[slot, users:, :] = filtered[: 2 * HALF] + (filtered[2 * HALF :] + rest)

    sides = [buffers[3 * k : 3 * k + 3] for k in range(len(planes))]

    def alone(block, carry):
        build(sides[0], block, planes[0])
        return carry

    lax.fori_loop(0, blocks, alone, 0, unroll=2)
    for slot, plane in enumerate(planes):
        multiply(sides[slot], plane, slot)
        if slot + 1 < len(planes):
            for block in range(blocks):
                build(sides[slot + 1], block, planes[slot + 1])


def tone_systems(distance, planes, received, state):
    users, _ = state[0].shape[3:]
    wide = received.shape[2]
    f32, bf16 = jnp.float32, jnp.bfloat16
    vmem = pl.BlockSpec(memory_space=pltpu.VMEM)
    channel_re = pltpu.VMEM((2, users + 4 * HALF, wide // 2), bf16)
    channel_im = pltpu.VMEM((2, 2 * users + 4 * HALF, wide // 2), bf16)
    rest = pltpu.VMEM((2, users, wide), bf16)
    return pl.pallas_call(
        functools.partial(tone_kernel, distance, planes),
        in_specs=[vmem] * (1 + len(state)),
        out_specs=[vmem, vmem],
        out_shape=[pltpu.VMEM((len(planes), users + 2 * HALF, users), f32)] * 2,
        scratch_shapes=[channel_re, channel_im, rest] * len(planes),
        compiler_params=pltpu.CompilerParams(vmem_limit_bytes=16 << 20),
        name="tone_systems",
    )(in_vmem(received), *state)


def three_parts(x):
    hi = x.astype(jnp.bfloat16)
    rest = x - hi.astype(jnp.float32)
    mid = rest.astype(jnp.bfloat16)
    return hi, mid, (rest - mid.astype(jnp.float32)).astype(jnp.bfloat16)


def solve_kernel(*refs):
    *part_refs, regularizer_ref, out_ref, system_ref, parts, x_ref, r_ref, p_ref, q_ref, work = refs
    system_ref[...] = sum(ref[0] for ref in part_refs)
    users = regularizer_ref.shape[1]
    f32 = jnp.float32
    g = system_ref[:users, :]
    flipped = g.T
    row = lax.broadcasted_iota(jnp.int32, (users, users), 0)
    column = lax.broadcasted_iota(jnp.int32, (users, users), 1)
    eye = row == column
    re = 0.5 * (g + flipped)
    im = 0.5 * (g - flipped)
    re = jnp.where(eye, re + regularizer_ref[...], re)
    diagonal = jnp.where(eye, re, 0.0)
    across = lax.rsqrt(jnp.sum(diagonal, 0, keepdims=True))
    down = lax.rsqrt(jnp.sum(diagonal, 1, keepdims=True))
    for k, matrix in enumerate((re, im)):
        for at, part in enumerate(three_parts(matrix * across * down)):
            parts[k, at] = part
    right = system_ref[users:, :] * across

    def together(v):
        total = jnp.sum(v[:HALF] + v[HALF:], 1, keepdims=True)
        return jnp.concatenate([total, total], 0)

    def dot(a, b):
        return jnp.dot(a, b, preferred_element_type=f32)

    rows = 2 * HALF

    def applied(p):
        hi, mid, low = three_parts(p)
        left3 = jnp.concatenate([hi, mid, low], 0)
        left2 = jnp.concatenate([hi, mid], 0)
        result = []
        for k in range(2):
            a = dot(left3, parts[k, 0])
            b = dot(left2, parts[k, 1])
            c = dot(hi, parts[k, 2])
            small = a[2 * rows :] + b[rows:] + c
            result.append(a[:rows] + ((a[rows : 2 * rows] + b[:rows]) + small))
        s, i = result
        return jnp.concatenate([s[:HALF] + i[HALF:], s[HALF:] - i[:HALF]], 0)

    norm = together(right * right)
    goal = norm * (TOLERANCE * TOLERANCE)
    nothing = jnp.zeros_like(right)
    x_ref[...], p_ref[...], q_ref[...] = nothing, nothing, nothing
    r_ref[...] = right

    def advance(state):
        done, _, earlier, alpha = state
        for _ in range(STEPS_A_CHECK):
            r = r_ref[...]
            applied_r = applied(r)
            rr = together(r * r)
            curvature = together(r * applied_r)
            beta = jnp.where(earlier > 0.0, rr / earlier, 0.0)
            curvature = curvature - jnp.where(alpha > 0.0, beta * rr / alpha, 0.0)
            alpha = jnp.where(curvature > 0.0, rr / curvature, 0.0)
            p = r + beta * p_ref[...]
            q = applied_r + beta * q_ref[...]
            p_ref[...], q_ref[...] = p, q
            x_ref[...] += alpha * p
            r_ref[...] = r - alpha * q
            earlier = rr
        r = r_ref[...]
        return done + STEPS_A_CHECK, jnp.max(jnp.where(together(r * r) <= goal, 0, 1)), earlier, alpha

    def unfinished(state):
        return (state[1] > 0) & (state[0] < SOLVE_STEPS)

    zero = jnp.zeros_like(norm)
    _, left, _, _ = lax.while_loop(unfinished, advance, (0, jnp.max(jnp.where(norm <= goal, 0, 1)), zero, zero))
    out_ref[...] = x_ref[...] * across

    @pl.when(left > 0)
    def _():
        work[0, :users, :] = re
        work[1, :users, :] = -im
        work[0, users:, :] = system_ref[users : users + HALF, :]
        work[1, users:, :] = system_ref[users + HALF :, :]
        lane = lax.broadcasted_iota(jnp.int32, (1, users), 1)

        def eliminate(j, carry):
            a, b = work[0], work[1]
            here = lane == j
            row_re = work[0, pl.ds(j, 1), :]
            row_im = work[1, pl.ds(j, 1), :]
            pivot = 1.0 / jnp.sum(jnp.where(here, row_re, 0.0), 1, keepdims=True)
            col_re = jnp.sum(jnp.where(here, a, 0.0), 1, keepdims=True) * pivot
            col_im = jnp.sum(jnp.where(here, b, 0.0), 1, keepdims=True) * pivot
            work[0] = jnp.where(here, col_re, a - (col_re * row_re - col_im * row_im))
            work[1] = jnp.where(here, col_im, b - (col_re * row_im + col_im * row_re))
            return carry

        lax.fori_loop(0, users, eliminate, 0)
        out_ref[:HALF, :] = work[0, users:, :]
        out_ref[HALF:, :] = work[1, users:, :]


def solved(systems, regularizer):
    _, rows, users = systems[0].shape
    f32 = jnp.float32
    vmem = pl.BlockSpec(memory_space=pltpu.VMEM)
    pair = pltpu.VMEM((2 * HALF, users), f32)
    return pl.pallas_call(
        solve_kernel,
        in_specs=[vmem] * (len(systems) + 1),
        out_specs=vmem,
        out_shape=jax.ShapeDtypeStruct((2 * HALF, users), f32),
        scratch_shapes=[
            pltpu.VMEM((rows, users), f32),
            pltpu.VMEM((2, 3, users, users), jnp.bfloat16),
            pair,
            pair,
            pair,
            pair,
            pltpu.VMEM((2, users + HALF, users), f32),
        ],
        compiler_params=pltpu.CompilerParams(vmem_limit_bytes=12 << 20),
        name="solved",
    )(*[in_vmem(s) for s in systems], regularizer.reshape(1, users))


def received_rows(observed_signal):
    _, samples, tones, antennas, width = observed_signal.shape
    y = jnp.moveaxis(observed_signal, 2, 0).reshape(tones, 2, samples, antennas * width)
    re, im = y[:, 0], y[:, 1]
    gap = ((0, 0), (0, HALF - samples), (0, 0))
    top = jnp.pad(jnp.concatenate([re, im], 2), gap)
    bottom = jnp.pad(jnp.concatenate([im, -re], 2), gap)
    return jnp.concatenate([top, bottom], 1)


def ap_at(z, y, core):
    return (z * Y_CHIPS + y % Y_CHIPS) * CORES + core


def over_ap(value, dz, dy, dcore):
    spots = [(z, y, c) for z in range(Z_CHIPS) for y in range(Y_CHIPS) for c in range(CORES)]
    pairs = [(ap_at(z, y, c), ap_at(z ^ dz, y + dy, c ^ dcore)) for z, y, c in spots]
    return lax.ppermute(value, "ap", pairs)


def over_sc(value, dz, dx):
    spots = [(z, x) for z in range(2) for x in range(X_CHIPS)]
    pairs = [(z * X_CHIPS + x, (z ^ dz) * X_CHIPS + (x + dx) % X_CHIPS) for z, x in spots]
    return lax.ppermute(value, "sc", pairs)


def gathered_tables(own):
    half = own.shape[0] // 2

    across = over_sc(own, 1, 0)
    up, down = over_sc(own, 0, 1), over_sc(own, 0, -1)
    up_twice, down_twice = over_sc(up[:half], 0, 1), over_sc(down[half:], 0, -1)
    across_up, across_down = over_sc(across, 0, 1), over_sc(across, 0, -1)
    opposite = jnp.concatenate([up_twice, down_twice], 0)
    return [own, across, up, down], [opposite, across_up, across_down, over_sc(opposite, 1, 0)]


def pack_kernel(*refs):
    *parts, out, sems = refs
    rows = out.shape[0] // len(parts)
    copies = [
        pltpu.make_async_copy(part, out.at[pl.ds(k * rows, rows)], sems.at[k]) for k, part in enumerate(parts)
    ]
    for copy in copies:
        copy.start()
    for copy in copies:
        copy.wait()


def packed_tables(parts):
    rows = sum(part.shape[0] for part in parts)
    vmem = pl.BlockSpec(memory_space=pltpu.VMEM)
    return pl.pallas_call(
        pack_kernel,
        in_specs=[pl.BlockSpec(memory_space=pltpu.HBM)] * len(parts),
        out_specs=vmem,
        out_shape=pltpu.VMEM((rows, *parts[0].shape[1:]), jnp.float32),
        scratch_shapes=[pltpu.SemaphoreType.DMA((len(parts),))],
        compiler_params=pltpu.CompilerParams(vmem_limit_bytes=4 << 20),
        name="packed_tables",
    )(*[pltpu.with_memory_space_constraint(p, pltpu.HBM) for p in parts])


def all_steps(observed_signal, delays, sines, path_gain_real, path_gain_imaginary, counts, regularizer):
    tones = observed_signal.shape[2]
    samples = observed_signal.shape[1]
    users = counts.shape[0]
    core = lax.axis_index("ap") % CORES
    own = packed_tables([delays, sines, path_gain_real, path_gain_imaginary])
    near, far = gathered_tables(own)
    state = prepared(tones, NEAR_SLOTS, near, counts)
    state = prepared(tones, FAR_SLOTS, far, counts, state)
    received = received_rows(observed_signal)
    rows = users + 2 * HALF
    top = rows // 2

    def systems(distance, planes, *after):
        y = lax.optimization_barrier((received, *after))[0] if after else received
        kept, sent = tone_systems(distance, planes, y, state)
        return kept, over_ap(sent, 0, 0, 1)

    def around(value, step):
        return over_ap(value, 0, step, 0)

    def joined(pieces, passed, at):
        total = pieces[0] + pieces[1]
        if at == 0:
            return jnp.concatenate([total[:, :top] + passed, total[:, top:]], 1)
        return jnp.concatenate([total[:, :top], total[:, top:] + passed], 1)

    def across_z(value):
        return over_ap(value, 1, 0, 0)

    kept, other = systems(2, (0, 1))
    up_far = systems(1, (1,), kept)
    farthest = kept + other
    up, down = around(farthest[:, :top], 1), around(farthest[:, top:], -1)
    up_own = systems(1, (0,), farthest, up_far[0])
    up_across = across_z(up_far[0] + up_far[1])
    down_far = systems(3, (1,), up_own[0])
    down_own = systems(3, (0,), down_far[0])
    down_across = across_z(down_far[0] + down_far[1])
    far_kept, far_other = systems(0, (1,), down_own[0])
    far_up, far_down = around(up[1:], 1), around(down[1:], -1)
    kept, other = systems(0, (0,), far_kept)
    up_own = joined(up_own, up[:1], 0) + up_across
    down_own = joined(down_own, down[:1], 1) + down_across
    up_own, kept = lax.optimization_barrier((up_own, kept))
    own_up, own_down = around(up_own, 1), around(down_own, -1)
    across = across_z((far_kept + far_other) + jnp.concatenate([far_up, far_down], 1))
    own_tone = solved([kept, other, own_up, own_down, across], regularizer)
    chips = lax.axis_size("ap") // CORES
    same = [[chip * CORES + c for chip in range(chips)] for c in range(CORES)]
    same_core = lax.all_to_all(
        jnp.broadcast_to(own_tone[None], (chips, *own_tone.shape)), "ap", 0, 0, tiled=True, axis_index_groups=same
    )
    other_core = over_ap(same_core, 0, 0, 1)
    first = jnp.where(core == 0, same_core, other_core)[::-1]
    second = jnp.where(core == 0, other_core, same_core)
    every = jnp.concatenate([first, second], 0).reshape(tones, 2, HALF, users)[:, :, :samples]
    return jnp.transpose(every, (1, 2, 0, 3))


def solution(mesh):
    placed = (
        P(None, None, "sc", None, "ap"),
        P(None, "sc", "ap"),
        P(None, "sc", "ap"),
        P(None, "sc", "ap"),
        P(None, "sc", "ap"),
        P(None, "ap"),
        P(),
    )
    return jax.shard_map(all_steps, mesh=mesh, in_specs=placed, out_specs=P(None, None, "sc", None), check_vma=False)
```

```python
import functools

import jax
import jax.numpy as jnp
import numpy as np
from jax import lax
from jax.experimental import pallas as pl
from jax.experimental.pallas import tpu as pltpu
from jax.sharding import PartitionSpec as P


CORES = 2
OWNERS = 8
NEAR_SLOTS = [((0, 0), 0, 0, 0, 8), ((1, 0), 1, 0, 1, 8), ((0, 1), 2, 0, 2, 8), ((0, 3), 3, 0, 3, 8)]
FAR_SLOTS = [((0, 2), 0, 0, 0, 8), ((1, 1), 1, 0, 1, 8), ((1, 3), 2, 0, 2, 8), ((1, 2), 3, 0, 3, 8)]
Y_CHIPS = 4
Z_CHIPS = 2
X_CHIPS = 4
ANTENNAS = 4
PATHS = 4
FFT_LEN = 512
FIT_POINTS = 4001
ROWS = 16
HALF = 16
SOLVE_STEPS = 40
TOLERANCE = 1e-6


def turn_fit():
    u = 0.25 * np.cos(np.pi * (np.arange(FIT_POINTS) + 0.5) / FIT_POINTS)
    cheb = np.polynomial.chebyshev.Chebyshev
    poly = np.polynomial.Polynomial
    x = u * u
    fits = []
    for values, degree in ((np.sin(2 * np.pi * u) / u, 4), (np.cos(2 * np.pi * u), 5)):
        fits.append([float(c) for c in cheb.fit(x, values, degree, domain=[0, 0.0625]).convert(kind=poly).coef])
    return fits


SIN_FIT, COS_FIT = turn_fit()


def horner(x, coefs):
    total = jnp.full_like(x, coefs[-1])
    for c in coefs[-2::-1]:
        total = total * x + c
    return total


def small_turn(u):
    x = u * u
    return horner(x, COS_FIT), u * horner(x, SIN_FIT)


def doubled(c, s):
    return 1.0 - 2.0 * (s * s), 2.0 * (s * c)


def times(a, b):
    return a[0] * b[0] - a[1] * b[1], a[0] * b[1] + a[1] * b[0]


NT = (((1,), (1,)), ((), ()))


def product(a, b):
    return lax.dot_general(a, b, NT, preferred_element_type=jnp.float32)


def prepare_kernel(slots, pieces, tones, *refs):
    tab_refs, count_ref = refs[:pieces], refs[pieces]
    lead, turn = refs[-2:]
    per_block = count_ref.shape[0] // OWNERS
    sc = lax.axis_index("sc")
    sc_z, sc_x = sc // X_CHIPS, sc % X_CHIPS
    centre = ((sc * tones).astype(jnp.float32) + 0.5 * (tones - 1)) * (1.0 / FFT_LEN)
    side = jnp.where(lax.axis_index("ap") % CORES == 0, -1.0, 1.0)

    def prepare(slot, block, carry):
        (across, along), angles, a_at, gains, g_at = slot
        angles, gains = tab_refs[angles], tab_refs[gains]
        owner = jnp.abs(sc_z - across) * X_CHIPS + (sc_x - along + X_CHIPS) % X_CHIPS
        inside = pl.ds(pl.multiple_of(block * ROWS, ROWS), ROWS)
        here = pl.ds(pl.multiple_of(owner * per_block + block * ROWS, ROWS), ROWS)
        count = count_ref[here, :]
        for p in range(PATHS):
            delay = angles[a_at + p, inside, :]
            sine = angles[a_at + PATHS + p, inside, :]
            alive = p < count
            re = jnp.where(alive, gains[g_at + p, inside, :], 0.0)
            im = jnp.where(alive, gains[g_at + PATHS + p, inside, :], 0.0)
            angle = small_turn(delay * (side * (0.5 / FFT_LEN)))
            one = doubled(*angle)
            for pair in range(tones // 2):
                turn[pair, p, 0, here, :], turn[pair, p, 1, here, :] = angle
                if pair + 1 < tones // 2:
                    angle = times(angle, one)
            turns = delay * centre
            turns = turns - jnp.round(turns)
            c, s = doubled(*small_turn(0.5 * turns))
            z = times((re, im), (c, -s))
            steer = doubled(*small_turn(0.25 * sine))
            for n in range(ANTENNAS):
                lead[n, p, 0, here, :], lead[n, p, 1, here, :] = z
                if n + 1 < ANTENNAS:
                    z = times(z, steer)
        return carry

    for slot in slots:
        lax.fori_loop(0, per_block // ROWS, functools.partial(prepare, slot), 0)


def in_vmem(x):
    return pltpu.with_memory_space_constraint(x, pltpu.VMEM)


def prepared(tones, slots, tables, counts, state=()):
    users, width = counts.shape
    f32 = jnp.float32
    vmem = pl.BlockSpec(memory_space=pltpu.VMEM)
    first = len(tables) + 1
    return pl.pallas_call(
        functools.partial(prepare_kernel, slots, len(tables), tones),
        in_specs=[vmem] * (first + len(state)),
        out_specs=[vmem] * 2,
        out_shape=[
            pltpu.VMEM((ANTENNAS, PATHS, 2, users, width), f32),
            pltpu.VMEM((tones // 2, PATHS, 2, users, width), f32),
        ],
        input_output_aliases={first + k: k for k in range(len(state))},
        compiler_params=pltpu.CompilerParams(vmem_limit_bytes=4 << 20),
        name="prepared",
    )(*[in_vmem(t) for t in tables], in_vmem(counts), *state)


def tone_kernel(distance, planes, y_ref, lead, turn, kept_ref, sent_ref, *buffers):
    users, width = lead.shape[3:]
    blocks = users // ROWS
    half = ANTENNAS * width
    pairs = Y_CHIPS * Z_CHIPS
    ap = lax.axis_index("ap")
    core, chip = ap % CORES, ap // CORES
    chip_z, target_y = chip // Y_CHIPS, (chip + distance) % Y_CHIPS

    def pair_of(plane):
        return jnp.abs(chip_z - plane) * Y_CHIPS + target_y

    def build(buffers, block, plane):
        pair = pair_of(plane)
        with_re, with_im, lo = buffers
        here = pl.ds(block * ROWS, ROWS)
        below = pl.ds(users + block * ROWS, ROWS)
        cs = [(turn[pair, p, 0, here, :], turn[pair, p, 1, here, :]) for p in range(PATHS)]
        for n in range(ANTENNAS):
            sums = None
            for p in range(PATHS):
                c, s = cs[p]
                re, im = lead[n, p, 0, here, :], lead[n, p, 1, here, :]
                products = (re * c, im * s, im * c, re * s)
                sums = products if sums is None else tuple(a + b for a, b in zip(sums, products))
            a, b, c, d = sums
            columns = slice(n * width, (n + 1) * width)
            for tone, (re, im) in enumerate(((a - b, c + d), (a + b, c - d))):
                for part, (value, ref) in enumerate(((re, with_re), (im, with_im))):
                    packed = value.astype(jnp.bfloat16)
                    ref[tone, here, columns] = packed
                    if part == 0:
                        with_im[tone, below, columns] = packed
                    rest = (value - packed.astype(jnp.float32)).astype(jnp.bfloat16)
                    lo[tone, here, slice(part * half + n * width, part * half + (n + 1) * width)] = rest

    def multiply(buffers, plane, slot):
        with_re, with_im, lo = buffers
        pair = pair_of(plane)
        plus, minus = pairs + pair, pairs - 1 - pair
        first = jnp.where(core == 0, plus, minus)
        for tone, (at, out_ref) in enumerate(((first, sent_ref), (plus + minus - first, kept_ref))):
            y = y_ref[at]
            y_hi = y.astype(jnp.bfloat16)
            y_lo = (y - y_hi.astype(jnp.float32)).astype(jnp.bfloat16)
            for part, ref in enumerate((with_re, with_im)):
                end = ref.shape[1]
                ref[tone, end - 4 * HALF : end - 2 * HALF] = y_hi[:, part * half : (part + 1) * half]
                ref[tone, end - 2 * HALF :] = y_lo[:, part * half : (part + 1) * half]
            by_re = product(with_re[tone], with_re[tone, :users])
            by_im = product(with_im[tone], with_im[tone, :users])
            crossed = by_im[users : 2 * users]
            out_ref[slot, :users, :] = (by_re[:users] + by_im[:users]) + (crossed - crossed.T)
            filtered = by_re[users:] + by_im[2 * users :]
            rest = product(y_hi, lo[tone])
            out_ref[slot, users:, :] = filtered[: 2 * HALF] + (filtered[2 * HALF :] + rest)

    sides = [buffers[3 * k : 3 * k + 3] for k in range(len(planes))]

    def alone(block, carry):
        build(sides[0], block, planes[0])
        return carry

    lax.fori_loop(0, blocks, alone, 0, unroll=2)
    for slot, plane in enumerate(planes):
        multiply(sides[slot], plane, slot)
        if slot + 1 < len(planes):
            for block in range(blocks):
                build(sides[slot + 1], block, planes[slot + 1])


def tone_systems(distance, planes, received, state):
    users, _ = state[0].shape[3:]
    wide = received.shape[2]
    f32, bf16 = jnp.float32, jnp.bfloat16
    vmem = pl.BlockSpec(memory_space=pltpu.VMEM)
    channel_re = pltpu.VMEM((2, users + 4 * HALF, wide // 2), bf16)
    channel_im = pltpu.VMEM((2, 2 * users + 4 * HALF, wide // 2), bf16)
    rest = pltpu.VMEM((2, users, wide), bf16)
    return pl.pallas_call(
        functools.partial(tone_kernel, distance, planes),
        in_specs=[vmem] * (1 + len(state)),
        out_specs=[vmem, vmem],
        out_shape=[pltpu.VMEM((len(planes), users + 2 * HALF, users), f32)] * 2,
        scratch_shapes=[channel_re, channel_im, rest] * len(planes),
        compiler_params=pltpu.CompilerParams(vmem_limit_bytes=16 << 20),
        name="tone_systems",
    )(in_vmem(received), *state)


def three_parts(x):
    hi = x.astype(jnp.bfloat16)
    rest = x - hi.astype(jnp.float32)
    mid = rest.astype(jnp.bfloat16)
    return hi, mid, (rest - mid.astype(jnp.float32)).astype(jnp.bfloat16)


def solve_kernel(*refs):
    *part_refs, regularizer_ref, out_ref, system_ref, parts, x_ref, r_ref, p_ref, q_ref, work = refs
    system_ref[...] = sum(ref[0] for ref in part_refs)
    users = regularizer_ref.shape[1]
    f32 = jnp.float32
    g = system_ref[:users, :]
    flipped = g.T
    row = lax.broadcasted_iota(jnp.int32, (users, users), 0)
    column = lax.broadcasted_iota(jnp.int32, (users, users), 1)
    eye = row == column
    re = 0.5 * (g + flipped)
    im = 0.5 * (g - flipped)
    re = jnp.where(eye, re + regularizer_ref[...], re)
    diagonal = jnp.where(eye, re, 0.0)
    across = lax.rsqrt(jnp.sum(diagonal, 0, keepdims=True))
    down = lax.rsqrt(jnp.sum(diagonal, 1, keepdims=True))
    for k, matrix in enumerate((re, im)):
        for at, part in enumerate(three_parts(matrix * across * down)):
            parts[k, at] = part
    right = system_ref[users:, :] * across

    def together(v):
        total = jnp.sum(v[:HALF] + v[HALF:], 1, keepdims=True)
        return jnp.concatenate([total, total], 0)

    def dot(a, b):
        return jnp.dot(a, b, preferred_element_type=f32)

    rows = 2 * HALF

    def applied(p):
        hi, mid, low = three_parts(p)
        left3 = jnp.concatenate([hi, mid, low], 0)
        left2 = jnp.concatenate([hi, mid], 0)
        result = []
        for k in range(2):
            a = dot(left3, parts[k, 0])
            b = dot(left2, parts[k, 1])
            c = dot(hi, parts[k, 2])
            small = a[2 * rows :] + b[rows:] + c
            result.append(a[:rows] + ((a[rows : 2 * rows] + b[:rows]) + small))
        s, i = result
        return jnp.concatenate([s[:HALF] + i[HALF:], s[HALF:] - i[:HALF]], 0)

    norm = together(right * right)
    goal = norm * (TOLERANCE * TOLERANCE)
    nothing = jnp.zeros_like(right)
    x_ref[...], p_ref[...], q_ref[...] = nothing, nothing, nothing
    r_ref[...] = right

    def advance(state):
        done, _, earlier, alpha = state
        for _ in range(2):
            r = r_ref[...]
            applied_r = applied(r)
            rr = together(r * r)
            curvature = together(r * applied_r)
            beta = jnp.where(earlier > 0.0, rr / earlier, 0.0)
            curvature = curvature - jnp.where(alpha > 0.0, beta * rr / alpha, 0.0)
            alpha = jnp.where(curvature > 0.0, rr / curvature, 0.0)
            p = r + beta * p_ref[...]
            q = applied_r + beta * q_ref[...]
            p_ref[...], q_ref[...] = p, q
            x_ref[...] += alpha * p
            r_ref[...] = r - alpha * q
            earlier = rr
        r = r_ref[...]
        return done + 2, jnp.max(jnp.where(together(r * r) <= goal, 0, 1)), earlier, alpha

    def unfinished(state):
        return (state[1] > 0) & (state[0] < SOLVE_STEPS)

    zero = jnp.zeros_like(norm)
    _, left, _, _ = lax.while_loop(unfinished, advance, (0, jnp.max(jnp.where(norm <= goal, 0, 1)), zero, zero))
    out_ref[...] = x_ref[...] * across

    @pl.when(left > 0)
    def _():
        work[0, :users, :] = re
        work[1, :users, :] = -im
        work[0, users:, :] = system_ref[users : users + HALF, :]
        work[1, users:, :] = system_ref[users + HALF :, :]
        lane = lax.broadcasted_iota(jnp.int32, (1, users), 1)

        def eliminate(j, carry):
            a, b = work[0], work[1]
            here = lane == j
            row_re = work[0, pl.ds(j, 1), :]
            row_im = work[1, pl.ds(j, 1), :]
            pivot = 1.0 / jnp.sum(jnp.where(here, row_re, 0.0), 1, keepdims=True)
            col_re = jnp.sum(jnp.where(here, a, 0.0), 1, keepdims=True) * pivot
            col_im = jnp.sum(jnp.where(here, b, 0.0), 1, keepdims=True) * pivot
            work[0] = jnp.where(here, col_re, a - (col_re * row_re - col_im * row_im))
            work[1] = jnp.where(here, col_im, b - (col_re * row_im + col_im * row_re))
            return carry

        lax.fori_loop(0, users, eliminate, 0)
        out_ref[:HALF, :] = work[0, users:, :]
        out_ref[HALF:, :] = work[1, users:, :]


def solved(systems, regularizer):
    _, rows, users = systems[0].shape
    f32 = jnp.float32
    vmem = pl.BlockSpec(memory_space=pltpu.VMEM)
    pair = pltpu.VMEM((2 * HALF, users), f32)
    return pl.pallas_call(
        solve_kernel,
        in_specs=[vmem] * (len(systems) + 1),
        out_specs=vmem,
        out_shape=jax.ShapeDtypeStruct((2 * HALF, users), f32),
        scratch_shapes=[
            pltpu.VMEM((rows, users), f32),
            pltpu.VMEM((2, 3, users, users), jnp.bfloat16),
            pair,
            pair,
            pair,
            pair,
            pltpu.VMEM((2, users + HALF, users), f32),
        ],
        compiler_params=pltpu.CompilerParams(vmem_limit_bytes=12 << 20),
        name="solved",
    )(*[in_vmem(s) for s in systems], regularizer.reshape(1, users))


def received_rows(observed_signal):
    _, samples, tones, antennas, width = observed_signal.shape
    y = jnp.moveaxis(observed_signal, 2, 0).reshape(tones, 2, samples, antennas * width)
    re, im = y[:, 0], y[:, 1]
    gap = ((0, 0), (0, HALF - samples), (0, 0))
    top = jnp.pad(jnp.concatenate([re, im], 2), gap)
    bottom = jnp.pad(jnp.concatenate([im, -re], 2), gap)
    return jnp.concatenate([top, bottom], 1)


def ap_at(z, y, core):
    return (z * Y_CHIPS + y % Y_CHIPS) * CORES + core


def over_ap(value, dz, dy, dcore):
    spots = [(z, y, c) for z in range(Z_CHIPS) for y in range(Y_CHIPS) for c in range(CORES)]
    pairs = [(ap_at(z, y, c), ap_at(z ^ dz, y + dy, c ^ dcore)) for z, y, c in spots]
    return lax.ppermute(value, "ap", pairs)


def over_sc(value, dz, dx):
    spots = [(z, x) for z in range(2) for x in range(X_CHIPS)]
    pairs = [(z * X_CHIPS + x, (z ^ dz) * X_CHIPS + (x + dx) % X_CHIPS) for z, x in spots]
    return lax.ppermute(value, "sc", pairs)


def gathered_tables(own):
    half = own.shape[0] // 2

    across = over_sc(own, 1, 0)
    up, down = over_sc(own, 0, 1), over_sc(own, 0, -1)
    up_twice, down_twice = over_sc(up[:half], 0, 1), over_sc(down[half:], 0, -1)
    across_up, across_down = over_sc(across, 0, 1), over_sc(across, 0, -1)
    opposite = jnp.concatenate([up_twice, down_twice], 0)
    return [own, across, up, down], [opposite, across_up, across_down, over_sc(opposite, 1, 0)]


def pack_kernel(*refs):
    *parts, out, sems = refs
    rows = out.shape[0] // len(parts)
    copies = [
        pltpu.make_async_copy(part, out.at[pl.ds(k * rows, rows)], sems.at[k]) for k, part in enumerate(parts)
    ]
    for copy in copies:
        copy.start()
    for copy in copies:
        copy.wait()


def packed_tables(parts):
    rows = sum(part.shape[0] for part in parts)
    vmem = pl.BlockSpec(memory_space=pltpu.VMEM)
    return pl.pallas_call(
        pack_kernel,
        in_specs=[pl.BlockSpec(memory_space=pltpu.HBM)] * len(parts),
        out_specs=vmem,
        out_shape=pltpu.VMEM((rows, *parts[0].shape[1:]), jnp.float32),
        scratch_shapes=[pltpu.SemaphoreType.DMA((len(parts),))],
        compiler_params=pltpu.CompilerParams(vmem_limit_bytes=4 << 20),
        name="packed_tables",
    )(*[pltpu.with_memory_space_constraint(p, pltpu.HBM) for p in parts])


def all_steps(observed_signal, delays, sines, path_gain_real, path_gain_imaginary, counts, regularizer):
    tones = observed_signal.shape[2]
    samples = observed_signal.shape[1]
    users = counts.shape[0]
    core = lax.axis_index("ap") % CORES
    own = packed_tables([delays, sines, path_gain_real, path_gain_imaginary])
    near, far = gathered_tables(own)
    state = prepared(tones, NEAR_SLOTS, near, counts)
    state = prepared(tones, FAR_SLOTS, far, counts, state)
    received = received_rows(observed_signal)
    rows = users + 2 * HALF
    top = rows // 2

    def systems(distance, planes, *after):
        y = lax.optimization_barrier((received, *after))[0] if after else received
        kept, sent = tone_systems(distance, planes, y, state)
        return kept, over_ap(sent, 0, 0, 1)

    def around(value, step):
        return over_ap(value, 0, step, 0)

    def joined(pieces, passed, at):
        total = pieces[0] + pieces[1]
        if at == 0:
            return jnp.concatenate([total[:, :top] + passed, total[:, top:]], 1)
        return jnp.concatenate([total[:, :top], total[:, top:] + passed], 1)

    def across_z(value):
        return over_ap(value, 1, 0, 0)

    far2 = systems(2, (1,))
    own2 = systems(2, (0,), far2[0])
    first = across_z(far2[0] + far2[1])
    far1 = systems(1, (1,), own2[0])
    own1 = systems(1, (0,), far1[0])
    up_across = across_z(far1[0] + far1[1])
    far3 = systems(3, (1,), own1[0])
    own3 = systems(3, (0,), far3[0])
    down_across = across_z(far3[0] + far3[1])
    passing = (own2[0] + own2[1]) + first
    up, down = around(passing[:, :top], 1), around(passing[:, top:], -1)
    far0 = systems(0, (1,), own3[0])
    kept, other = systems(0, (0,), far0[0])
    across = across_z(far0[0] + far0[1])
    up_own = joined(own1, up, 0) + up_across
    down_own = joined(own3, down, 1) + down_across
    own_up, own_down = around(up_own, 1), around(down_own, -1)
    own_tone = solved([kept, other, own_up, own_down, across], regularizer)
    chips = lax.axis_size("ap") // CORES
    same = [[chip * CORES + c for chip in range(chips)] for c in range(CORES)]
    same_core = lax.all_to_all(
        jnp.broadcast_to(own_tone[None], (chips, *own_tone.shape)), "ap", 0, 0, tiled=True, axis_index_groups=same
    )
    other_core = over_ap(same_core, 0, 0, 1)
    first = jnp.where(core == 0, same_core, other_core)[::-1]
    second = jnp.where(core == 0, other_core, same_core)
    every = jnp.concatenate([first, second], 0).reshape(tones, 2, HALF, users)[:, :, :samples]
    return jnp.transpose(every, (1, 2, 0, 3))


def solution(mesh):
    placed = (
        P(None, None, "sc", None, "ap"),
        P(None, "sc", "ap"),
        P(None, "sc", "ap"),
        P(None, "sc", "ap"),
        P(None, "sc", "ap"),
        P(None, "ap"),
        P(),
    )
    return jax.shard_map(all_steps, mesh=mesh, in_specs=placed, out_specs=P(None, None, "sc", None), check_vma=False)
```

```python
import functools

import jax
import jax.numpy as jnp
import numpy as np
from jax import lax
from jax.experimental import pallas as pl
from jax.experimental.pallas import tpu as pltpu
from jax.sharding import PartitionSpec as P


CORES = 2
OWNERS = 8
NEAR_SLOTS = [((0, 0), 0, 0, 0, 8), ((1, 0), 1, 0, 1, 8), ((0, 1), 2, 0, 2, 8), ((0, 3), 3, 0, 3, 8)]
FAR_SLOTS = [((0, 2), 0, 0, 0, 8), ((1, 1), 1, 0, 1, 8), ((1, 3), 2, 0, 2, 8), ((1, 2), 3, 0, 3, 8)]
Y_CHIPS = 4
Z_CHIPS = 2
X_CHIPS = 4
ANTENNAS = 4
PATHS = 4
FFT_LEN = 512
FIT_POINTS = 4001
ROWS = 16
HALF = 16
SOLVE_STEPS = 40
STEPS_A_CHECK = 5
TOLERANCE = 1e-6


def turn_fit():
    u = 0.25 * np.cos(np.pi * (np.arange(FIT_POINTS) + 0.5) / FIT_POINTS)
    cheb = np.polynomial.chebyshev.Chebyshev
    poly = np.polynomial.Polynomial
    x = u * u
    fits = []
    for values, degree in ((np.sin(2 * np.pi * u) / u, 4), (np.cos(2 * np.pi * u), 5)):
        fits.append([float(c) for c in cheb.fit(x, values, degree, domain=[0, 0.0625]).convert(kind=poly).coef])
    return fits


SIN_FIT, COS_FIT = turn_fit()


def horner(x, coefs):
    total = jnp.full_like(x, coefs[-1])
    for c in coefs[-2::-1]:
        total = total * x + c
    return total


def small_turn(u):
    x = u * u
    return horner(x, COS_FIT), u * horner(x, SIN_FIT)


def doubled(c, s):
    return 1.0 - 2.0 * (s * s), 2.0 * (s * c)


def times(a, b):
    return a[0] * b[0] - a[1] * b[1], a[0] * b[1] + a[1] * b[0]


NT = (((1,), (1,)), ((), ()))


def product(a, b):
    return lax.dot_general(a, b, NT, preferred_element_type=jnp.float32)


def prepare_kernel(slots, pieces, tones, *refs):
    tab_refs, count_ref = refs[:pieces], refs[pieces]
    lead, turn = refs[-2:]
    per_block = count_ref.shape[0] // OWNERS
    sc = lax.axis_index("sc")
    sc_z, sc_x = sc // X_CHIPS, sc % X_CHIPS
    centre = ((sc * tones).astype(jnp.float32) + 0.5 * (tones - 1)) * (1.0 / FFT_LEN)
    side = jnp.where(lax.axis_index("ap") % CORES == 0, -1.0, 1.0)

    def prepare(slot, block, carry):
        (across, along), angles, a_at, gains, g_at = slot
        angles, gains = tab_refs[angles], tab_refs[gains]
        owner = jnp.abs(sc_z - across) * X_CHIPS + (sc_x - along + X_CHIPS) % X_CHIPS
        inside = pl.ds(pl.multiple_of(block * ROWS, ROWS), ROWS)
        here = pl.ds(pl.multiple_of(owner * per_block + block * ROWS, ROWS), ROWS)
        count = count_ref[here, :]
        for p in range(PATHS):
            delay = angles[a_at + p, inside, :]
            sine = angles[a_at + PATHS + p, inside, :]
            alive = p < count
            re = jnp.where(alive, gains[g_at + p, inside, :], 0.0)
            im = jnp.where(alive, gains[g_at + PATHS + p, inside, :], 0.0)
            angle = small_turn(delay * (side * (0.5 / FFT_LEN)))
            one = doubled(*angle)
            for pair in range(tones // 2):
                turn[pair, p, 0, here, :], turn[pair, p, 1, here, :] = angle
                if pair + 1 < tones // 2:
                    angle = times(angle, one)
            turns = delay * centre
            turns = turns - jnp.round(turns)
            c, s = doubled(*small_turn(0.5 * turns))
            z = times((re, im), (c, -s))
            steer = doubled(*small_turn(0.25 * sine))
            for n in range(ANTENNAS):
                lead[n, p, 0, here, :], lead[n, p, 1, here, :] = z
                if n + 1 < ANTENNAS:
                    z = times(z, steer)
        return carry

    for slot in slots:
        lax.fori_loop(0, per_block // ROWS, functools.partial(prepare, slot), 0)


def in_vmem(x):
    return pltpu.with_memory_space_constraint(x, pltpu.VMEM)


def prepared(tones, slots, tables, counts, state=()):
    users, width = counts.shape
    f32 = jnp.float32
    vmem = pl.BlockSpec(memory_space=pltpu.VMEM)
    first = len(tables) + 1
    return pl.pallas_call(
        functools.partial(prepare_kernel, slots, len(tables), tones),
        in_specs=[vmem] * (first + len(state)),
        out_specs=[vmem] * 2,
        out_shape=[
            pltpu.VMEM((ANTENNAS, PATHS, 2, users, width), f32),
            pltpu.VMEM((tones // 2, PATHS, 2, users, width), f32),
        ],
        input_output_aliases={first + k: k for k in range(len(state))},
        compiler_params=pltpu.CompilerParams(vmem_limit_bytes=4 << 20),
        name="prepared",
    )(*[in_vmem(t) for t in tables], in_vmem(counts), *state)


def tone_kernel(distance, planes, y_ref, lead, turn, kept_ref, sent_ref, *buffers):
    users, width = lead.shape[3:]
    blocks = users // ROWS
    half = ANTENNAS * width
    pairs = Y_CHIPS * Z_CHIPS
    ap = lax.axis_index("ap")
    core, chip = ap % CORES, ap // CORES
    chip_z, target_y = chip // Y_CHIPS, (chip + distance) % Y_CHIPS

    def pair_of(plane):
        return jnp.abs(chip_z - plane) * Y_CHIPS + target_y

    def build(buffers, block, plane):
        pair = pair_of(plane)
        with_re, with_im, lo = buffers
        here = pl.ds(block * ROWS, ROWS)
        below = pl.ds(users + block * ROWS, ROWS)
        cs = [(turn[pair, p, 0, here, :], turn[pair, p, 1, here, :]) for p in range(PATHS)]
        for n in range(ANTENNAS):
            sums = None
            for p in range(PATHS):
                c, s = cs[p]
                re, im = lead[n, p, 0, here, :], lead[n, p, 1, here, :]
                products = (re * c, im * s, im * c, re * s)
                sums = products if sums is None else tuple(a + b for a, b in zip(sums, products))
            a, b, c, d = sums
            columns = slice(n * width, (n + 1) * width)
            for tone, (re, im) in enumerate(((a - b, c + d), (a + b, c - d))):
                for part, (value, ref) in enumerate(((re, with_re), (im, with_im))):
                    packed = value.astype(jnp.bfloat16)
                    ref[tone, here, columns] = packed
                    if part == 0:
                        with_im[tone, below, columns] = packed
                    rest = (value - packed.astype(jnp.float32)).astype(jnp.bfloat16)
                    lo[tone, here, slice(part * half + n * width, part * half + (n + 1) * width)] = rest

    def multiply(buffers, plane, slot):
        with_re, with_im, lo = buffers
        pair = pair_of(plane)
        plus, minus = pairs + pair, pairs - 1 - pair
        first = jnp.where(core == 0, plus, minus)
        for tone, (at, out_ref) in enumerate(((first, sent_ref), (plus + minus - first, kept_ref))):
            y = y_ref[at]
            y_hi = y.astype(jnp.bfloat16)
            y_lo = (y - y_hi.astype(jnp.float32)).astype(jnp.bfloat16)
            for part, ref in enumerate((with_re, with_im)):
                end = ref.shape[1]
                ref[tone, end - 4 * HALF : end - 2 * HALF] = y_hi[:, part * half : (part + 1) * half]
                ref[tone, end - 2 * HALF :] = y_lo[:, part * half : (part + 1) * half]
            by_re = product(with_re[tone], with_re[tone, :users])
            by_im = product(with_im[tone], with_im[tone, :users])
            crossed = by_im[users : 2 * users]
            out_ref[slot, :users, :] = (by_re[:users] + by_im[:users]) + (crossed - crossed.T)
            filtered = by_re[users:] + by_im[2 * users :]
            rest = product(y_hi, lo[tone])
            out_ref[slot, users:, :] = filtered[: 2 * HALF] + (filtered[2 * HALF :] + rest)

    sides = [buffers[3 * k : 3 * k + 3] for k in range(len(planes))]

    def alone(block, carry):
        build(sides[0], block, planes[0])
        return carry

    lax.fori_loop(0, blocks, alone, 0, unroll=2)
    for slot, plane in enumerate(planes):
        multiply(sides[slot], plane, slot)
        if slot + 1 < len(planes):
            for block in range(blocks):
                build(sides[slot + 1], block, planes[slot + 1])


def tone_systems(distance, planes, received, state):
    users, _ = state[0].shape[3:]
    wide = received.shape[2]
    f32, bf16 = jnp.float32, jnp.bfloat16
    vmem = pl.BlockSpec(memory_space=pltpu.VMEM)
    channel_re = pltpu.VMEM((2, users + 4 * HALF, wide // 2), bf16)
    channel_im = pltpu.VMEM((2, 2 * users + 4 * HALF, wide // 2), bf16)
    rest = pltpu.VMEM((2, users, wide), bf16)
    return pl.pallas_call(
        functools.partial(tone_kernel, distance, planes),
        in_specs=[vmem] * (1 + len(state)),
        out_specs=[vmem, vmem],
        out_shape=[pltpu.VMEM((len(planes), users + 2 * HALF, users), f32)] * 2,
        scratch_shapes=[channel_re, channel_im, rest] * len(planes),
        compiler_params=pltpu.CompilerParams(vmem_limit_bytes=16 << 20),
        name="tone_systems",
    )(in_vmem(received), *state)


def three_parts(x):
    hi = x.astype(jnp.bfloat16)
    rest = x - hi.astype(jnp.float32)
    mid = rest.astype(jnp.bfloat16)
    return hi, mid, (rest - mid.astype(jnp.float32)).astype(jnp.bfloat16)


def solve_kernel(*refs):
    *part_refs, regularizer_ref, out_ref, system_ref, parts, x_ref, r_ref, p_ref, q_ref, work = refs
    system_ref[...] = sum(ref[0] for ref in part_refs)
    users = regularizer_ref.shape[1]
    f32 = jnp.float32
    g = system_ref[:users, :]
    flipped = g.T
    row = lax.broadcasted_iota(jnp.int32, (users, users), 0)
    column = lax.broadcasted_iota(jnp.int32, (users, users), 1)
    eye = row == column
    re = 0.5 * (g + flipped)
    im = 0.5 * (g - flipped)
    re = jnp.where(eye, re + regularizer_ref[...], re)
    diagonal = jnp.where(eye, re, 0.0)
    across = lax.rsqrt(jnp.sum(diagonal, 0, keepdims=True))
    down = lax.rsqrt(jnp.sum(diagonal, 1, keepdims=True))
    for k, matrix in enumerate((re, im)):
        for at, part in enumerate(three_parts(matrix * across * down)):
            parts[k, at] = part
    right = system_ref[users:, :] * across

    def together(v):
        total = jnp.sum(v[:HALF] + v[HALF:], 1, keepdims=True)
        return jnp.concatenate([total, total], 0)

    def dot(a, b):
        return jnp.dot(a, b, preferred_element_type=f32)

    rows = 2 * HALF

    def applied(p):
        hi, mid, low = three_parts(p)
        left3 = jnp.concatenate([hi, mid, low], 0)
        left2 = jnp.concatenate([hi, mid], 0)
        result = []
        for k in range(2):
            a = dot(left3, parts[k, 0])
            b = dot(left2, parts[k, 1])
            c = dot(hi, parts[k, 2])
            small = a[2 * rows :] + b[rows:] + c
            result.append(a[:rows] + ((a[rows : 2 * rows] + b[:rows]) + small))
        s, i = result
        return jnp.concatenate([s[:HALF] + i[HALF:], s[HALF:] - i[:HALF]], 0)

    norm = together(right * right)
    goal = norm * (TOLERANCE * TOLERANCE)
    nothing = jnp.zeros_like(right)
    x_ref[...], p_ref[...], q_ref[...] = nothing, nothing, nothing
    r_ref[...] = right

    def advance(state):
        done, _, earlier, alpha = state
        for _ in range(STEPS_A_CHECK):
            r = r_ref[...]
            applied_r = applied(r)
            rr = together(r * r)
            curvature = together(r * applied_r)
            beta = jnp.where(earlier > 0.0, rr / earlier, 0.0)
            curvature = curvature - jnp.where(alpha > 0.0, beta * rr / alpha, 0.0)
            alpha = jnp.where(curvature > 0.0, rr / curvature, 0.0)
            p = r + beta * p_ref[...]
            q = applied_r + beta * q_ref[...]
            p_ref[...], q_ref[...] = p, q
            x_ref[...] += alpha * p
            r_ref[...] = r - alpha * q
            earlier = rr
        r = r_ref[...]
        return done + STEPS_A_CHECK, jnp.max(jnp.where(together(r * r) <= goal, 0, 1)), earlier, alpha

    def unfinished(state):
        return (state[1] > 0) & (state[0] < SOLVE_STEPS)

    zero = jnp.zeros_like(norm)
    _, left, _, _ = lax.while_loop(unfinished, advance, (0, jnp.max(jnp.where(norm <= goal, 0, 1)), zero, zero))
    out_ref[...] = x_ref[...] * across

    @pl.when(left > 0)
    def _():
        work[0, :users, :] = re
        work[1, :users, :] = -im
        work[0, users:, :] = system_ref[users : users + HALF, :]
        work[1, users:, :] = system_ref[users + HALF :, :]
        lane = lax.broadcasted_iota(jnp.int32, (1, users), 1)

        def eliminate(j, carry):
            a, b = work[0], work[1]
            here = lane == j
            row_re = work[0, pl.ds(j, 1), :]
            row_im = work[1, pl.ds(j, 1), :]
            pivot = 1.0 / jnp.sum(jnp.where(here, row_re, 0.0), 1, keepdims=True)
            col_re = jnp.sum(jnp.where(here, a, 0.0), 1, keepdims=True) * pivot
            col_im = jnp.sum(jnp.where(here, b, 0.0), 1, keepdims=True) * pivot
            work[0] = jnp.where(here, col_re, a - (col_re * row_re - col_im * row_im))
            work[1] = jnp.where(here, col_im, b - (col_re * row_im + col_im * row_re))
            return carry

        lax.fori_loop(0, users, eliminate, 0)
        out_ref[:HALF, :] = work[0, users:, :]
        out_ref[HALF:, :] = work[1, users:, :]


def solved(systems, regularizer):
    _, rows, users = systems[0].shape
    f32 = jnp.float32
    vmem = pl.BlockSpec(memory_space=pltpu.VMEM)
    pair = pltpu.VMEM((2 * HALF, users), f32)
    return pl.pallas_call(
        solve_kernel,
        in_specs=[vmem] * (len(systems) + 1),
        out_specs=vmem,
        out_shape=jax.ShapeDtypeStruct((2 * HALF, users), f32),
        scratch_shapes=[
            pltpu.VMEM((rows, users), f32),
            pltpu.VMEM((2, 3, users, users), jnp.bfloat16),
            pair,
            pair,
            pair,
            pair,
            pltpu.VMEM((2, users + HALF, users), f32),
        ],
        compiler_params=pltpu.CompilerParams(vmem_limit_bytes=12 << 20),
        name="solved",
    )(*[in_vmem(s) for s in systems], regularizer.reshape(1, users))


def received_rows(observed_signal):
    _, samples, tones, antennas, width = observed_signal.shape
    y = jnp.moveaxis(observed_signal, 2, 0).reshape(tones, 2, samples, antennas * width)
    re, im = y[:, 0], y[:, 1]
    gap = ((0, 0), (0, HALF - samples), (0, 0))
    top = jnp.pad(jnp.concatenate([re, im], 2), gap)
    bottom = jnp.pad(jnp.concatenate([im, -re], 2), gap)
    return jnp.concatenate([top, bottom], 1)


def ap_at(z, y, core):
    return (z * Y_CHIPS + y % Y_CHIPS) * CORES + core


def over_ap(value, dz, dy, dcore):
    spots = [(z, y, c) for z in range(Z_CHIPS) for y in range(Y_CHIPS) for c in range(CORES)]
    pairs = [(ap_at(z, y, c), ap_at(z ^ dz, y + dy, c ^ dcore)) for z, y, c in spots]
    return lax.ppermute(value, "ap", pairs)


def over_sc(value, dz, dx):
    spots = [(z, x) for z in range(2) for x in range(X_CHIPS)]
    pairs = [(z * X_CHIPS + x, (z ^ dz) * X_CHIPS + (x + dx) % X_CHIPS) for z, x in spots]
    return lax.ppermute(value, "sc", pairs)


def gathered_tables(own):
    half = own.shape[0] // 2

    across = over_sc(own, 1, 0)
    up, down = over_sc(own, 0, 1), over_sc(own, 0, -1)
    up_twice, down_twice = over_sc(up[:half], 0, 1), over_sc(down[half:], 0, -1)
    across_up, across_down = over_sc(across, 0, 1), over_sc(across, 0, -1)
    opposite = jnp.concatenate([up_twice, down_twice], 0)
    return [own, across, up, down], [opposite, across_up, across_down, over_sc(opposite, 1, 0)]


def pack_kernel(*refs):
    *parts, out, sems = refs
    rows = out.shape[0] // len(parts)
    copies = [
        pltpu.make_async_copy(part, out.at[pl.ds(k * rows, rows)], sems.at[k]) for k, part in enumerate(parts)
    ]
    for copy in copies:
        copy.start()
    for copy in copies:
        copy.wait()


def packed_tables(parts):
    rows = sum(part.shape[0] for part in parts)
    vmem = pl.BlockSpec(memory_space=pltpu.VMEM)
    return pl.pallas_call(
        pack_kernel,
        in_specs=[pl.BlockSpec(memory_space=pltpu.HBM)] * len(parts),
        out_specs=vmem,
        out_shape=pltpu.VMEM((rows, *parts[0].shape[1:]), jnp.float32),
        scratch_shapes=[pltpu.SemaphoreType.DMA((len(parts),))],
        compiler_params=pltpu.CompilerParams(vmem_limit_bytes=4 << 20),
        name="packed_tables",
    )(*[pltpu.with_memory_space_constraint(p, pltpu.HBM) for p in parts])


def all_steps(observed_signal, delays, sines, path_gain_real, path_gain_imaginary, counts, regularizer):
    tones = observed_signal.shape[2]
    samples = observed_signal.shape[1]
    users = counts.shape[0]
    core = lax.axis_index("ap") % CORES
    own = packed_tables([delays, sines, path_gain_real, path_gain_imaginary])
    near, far = gathered_tables(own)
    state = prepared(tones, NEAR_SLOTS, near, counts)
    state = prepared(tones, FAR_SLOTS, far, counts, state)
    received = received_rows(observed_signal)
    rows = users + 2 * HALF
    top = rows // 2

    def systems(distance, planes, *after):
        y = lax.optimization_barrier((received, *after))[0] if after else received
        kept, sent = tone_systems(distance, planes, y, state)
        return kept, over_ap(sent, 0, 0, 1)

    def around(value, step):
        return over_ap(value, 0, step, 0)

    def joined(pieces, passed, at):
        total = pieces[0] + pieces[1]
        if at == 0:
            return jnp.concatenate([total[:, :top] + passed, total[:, top:]], 1)
        return jnp.concatenate([total[:, :top], total[:, top:] + passed], 1)

    def across_z(value):
        return over_ap(value, 1, 0, 0)

    far2 = systems(2, (1,))
    own2 = systems(2, (0,), far2[0])
    first = across_z(far2[0] + far2[1])
    far1 = systems(1, (1,), own2[0])
    own1 = systems(1, (0,), far1[0])
    up_across = across_z(far1[0] + far1[1])
    far3 = systems(3, (1,), own1[0])
    own3 = systems(3, (0,), far3[0])
    down_across = across_z(far3[0] + far3[1])
    passing = (own2[0] + own2[1]) + first
    up, down = around(passing[:, :top], 1), around(passing[:, top:], -1)
    far0 = systems(0, (1,), own3[0])
    kept, other = systems(0, (0,), far0[0])
    across = across_z(far0[0] + far0[1])
    up_own = joined(own1, up, 0) + up_across
    down_own = joined(own3, down, 1) + down_across
    own_up, own_down = around(up_own, 1), around(down_own, -1)
    own_tone = solved([kept, other, own_up, own_down, across], regularizer)
    chips = lax.axis_size("ap") // CORES
    same = [[chip * CORES + c for chip in range(chips)] for c in range(CORES)]
    same_core = lax.all_to_all(
        jnp.broadcast_to(own_tone[None], (chips, *own_tone.shape)), "ap", 0, 0, tiled=True, axis_index_groups=same
    )
    other_core = over_ap(same_core, 0, 0, 1)
    first = jnp.where(core == 0, same_core, other_core)[::-1]
    second = jnp.where(core == 0, other_core, same_core)
    every = jnp.concatenate([first, second], 0).reshape(tones, 2, HALF, users)[:, :, :samples]
    return jnp.transpose(every, (1, 2, 0, 3))


def solution(mesh):
    placed = (
        P(None, None, "sc", None, "ap"),
        P(None, "sc", "ap"),
        P(None, "sc", "ap"),
        P(None, "sc", "ap"),
        P(None, "sc", "ap"),
        P(None, "ap"),
        P(),
    )
    return jax.shard_map(all_steps, mesh=mesh, in_specs=placed, out_specs=P(None, None, "sc", None), check_vma=False)
```
